32 devices in a mesh: fsdp: 32 (over z, y, x, core).
Axes of the slice: x: 2, y: 2, z: 4, core: 2. Of those that a mesh axis runs over, the one named last changes fastest.
Arguments:
- latents: float32 [128, 256, 16], P('fsdp'), may hold values from -6 to 6
- noise: float32 [128, 256, 16], P('fsdp'), may hold values from -6 to 6
- timesteps: int32 [128], P('fsdp'), may hold values from 0 to 999
- labels: int32 [128], P('fsdp'), may hold values from 0 to 999
- qkv_weight: float32 [2, 768, 2304], P(None, 'fsdp'), may hold values from -0.21875 to 0.21875
- proj_weight: float32 [2, 768, 768], P(None, 'fsdp'), may hold values from -0.875 to 0.875
- up_weight: float32 [2, 768, 3072], P(None, 'fsdp'), may hold values from -0.21875 to 0.21875
- down_weight: float32 [2, 3072, 768], P(None, 'fsdp'), may hold values from -0.109375 to 0.109375
- mod_weight: float32 [768, 10752], P('fsdp'), may hold values from -0.21875 to 0.21875
- tables: float32 [2056, 768], P(None, 'fsdp'), may hold values from -4 to 4
- biases: float32 [25360], replicated, may hold values from -4 to 4
- qkv_first: float32 [2, 768, 2304], P(None, 'fsdp'), may hold values from -0.00030517578 to 0.00030517578
- proj_first: float32 [2, 768, 768], P(None, 'fsdp'), may hold values from -0.00030517578 to 0.00030517578
- up_first: float32 [2, 768, 3072], P(None, 'fsdp'), may hold values from -0.00030517578 to 0.00030517578
- down_first: float32 [2, 3072, 768], P(None, 'fsdp'), may hold values from -0.00030517578 to 0.00030517578
- mod_first: float32 [768, 10752], P('fsdp'), may hold values from -0.00030517578 to 0.00030517578
- tables_first: float32 [2056, 768], P(None, 'fsdp'), may hold values from -0.00030517578 to 0.00030517578
- biases_first: float32 [25360], replicated, may hold values from -0.00030517578 to 0.00030517578
- qkv_second: float32 [2, 768, 2304], P(None, 'fsdp'), may hold values from 3e-09 to 5e-08
- proj_second: float32 [2, 768, 768], P(None, 'fsdp'), may hold values from 3e-09 to 5e-08
- up_second: float32 [2, 768, 3072], P(None, 'fsdp'), may hold values from 3e-09 to 5e-08
- down_second: float32 [2, 3072, 768], P(None, 'fsdp'), may hold values from 3e-09 to 5e-08
- mod_second: float32 [768, 10752], P('fsdp'), may hold values from 3e-09 to 5e-08
- tables_second: float32 [2056, 768], P(None, 'fsdp'), may hold values from 3e-09 to 5e-08
- biases_second: float32 [25360], replicated, may hold values from 3e-09 to 5e-08
Outputs:
- loss_value: float32 [], replicated
- grad_norm: float32 [], replicated
- qkv_update: float32 [2, 768, 2304], P(None, 'fsdp')
- qkv_first_new: float32 [2, 768, 2304], P(None, 'fsdp')
- qkv_second_new: float32 [2, 768, 2304], P(None, 'fsdp')
- proj_update: float32 [2, 768, 768], P(None, 'fsdp')
- proj_first_new: float32 [2, 768, 768], P(None, 'fsdp')
- proj_second_new: float32 [2, 768, 768], P(None, 'fsdp')
- up_update: float32 [2, 768, 3072], P(None, 'fsdp')
- up_first_new: float32 [2, 768, 3072], P(None, 'fsdp')
- up_second_new: float32 [2, 768, 3072], P(None, 'fsdp')
- down_update: float32 [2, 3072, 768], P(None, 'fsdp')
- down_first_new: float32 [2, 3072, 768], P(None, 'fsdp')
- down_second_new: float32 [2, 3072, 768], P(None, 'fsdp')
- mod_update: float32 [768, 10752], P('fsdp')
- mod_first_new: float32 [768, 10752], P('fsdp')
- mod_second_new: float32 [768, 10752], P('fsdp')
- tables_update: float32 [2056, 768], P(None, 'fsdp')
- tables_first_new: float32 [2056, 768], P(None, 'fsdp')
- tables_second_new: float32 [2056, 768], P(None, 'fsdp')
- biases_update: float32 [25360], replicated
- biases_first_new: float32 [25360], replicated
- biases_second_new: float32 [25360], replicated
The draws below stay inside these ranges and needn't reach their ends.
All inputs are finite; a program needn't handle non-finite values.
Results may differ from the reference program's by a relative error of at most 0.011.
Values may be sent and summed in bfloat16 or wider, within the bound.
No kernel may reach another device: no remote copies, remote signals or barrier semaphores. Data moves between devices by JAX's collectives and lax.ppermute only.
A program may use at most 384 MiB of HBM per device.

```python
import math
import jax
import jax.numpy as jnp
from jax import lax

D = 768
HEADS = 12
HD = 64
FF = 3072
FREQ = 256
CLASSES = 1000
DIFF_STEPS = 1000
LAYERS = 2
TOK = 256
PD = 16
SAMPLES = 128
MODW = 10752
ROWS_T = 2056
BIAS = 25360


def draw_tables(key, part):
    row_index = jnp.arange(ROWS_T)
    fan_in = jnp.where(row_index < PD, PD, jnp.where(row_index < PD + FREQ, FREQ, D)).astype(jnp.float32)
    scales = lax.rsqrt(fan_in)
    class_rows = (row_index >= PD + FREQ + D) & (row_index < PD + FREQ + D + CLASSES)
    scales = jnp.where(class_rows, 1.0, scales)
    values = jnp.clip(jax.random.normal(key, (ROWS_T, D), jnp.float32), -4.0, 4.0)
    return values * scales[:, None]


def with_ends(entries, rng, least, largest):
    longest = entries.shape.index(max(entries.shape))
    spots = []
    for shift in (0, 1):
        where = [jax.random.randint(jax.random.fold_in(rng, axis), (), 0, length) for axis, length in enumerate(entries.shape)]
        where[longest] = (where[longest] + shift) % entries.shape[longest]
        spots.append(tuple(where))
    return entries.at[spots[0]].set(least).at[spots[1]].set(largest)


def shard_levels(own_key, extent, shards, low, top_value):
    loudness = 1.0
    for dim, shards_of in shards:
        draws = jax.random.uniform(jax.random.fold_in(jax.random.fold_in(own_key, 6), dim), (shards_of,), jnp.float32, low / len(shards), top_value / len(shards))
        loudness = loudness * jnp.repeat(jnp.exp(draws), extent[dim] // shards_of).reshape((-1,) + (1,) * (len(extent) - 1 - dim))
    return loudness


def bell_draw(own_key, dims, width, most, split=(), kind=jnp.bfloat16):
    drawn = width * jax.random.normal(own_key, dims, jnp.float32)
    if split:
        drawn = drawn * shard_levels(own_key, dims, split, -0.22, 0.18)
    return jnp.clip(drawn, -most, most).astype(kind)


def setup_inputs(seed: int = 0) -> dict:
    splits = jax.random.split(jax.random.key(seed), 26)
    return {
        "latents": bell_draw(splits[0], (SAMPLES, TOK, PD), 1.0, 6.0, ((0, 32),), jnp.float32),
        "noise": bell_draw(splits[1], (SAMPLES, TOK, PD), 1.0, 6.0, ((0, 32),), jnp.float32),
        "timesteps": with_ends(jax.random.randint(splits[2], (SAMPLES,), 0, DIFF_STEPS), jax.random.fold_in(splits[2], 1), 0, DIFF_STEPS - 1).astype(jnp.int32),
        "labels": with_ends(jax.random.randint(splits[3], (SAMPLES,), 0, CLASSES), jax.random.fold_in(splits[3], 1), 0, CLASSES - 1).astype(jnp.int32),
        "qkv_weight": bell_draw(splits[4], (LAYERS, D, 3 * D), D ** -0.5, 0.21875, ((1, 32),), jnp.float32),
        "proj_weight": bell_draw(splits[5], (LAYERS, D, D), (D // 16) ** -0.5, 0.875, ((1, 32),), jnp.float32),
        "up_weight": bell_draw(splits[6], (LAYERS, D, FF), D ** -0.5, 0.21875, ((1, 32),), jnp.float32),
        "down_weight": bell_draw(splits[7], (LAYERS, FF, D), FF ** -0.5, 0.109375, ((1, 32),), jnp.float32),
        "mod_weight": bell_draw(splits[8], (D, MODW), D ** -0.5, 0.21875, ((0, 32),), jnp.float32),
        "tables": draw_tables(jax.random.fold_in(splits[25], 71), 0),
        "biases": bell_draw(splits[10], (BIAS,), 0.3, 4.0, (), jnp.float32),
        "qkv_first": bell_draw(splits[11], (LAYERS, D, 3 * D), (5e-5), 0.00030517578, ((1, 32),), jnp.float32),
        "proj_first": bell_draw(splits[12], (LAYERS, D, D), (5e-5), 0.00030517578, ((1, 32),), jnp.float32),
        "up_first": bell_draw(splits[13], (LAYERS, D, FF), (5e-5), 0.00030517578, ((1, 32),), jnp.float32),
        "down_first": bell_draw(splits[14], (LAYERS, FF, D), (5e-5), 0.00030517578, ((1, 32),), jnp.float32),
        "mod_first": bell_draw(splits[15], (D, MODW), (5e-5), 0.00030517578, ((0, 32),), jnp.float32),
        "tables_first": bell_draw(splits[16], (ROWS_T, D), (5e-5), 0.00030517578, ((1, 32),), jnp.float32),
        "biases_first": bell_draw(splits[17], (BIAS,), (5e-5), 0.00030517578, (), jnp.float32),
        "qkv_second": jnp.clip(jnp.exp(math.log(5.000000058430487e-08) - 2.8134107 * jax.random.uniform(splits[18], (LAYERS, D, 3 * D), jnp.float32) ** shard_levels(splits[18], (LAYERS, D, 3 * D), ((1, 32),), -0.2, 0.2)), 3.000000026176508e-09, 5.000000058430487e-08),
        "proj_second": jnp.clip(jnp.exp(math.log(5.000000058430487e-08) - 2.8134107 * jax.random.uniform(splits[19], (LAYERS, D, D), jnp.float32) ** shard_levels(splits[19], (LAYERS, D, D), ((1, 32),), -0.2, 0.2)), 3.000000026176508e-09, 5.000000058430487e-08),
        "up_second": jnp.clip(jnp.exp(math.log(5.000000058430487e-08) - 2.8134107 * jax.random.uniform(splits[20], (LAYERS, D, FF), jnp.float32) ** shard_levels(splits[20], (LAYERS, D, FF), ((1, 32),), -0.2, 0.2)), 3.000000026176508e-09, 5.000000058430487e-08),
        "down_second": jnp.clip(jnp.exp(math.log(5.000000058430487e-08) - 2.8134107 * jax.random.uniform(splits[21], (LAYERS, FF, D), jnp.float32) ** shard_levels(splits[21], (LAYERS, FF, D), ((1, 32),), -0.2, 0.2)), 3.000000026176508e-09, 5.000000058430487e-08),
        "mod_second": jnp.clip(jnp.exp(math.log(5.000000058430487e-08) - 2.8134107 * jax.random.uniform(splits[22], (D, MODW), jnp.float32) ** shard_levels(splits[22], (D, MODW), ((0, 32),), -0.2, 0.2)), 3.000000026176508e-09, 5.000000058430487e-08),
        "tables_second": jnp.clip(jnp.exp(math.log(5.000000058430487e-08) - 2.8134107 * jax.random.uniform(splits[23], (ROWS_T, D), jnp.float32) ** shard_levels(splits[23], (ROWS_T, D), ((1, 32),), -0.2, 0.2)), 3.000000026176508e-09, 5.000000058430487e-08),
        "biases_second": jnp.clip(jnp.exp(jax.random.uniform(splits[24], (BIAS,), jnp.float32, math.log(3.000000026176508e-09), math.log(5.000000058430487e-08))), 3.000000026176508e-09, 5.000000058430487e-08),
    }


@jax.custom_vjp
def low(v):
    return lax.optimization_barrier(v.astype(jnp.bfloat16)).astype(jnp.float32)

@jax.custom_vjp
def low_back(v):
    return v

def low_keep(v):
    return (low(v), None)

def low_pass(kept, grad):
    return (grad,)

def back_keep(v):
    return (v, None)

def back_low(kept, grad):
    return (low(grad),)
low.defvjp(low_keep, low_pass)
low_back.defvjp(back_keep, back_low)
highest = lax.Precision.HIGHEST
norm_eps = 1e-06
clip_limit = 2.5
learn_rate = 0.01
beta_first = 0.9
beta_second = 0.95
adam_eps = 1e-08
weight_decay = 0.01
first_fix = 1.0 - 0.9 ** 10
second_fix = 1.0 - 0.95 ** 10

def modulate(residual, shift_term, scale_term):
    centred = residual - lax.optimization_barrier(jnp.mean(residual, axis=-1, keepdims=True))
    spread = lax.optimization_barrier(jnp.mean(centred * centred, axis=-1, keepdims=True))
    normed = centred * lax.rsqrt(spread + norm_eps)
    return normed * (1.0 + scale_term[:, None, :]) + shift_term[:, None, :]

def dense(inputs, weight, offset):
    return low_back(jnp.dot(low(inputs), weight, precision=highest) + offset)

def time_features(steps_in):
    half_count = FREQ // 2
    frequencies = jnp.exp(-math.log(10000.0) * jnp.arange(half_count, dtype=jnp.float32) / half_count)
    angles = steps_in.astype(jnp.float32)[:, None] * frequencies[None, :]
    return jnp.concatenate([jnp.cos(angles), jnp.sin(angles)], axis=1)

def noise_share(steps_in):
    beta_values = jnp.linspace(0.0001, 0.02, DIFF_STEPS, dtype=jnp.float32)
    log_keep = jnp.cumsum(jnp.log(1.0 - beta_values))
    return jnp.exp(jnp.take(log_keep, steps_in.astype(jnp.int32)))

def bias_parts(biases):
    per_layer = 10 * D + FF
    layer_parts = []
    for layer_index in range(LAYERS):
        anchor = layer_index * per_layer
        layer_parts.append((biases[anchor:anchor + D], biases[anchor + D:anchor + 2 * D], biases[anchor + 2 * D:anchor + 3 * D], biases[anchor + 3 * D:anchor + 3 * D + FF], biases[anchor + 3 * D + FF:anchor + 4 * D + FF], biases[anchor + 4 * D + FF:anchor + per_layer]))
    anchor = LAYERS * per_layer
    global_parts = (biases[anchor:anchor + 2 * D], biases[anchor + 2 * D:anchor + 3 * D], biases[anchor + 3 * D:anchor + 4 * D], biases[anchor + 4 * D:anchor + 5 * D], biases[anchor + 5 * D:anchor + 5 * D + PD])
    return (layer_parts, global_parts)

def attend(packed):
    sample_count = packed.shape[0]
    queries = packed[:, :, :D].reshape(sample_count, TOK, HEADS, HD)
    keys_all = packed[:, :, D:2 * D].reshape(sample_count, TOK, HEADS, HD)
    values_all = packed[:, :, 2 * D:].reshape(sample_count, TOK, HEADS, HD)
    scores = low_back(jnp.einsum('bqhd,bkhd->bhqk', queries, keys_all, precision=highest) * HD ** (-0.5))
    soft_weights = jax.nn.softmax(scores, axis=-1)
    mixed = jnp.einsum('bhqk,bkhd->bqhd', low(soft_weights), values_all, precision=highest)
    return low_back(mixed.reshape(sample_count, TOK, D))

def group_loss(rounded, biases, latents, noise, timesteps, labels):
    qkv_low, proj_low, up_low, down_low, mod_low, tables_low = rounded
    sample_count = latents.shape[0]
    row_count = sample_count * TOK
    layer_parts, global_parts = bias_parts(biases)
    final_bias, patch_bias, first_bias, second_bias, head_bias = global_parts
    patch_rows = tables_low[:PD]
    first_rows = tables_low[PD:PD + FREQ]
    second_rows = tables_low[PD + FREQ:PD + FREQ + D]
    class_rows = tables_low[PD + FREQ + D:PD + FREQ + D + CLASSES]
    head_rows = tables_low[PD + FREQ + D + CLASSES:]
    keep_share = noise_share(timesteps)
    noised = jnp.sqrt(keep_share)[:, None, None] * latents + jnp.sqrt(1.0 - keep_share)[:, None, None] * noise
    residual = dense(noised.reshape(row_count, PD), patch_rows, patch_bias).reshape(sample_count, TOK, D)
    first_pre = dense(time_features(timesteps), first_rows, first_bias)
    time_embed = dense(jax.nn.silu(first_pre), second_rows, second_bias)
    condition = time_embed + jnp.take(class_rows, labels.astype(jnp.int32), axis=0)
    mod_bias = jnp.concatenate([part_item[5] for part_item in layer_parts] + [final_bias])
    modulations = dense(jax.nn.silu(condition), mod_low, mod_bias)
    for layer_index in range(LAYERS):
        query_bias, value_bias, proj_bias, up_bias, down_bias, unused = layer_parts[layer_index]
        segment = modulations[:, layer_index * 6 * D:(layer_index + 1) * 6 * D]
        mod_terms = [segment[:, part_index * D:(part_index + 1) * D] for part_index in range(6)]
        shift_attn, scale_attn, gate_attn, shift_mlp, scale_mlp, gate_mlp = mod_terms
        hidden = modulate(residual, shift_attn, scale_attn)
        packed_bias = jnp.concatenate([query_bias, jnp.zeros((D,), jnp.float32), value_bias])
        packed = dense(hidden.reshape(row_count, D), qkv_low[layer_index], packed_bias).reshape(sample_count, TOK, 3 * D)
        mixed = attend(low(packed))
        attn_out = dense(mixed.reshape(row_count, D), proj_low[layer_index], proj_bias).reshape(sample_count, TOK, D)
        residual = residual + gate_attn[:, None, :] * attn_out
        hidden = modulate(residual, shift_mlp, scale_mlp)
        pre_act = dense(hidden.reshape(row_count, D), up_low[layer_index], up_bias)
        mlp_out = dense(jax.nn.gelu(pre_act, approximate=True), down_low[layer_index], down_bias).reshape(sample_count, TOK, D)
        residual = residual + gate_mlp[:, None, :] * mlp_out
    final_mods = modulations[:, LAYERS * 6 * D:]
    final_hidden = modulate(residual, final_mods[:, :D], final_mods[:, D:])
    predicted = dense(final_hidden.reshape(row_count, D), head_rows.T, head_bias)
    errors = predicted - noise.reshape(row_count, PD)
    return jnp.sum(errors * errors) / (SAMPLES * TOK * PD)

def adam_step(weight_now, grad_now, first_old, second_old, factor):
    clipped = grad_now * factor
    first_new = beta_first * first_old + (1.0 - beta_first) * clipped
    second_new = beta_second * second_old + (1.0 - beta_second) * clipped * clipped
    step_size = -learn_rate * (first_new / first_fix / (jnp.sqrt(second_new / second_fix) + adam_eps) + weight_decay * weight_now)
    return (step_size, first_new, second_new)

def reference(latents, noise, timesteps, labels, qkv_weight, proj_weight, up_weight, down_weight, mod_weight, tables, biases, qkv_first, proj_first, up_first, down_first, mod_first, tables_first, biases_first, qkv_second, proj_second, up_second, down_second, mod_second, tables_second, biases_second):
    parameters = (qkv_weight, proj_weight, up_weight, down_weight, mod_weight, tables, biases)
    group_size = math.gcd(SAMPLES, 16)
    group_count = SAMPLES // group_size
    batches = (latents.reshape(group_count, group_size, TOK, PD), noise.reshape(group_count, group_size, TOK, PD), timesteps.reshape(group_count, group_size), labels.reshape(group_count, group_size))
    checked = jax.checkpoint(group_loss)

    def total(params_in):
        rounded = tuple((low(weight_item) for weight_item in params_in[:6]))
        biases_in = params_in[6]

        def scan_step(running, slices):
            return (running + checked(rounded, biases_in, slices[0], slices[1], slices[2], slices[3]), None)
        total_loss, unused = lax.scan(scan_step, jnp.zeros((), jnp.float32), batches)
        return total_loss
    loss_value, pullback = jax.vjp(total, parameters)
    gradients = pullback(jnp.ones((), jnp.float32))[0]
    squares = jnp.zeros((), jnp.float32)
    for grad_item in gradients:
        squares = squares + jnp.sum(grad_item * grad_item)
    grad_norm = jnp.sqrt(squares)
    factor = jnp.minimum(1.0, clip_limit / (grad_norm + 1e-06))
    qkv_update, qkv_first_new, qkv_second_new = adam_step(qkv_weight, gradients[0], qkv_first, qkv_second, factor)
    proj_update, proj_first_new, proj_second_new = adam_step(proj_weight, gradients[1], proj_first, proj_second, factor)
    up_update, up_first_new, up_second_new = adam_step(up_weight, gradients[2], up_first, up_second, factor)
    down_update, down_first_new, down_second_new = adam_step(down_weight, gradients[3], down_first, down_second, factor)
    mod_update, mod_first_new, mod_second_new = adam_step(mod_weight, gradients[4], mod_first, mod_second, factor)
    tables_update, tables_first_new, tables_second_new = adam_step(tables, gradients[5], tables_first, tables_second, factor)
    biases_update, biases_first_new, biases_second_new = adam_step(biases, gradients[6], biases_first, biases_second, factor)
    return (loss_value, grad_norm, qkv_update, qkv_first_new, qkv_second_new, proj_update, proj_first_new, proj_second_new, up_update, up_first_new, up_second_new, down_update, down_first_new, down_second_new, mod_update, mod_first_new, mod_second_new, tables_update, tables_first_new, tables_second_new, biases_update, biases_first_new, biases_second_new)
```

```python
import math

import jax
import jax.numpy as jnp
from jax import lax
from jax.experimental import pallas as pl
from jax.sharding import PartitionSpec as P

D = 768
HEADS = 12
HD = 64
FF = 3072
FREQ = 256
CLASSES = 1000
DIFF_STEPS = 1000
LAYERS = 2
TOK = 256
PD = 16
MODW = 10752


norm_eps = 1e-06
clip_limit = 2.5
learn_rate = 0.01
beta_first = 0.9
beta_second = 0.95
adam_eps = 1e-08
weight_decay = 0.01
first_fix = 1.0 - 0.9**10
second_fix = 1.0 - 0.95**10


def modulate(residual, shift_term, scale_term):
    centred = residual - jnp.mean(residual, axis=-1, keepdims=True)
    spread = jnp.mean(centred * centred, axis=-1, keepdims=True)
    normed = centred * lax.rsqrt(spread + norm_eps)
    return normed * (1.0 + scale_term[:, None, :]) + shift_term[:, None, :]


def gelu_tanh(values):
    return jax.nn.gelu(values, approximate=True)


def product(left_side, right_side):
    return jnp.dot(left_side, right_side, preferred_element_type=jnp.float32)


def left_product(left_side, right_side):
    return lax.dot_general(
        left_side, right_side, (((0,), (0,)), ((), ())), preferred_element_type=jnp.float32
    )


def right_product(left_side, right_side):
    return lax.dot_general(
        left_side, right_side, (((1,), (1,)), ((), ())), preferred_element_type=jnp.float32
    )


def time_features(steps_in):
    half_count = FREQ // 2
    frequencies = jnp.exp(
        -math.log(10000.0) * jnp.arange(half_count, dtype=jnp.float32) / half_count
    )
    angles = steps_in.astype(jnp.float32)[:, None] * frequencies[None, :]
    return jnp.concatenate([jnp.cos(angles), jnp.sin(angles)], axis=1)


def noise_share(steps_in):
    beta_values = jnp.linspace(0.0001, 0.02, DIFF_STEPS, dtype=jnp.float32)
    log_keep = jnp.log(1.0 - beta_values)
    taken = jnp.arange(DIFF_STEPS, dtype=jnp.int32)[None, :] <= steps_in[:, None]
    return jnp.exp(jnp.sum(jnp.where(taken, log_keep[None, :], 0.0), axis=1))


def bias_parts(biases):
    per_layer = 10 * D + FF
    layer_parts = []
    for layer_index in range(LAYERS):
        anchor = layer_index * per_layer
        layer_parts.append(
            (
                biases[anchor : anchor + D],
                biases[anchor + D : anchor + 2 * D],
                biases[anchor + 2 * D : anchor + 3 * D],
                biases[anchor + 3 * D : anchor + 3 * D + FF],
                biases[anchor + 3 * D + FF : anchor + 4 * D + FF],
                biases[anchor + 4 * D + FF : anchor + per_layer],
            )
        )
    anchor = LAYERS * per_layer
    global_parts = (
        biases[anchor : anchor + 2 * D],
        biases[anchor + 2 * D : anchor + 3 * D],
        biases[anchor + 3 * D : anchor + 4 * D],
        biases[anchor + 4 * D : anchor + 5 * D],
        biases[anchor + 5 * D : anchor + 5 * D + PD],
    )
    return (layer_parts, global_parts)


def hop_plan(count):
    if count == 32:
        return [(8, 4), (2, 2), (4, 2), (1, 2)]
    plan = []
    stride = 1
    while stride < count:
        plan.append((stride, 2))
        stride *= 2
    return plan


def shifted(index, stride, size, amount):
    coord = (index // stride) % size
    return index + ((coord + amount) % size - coord) * stride


def send(value, count, stride, size, amount=1):
    pairs = [(index, shifted(index, stride, size, amount)) for index in range(count)]
    return lax.ppermute(value, "fsdp", pairs)


def gather_near(value, count):
    gathered = value[None]
    for stride, size in hop_plan(count):
        pieces = [gathered]
        for unused in range(size - 1):
            pieces.append(send(pieces[-1], count, stride, size))
        gathered = jnp.concatenate(pieces, axis=0)
    return gathered


def near_places(count):
    me = lax.axis_index("fsdp")
    others = jnp.arange(count, dtype=jnp.int32)
    places = jnp.zeros((count,), jnp.int32)
    weight = 1
    for stride, size in hop_plan(count):
        steps = ((me // stride) % size - (others // stride) % size) % size
        places = places + steps * weight
        weight *= size
    return places


def mesh_dims(count):
    if count == 32:
        return (4, 2, 2, 2)
    return (2,) * (count.bit_length() - 1)


def fold(parts, axis, stride, count):
    size = parts[0].shape[axis]
    mine = (lax.axis_index("fsdp") // stride) % size

    def entry(index):
        picked = [lax.dynamic_index_in_dim(part, index, axis, keepdims=False) for part in parts]
        return picked[0] if len(picked) == 1 else jnp.concatenate(picked, axis=-2)

    arrived = [
        send(entry((mine + step) % size), count, stride, size, step) for step in range(1, size)
    ]
    total = entry(mine).astype(jnp.float32)
    for piece in arrived:
        total = total + piece.astype(jnp.float32)
    return total


def scatter_sum(parts, count):
    dims = mesh_dims(count)
    strides = [1]
    for size in reversed(dims[1:]):
        strides.insert(0, strides[0] * size)
    last = len(dims) - 1
    shaped = [part.reshape(dims + part.shape[1:]) for part in parts]
    paired = fold(shaped, last, strides[last], count).astype(jnp.bfloat16)
    half = paired.shape[-2] // 2
    results = []
    for lane, order in enumerate((range(last - 1, -1, -1), range(last - 1, -1, -1))):
        axes = list(range(last))
        chosen_axes = list(order)
        if lane == 1 and last >= 2:
            chosen_axes[0], chosen_axes[1] = chosen_axes[1], chosen_axes[0]
        value = paired[..., :half, :] if lane == 0 else paired[..., half:, :]
        for step, axis in enumerate(chosen_axes):
            place = axes.index(axis)
            value = fold([value], place, strides[axis], count)
            axes.remove(axis)
            if step + 1 < last:
                value = value.astype(jnp.bfloat16)
        results.append(value)
    return jnp.concatenate(results, axis=0)


def sum_all(value, count):
    stride = 1
    while stride < count:
        value = value + send(value, count, stride, 2)
        stride *= 2
    return value


def pair_scores(queries, keys_all, first_half):
    only = jnp.where(first_half, queries, jnp.zeros_like(queries))
    return only, right_product(only, keys_all) * HD ** (-0.5)


def attention_forward_kernel(queries_ref, keys_ref, values_ref, mixed_ref, total_ref):
    lanes = lax.broadcasted_iota(jnp.int32, (TOK, 2 * HD), 1)
    totals = jnp.zeros((TOK, 2 * HD), jnp.float32)
    for pair in range(HEADS // 2):
        span = slice(pair * 2 * HD, (pair + 1) * 2 * HD)
        queries, keys_all, values_all = queries_ref[:, span], keys_ref[:, span], values_ref[:, span]
        halves = []
        for half in range(2):
            mine = (lanes < HD) if half == 0 else (lanes >= HD)
            unused, scores = pair_scores(queries, keys_all, mine)
            row_max = jnp.max(scores, axis=1, keepdims=True)
            raised = jnp.exp(scores - row_max)
            row_sum = jnp.sum(raised, axis=1, keepdims=True)
            soft_low = (raised / row_sum).astype(jnp.bfloat16)
            halves.append(product(soft_low, values_all))
            totals = jnp.where(lanes == 2 * pair + half, row_max + jnp.log(row_sum), totals)
        mixed_ref[:, span] = jnp.where(lanes < HD, halves[0], halves[1]).astype(jnp.bfloat16)
    total_ref[...] = totals


def attention_backward_kernel(
    queries_ref, keys_ref, values_ref, total_ref, grad_ref, dqueries_ref, dkeys_ref, dvalues_ref
):
    lanes = lax.broadcasted_iota(jnp.int32, (TOK, 2 * HD), 1)
    for pair in range(HEADS // 2):
        span = slice(pair * 2 * HD, (pair + 1) * 2 * HD)
        queries, keys_all, values_all = queries_ref[:, span], keys_ref[:, span], values_ref[:, span]
        grads = grad_ref[:, span]
        made = []
        for half in range(2):
            mine = (lanes < HD) if half == 0 else (lanes >= HD)
            unused, scores = pair_scores(queries, keys_all, mine)
            head = 2 * pair + half
            soft_weights = jnp.exp(scores - total_ref[:, head : head + 1])
            grad_values = left_product(soft_weights.astype(jnp.bfloat16), grads)
            grad_soft = right_product(jnp.where(mine, grads, jnp.zeros_like(grads)), values_all)
            spread = jnp.sum(soft_weights * grad_soft, axis=1, keepdims=True)
            score_low = (soft_weights * (grad_soft - spread)).astype(jnp.bfloat16)
            made.append(
                (
                    product(score_low, keys_all) * HD ** (-0.5),
                    left_product(score_low, queries) * HD ** (-0.5),
                    grad_values,
                )
            )
        for part, target in enumerate((dqueries_ref, dkeys_ref, dvalues_ref)):
            target[:, span] = jnp.where(lanes < HD, made[0][part], made[1][part]).astype(
                jnp.bfloat16
            )


def token_block(width):
    return pl.BlockSpec((TOK, width), lambda sample: (sample, 0))


def attention_forward(packed_low, sample_count):
    row_count = sample_count * TOK
    return pl.pallas_call(
        attention_forward_kernel,
        grid=(sample_count,),
        in_specs=[token_block(D)] * 3,
        out_specs=[token_block(D), token_block(2 * HD)],
        out_shape=[
            jax.ShapeDtypeStruct((row_count, D), jnp.bfloat16),
            jax.ShapeDtypeStruct((row_count, 2 * HD), jnp.float32),
        ],
        name="attention_forward",
    )(*packed_low)


def attention_backward(packed_low, log_total, grad_mixed_low, sample_count):
    row_count = sample_count * TOK
    return pl.pallas_call(
        attention_backward_kernel,
        grid=(sample_count,),
        in_specs=[token_block(D)] * 3 + [token_block(2 * HD), token_block(D)],
        out_specs=[token_block(D)] * 3,
        out_shape=[jax.ShapeDtypeStruct((row_count, D), jnp.bfloat16)] * 3,
        name="attention_backward",
    )(*packed_low, log_total, grad_mixed_low)


def adam_step(weight_now, grad_now, first_old, second_old, factor):
    clipped = grad_now * factor
    first_new = beta_first * first_old + (1.0 - beta_first) * clipped
    second_new = beta_second * second_old + (1.0 - beta_second) * clipped * clipped
    step_size = -learn_rate * (
        first_new / first_fix / (jnp.sqrt(second_new / second_fix) + adam_eps)
        + weight_decay * weight_now
    )
    return (step_size, first_new, second_new)


def body(
    latents,
    noise,
    timesteps,
    labels,
    qkv_weight,
    proj_weight,
    up_weight,
    down_weight,
    mod_weight,
    tables,
    biases,
    qkv_first,
    proj_first,
    up_first,
    down_first,
    mod_first,
    tables_first,
    biases_first,
    qkv_second,
    proj_second,
    up_second,
    down_second,
    mod_second,
    tables_second,
    biases_second,
):
    count = lax.axis_size("fsdp")
    me = lax.axis_index("fsdp")
    local = latents.shape[0]
    samples = local * count
    rows = D // count
    row_count = local * TOK
    total_count = samples * TOK * PD
    low = jnp.bfloat16
    f32 = jnp.float32
    layer_parts, global_parts = bias_parts(biases)
    final_bias, patch_bias, first_bias, second_bias, head_bias = global_parts
    mod_bias = jnp.concatenate([part_item[5] for part_item in layer_parts] + [final_bias])

    gathered = []
    for layer_index in range(LAYERS):
        pieces = [qkv_weight[layer_index][:, part * D : (part + 1) * D] for part in range(3)]
        pieces.append(proj_weight[layer_index])
        pieces += [up_weight[layer_index][:, part * D : (part + 1) * D] for part in range(4)]
        pieces.append(down_weight[layer_index])
        packed = jnp.concatenate(pieces, axis=0).astype(low)
        gathered.append(
            lax.all_gather(packed, "fsdp", axis=0, tiled=True).reshape(count, 12 * rows, D)
        )

    mod_low = mod_weight.astype(low)
    mod_columns = lax.all_to_all(mod_low, "fsdp", split_axis=1, concat_axis=0, tiled=True)
    digits = jnp.concatenate([timesteps // 32, timesteps % 32, labels // 32, labels % 32]).astype(low)
    table_low = tables.astype(low).T
    room = -(-CLASSES // 128) * 128
    first_at, class_at, patch_at = D, D + FREQ, D + FREQ + room
    head_at, digit_at = patch_at + PD, patch_at + 2 * PD
    tables_low = jnp.concatenate(
        [
            table_low[:, PD + FREQ : PD + FREQ + D],
            table_low[:, PD : PD + FREQ],
            table_low[:, PD + FREQ + D : PD + FREQ + D + CLASSES],
            jnp.zeros((rows, room - CLASSES), low),
            table_low[:, :PD],
            table_low[:, PD + FREQ + D + CLASSES :],
            jnp.broadcast_to(digits[None, :], (rows, 4 * local)),
        ],
        axis=1,
    )
    tables_near = gather_near(tables_low, count)
    places = near_places(count)
    tables_far = jnp.take(tables_near, places, axis=0, mode="clip")
    tables_full = tables_far.reshape(D, digit_at + 4 * local)
    second_near = tables_near[:, :, :D].reshape(D, D)

    def read_digits(from_devices):
        numbers = from_devices[:, 0, digit_at:].astype(jnp.int32).reshape(count, 4, local)
        steps_all = (numbers[:, 0] * 32 + numbers[:, 1]).reshape(samples)
        labels_all = (numbers[:, 2] * 32 + numbers[:, 3]).reshape(samples)
        return steps_all, labels_all

    def embed(steps_all):
        features_low = time_features(steps_all).astype(low)
        first_pre = right_product(features_low, tables_full[:, first_at:class_at]) + first_bias
        return features_low, first_pre, jax.nn.silu(first_pre).astype(low)

    def chosen(labels_all):
        return (labels_all[:, None] == jnp.arange(room, dtype=jnp.int32)[None, :]).astype(low)

    steps_far, labels_far = read_digits(tables_far)
    features_far, first_pre_far, first_low_far = embed(steps_far)
    condition_far = (
        right_product(first_low_far, tables_full[:, :D])
        + second_bias
        + right_product(chosen(labels_far), tables_full[:, class_at:patch_at])
    )
    mods_columns = product(jax.nn.silu(condition_far).astype(low), mod_columns)
    modulations = (
        lax.all_to_all(mods_columns, "fsdp", split_axis=0, concat_axis=1, tiled=True) + mod_bias
    )

    keep_share = noise_share(timesteps)
    noised = (
        jnp.sqrt(keep_share)[:, None, None] * latents
        + jnp.sqrt(1.0 - keep_share)[:, None, None] * noise
    )
    noised_low = noised.reshape(row_count, PD).astype(low)
    patch_columns = tables_full[:, patch_at:head_at]
    head_columns = tables_full[:, head_at:digit_at]
    residual = (right_product(noised_low, patch_columns) + patch_bias).reshape(local, TOK, D)

    def weights_of(layer_index):
        whole = gathered[layer_index]
        square = [
            whole[:, part * rows : (part + 1) * rows].reshape(D, D) for part in range(8)
        ]
        up_full = jnp.concatenate(square[4:], axis=1)
        down_full = whole[:, 8 * rows :].reshape(FF, D)
        return square[:3], square[3], up_full, down_full

    stored = []
    for layer_index in range(LAYERS):
        gathered[layer_index], residual = lax.optimization_barrier(
            (gathered[layer_index], residual)
        )
        qkv_full, proj_full, up_full, down_full = weights_of(layer_index)
        query_bias, value_bias, proj_bias, up_bias, down_bias, unused = layer_parts[layer_index]
        segment = modulations[:, layer_index * 6 * D : (layer_index + 1) * 6 * D]
        mod_terms = [segment[:, part_index * D : (part_index + 1) * D] for part_index in range(6)]
        shift_attn, scale_attn, gate_attn, shift_mlp, scale_mlp, gate_mlp = mod_terms
        residual_in = residual
        hidden_low = modulate(residual_in, shift_attn, scale_attn).reshape(row_count, D).astype(low)
        packed_low = [
            (product(hidden_low, qkv_full[0]) + query_bias).astype(low),
            product(hidden_low, qkv_full[1]).astype(low),
            (product(hidden_low, qkv_full[2]) + value_bias).astype(low),
        ]
        mixed, log_total = attention_forward(packed_low, local)
        mixed_low = mixed.astype(low)
        attn_out = (product(mixed_low, proj_full) + proj_bias).reshape(local, TOK, D)
        residual_mid = residual_in + gate_attn[:, None, :] * attn_out
        hidden_two_low = modulate(residual_mid, shift_mlp, scale_mlp).reshape(row_count, D).astype(low)
        pre_act = product(hidden_two_low, up_full) + up_bias
        act_low = gelu_tanh(pre_act).astype(low)
        mlp_out = (product(act_low, down_full) + down_bias).reshape(local, TOK, D)
        residual = residual_mid + gate_mlp[:, None, :] * mlp_out
        stored.append(
            (
                residual_in,
                hidden_low,
                packed_low,
                log_total,
                mixed_low,
                attn_out,
                residual_mid,
                hidden_two_low,
                pre_act,
                act_low,
                mlp_out,
            )
        )
    final_mods = modulations[:, LAYERS * 6 * D :]
    final_hidden = modulate(residual, final_mods[:, :D], final_mods[:, D:])
    final_low = final_hidden.reshape(row_count, D).astype(low)
    predicted = product(final_low, head_columns) + head_bias
    errors = predicted - noise.reshape(row_count, PD)
    loss_local = jnp.sum(errors * errors) / total_count
    grad_pred_low = (2.0 * errors / total_count).astype(low)
    grad_head_bias = jnp.sum(grad_pred_low.astype(f32), axis=0)
    grad_head = left_product(grad_pred_low, final_low)
    grad_final = right_product(grad_pred_low, head_columns).reshape(local, TOK, D)
    unused, final_pull = jax.vjp(modulate, residual, final_mods[:, :D], final_mods[:, D:])
    grad_residual, grad_shift_final, grad_scale_final = final_pull(grad_final)
    mod_grads = [None] * LAYERS
    shards = [None] * LAYERS
    bias_pieces = [None] * LAYERS
    for layer_index in reversed(range(LAYERS)):
        qkv_full, proj_full, up_full, down_full = weights_of(layer_index)
        (
            residual_in,
            hidden_low,
            packed_low,
            log_total,
            mixed_low,
            attn_out,
            residual_mid,
            hidden_two_low,
            pre_act,
            act_low,
            mlp_out,
        ) = stored[layer_index]
        segment = modulations[:, layer_index * 6 * D : (layer_index + 1) * 6 * D]
        mod_terms = [segment[:, part_index * D : (part_index + 1) * D] for part_index in range(6)]
        shift_attn, scale_attn, gate_attn, shift_mlp, scale_mlp, gate_mlp = mod_terms
        grad_gate_mlp = jnp.sum(grad_residual * mlp_out, axis=1)
        grad_mlp_low = (grad_residual * gate_mlp[:, None, :]).reshape(row_count, D).astype(low)
        grad_down_bias = jnp.sum(grad_mlp_low.astype(f32), axis=0)
        grad_down = left_product(act_low, grad_mlp_low)
        grad_act = right_product(grad_mlp_low, down_full)
        unused, gelu_pull = jax.vjp(gelu_tanh, pre_act)
        grad_pre_low = gelu_pull(grad_act)[0].astype(low)
        grad_up_bias = jnp.sum(grad_pre_low.astype(f32), axis=0)
        grad_up = left_product(hidden_two_low, grad_pre_low)
        grad_hidden_two = right_product(grad_pre_low, up_full).reshape(local, TOK, D)
        unused, mlp_pull = jax.vjp(modulate, residual_mid, shift_mlp, scale_mlp)
        part_residual, grad_shift_mlp, grad_scale_mlp = mlp_pull(grad_hidden_two)
        grad_residual = grad_residual + part_residual
        grad_gate_attn = jnp.sum(grad_residual * attn_out, axis=1)
        grad_attn_low = (grad_residual * gate_attn[:, None, :]).reshape(row_count, D).astype(low)
        grad_proj_bias = jnp.sum(grad_attn_low.astype(f32), axis=0)
        grad_proj = left_product(mixed_low, grad_attn_low)
        grad_mixed_low = right_product(grad_attn_low, proj_full).astype(low)
        grad_packed_low = attention_backward(packed_low, log_total, grad_mixed_low, local)
        grad_query_bias = jnp.sum(grad_packed_low[0].astype(f32), axis=0)
        grad_value_bias = jnp.sum(grad_packed_low[2].astype(f32), axis=0)
        grad_qkv = [left_product(hidden_low, item) for item in grad_packed_low]
        grad_hidden = (
            right_product(grad_packed_low[0], qkv_full[0])
            + right_product(grad_packed_low[1], qkv_full[1])
            + right_product(grad_packed_low[2], qkv_full[2])
        ).reshape(local, TOK, D)
        unused, attn_pull = jax.vjp(modulate, residual_in, shift_attn, scale_attn)
        part_residual, grad_shift_attn, grad_scale_attn = attn_pull(grad_hidden)
        grad_residual = grad_residual + part_residual
        mod_grads[layer_index] = jnp.concatenate(
            [
                grad_shift_attn,
                grad_scale_attn,
                grad_gate_attn,
                grad_shift_mlp,
                grad_scale_mlp,
                grad_gate_mlp,
            ],
            axis=1,
        )
        sent = [item.astype(low).reshape(count, rows, D) for item in grad_qkv + [grad_proj]]
        sent += [
            grad_up[:, part * D : (part + 1) * D].astype(low).reshape(count, rows, D)
            for part in range(4)
        ]
        sent.append(grad_down.astype(low).reshape(count, 4 * rows, D))
        if layer_index > 0:
            sent = jnp.concatenate(sent, axis=1).reshape(count * 12 * rows, D)
            sent, grad_residual = lax.optimization_barrier((sent, grad_residual))
            shard = lax.psum_scatter(sent, "fsdp", scatter_dimension=0, tiled=True).astype(f32)
        else:
            shard = scatter_sum(sent, count)
        parts = [shard[part * rows : (part + 1) * rows] for part in range(8)]
        shards[layer_index] = (
            jnp.concatenate(parts[:3], axis=1),
            parts[3],
            jnp.concatenate(parts[4:], axis=1),
            shard[8 * rows :],
        )
        bias_pieces[layer_index] = [
            grad_query_bias,
            grad_value_bias,
            grad_proj_bias,
            grad_up_bias,
            grad_down_bias,
        ]
    grad_zero_low = grad_residual.reshape(row_count, D).astype(low)
    grad_patch_bias = jnp.sum(grad_zero_low.astype(f32), axis=0)
    grad_patch = left_product(noised_low, grad_zero_low)

    grad_mods_low = jnp.concatenate(mod_grads + [grad_shift_final, grad_scale_final], axis=1)
    grad_mods_near = gather_near(grad_mods_low.astype(low), count).reshape(samples, MODW)
    steps_near, labels_near = read_digits(tables_near)
    unused, unused_pre, first_low = embed(steps_near)
    class_near = chosen(labels_near)
    own_second = tables_low[:, :D]
    own_class = tables_low[:, class_at:patch_at]
    own_bias = lax.dynamic_slice(second_bias, (me * rows,), (rows,))
    condition = (
        right_product(first_low, own_second) + own_bias + right_product(class_near, own_class)
    )
    condition_act, silu_pull = jax.vjp(jax.nn.silu, condition)
    shard_mod = left_product(condition_act.astype(low), grad_mods_near)
    grad_mod_bias = jnp.sum(grad_mods_near.astype(f32), axis=0)
    grad_condition = silu_pull(right_product(grad_mods_near, mod_low))[0]
    grad_class = lax.dot_general(
        class_near.astype(f32),
        grad_condition,
        (((0,), (0,)), ((), ())),
        precision=lax.Precision.HIGHEST,
        preferred_element_type=f32,
    )[:CLASSES]
    grad_time_low = grad_condition.astype(low)
    grad_second_bias = jnp.sum(grad_time_low.astype(f32), axis=0)
    grad_second = left_product(first_low, grad_time_low)
    far_order = (places[:, None] * local + jnp.arange(local, dtype=jnp.int32)[None, :]).reshape(-1)
    reorder = (jnp.arange(samples, dtype=jnp.int32)[:, None] == far_order[None, :]).astype(low)
    grad_time_far = left_product(grad_time_low, reorder).astype(low)
    grad_time_near = gather_near(grad_time_far, count).reshape(D, samples)
    grad_first_act = left_product(grad_time_near, second_near)
    unused, first_pull = jax.vjp(jax.nn.silu, first_pre_far)
    grad_first_low = first_pull(grad_first_act)[0].astype(low)
    grad_first_low = lax.dynamic_slice(grad_first_low, (0, me * rows), (samples, rows))
    grad_first_bias = jnp.sum(grad_first_low.astype(f32), axis=0)
    grad_first = left_product(features_far, grad_first_low)

    def spread(piece, length):
        return lax.dynamic_update_slice(jnp.zeros((length,), f32), piece, (me * piece.shape[0],))

    columns = MODW // count
    own_mod_bias = spread(lax.dynamic_slice(grad_mod_bias, (me * columns,), (columns,)), MODW)
    pieces = []
    for layer_index in range(LAYERS):
        pieces += bias_pieces[layer_index]
        pieces.append(own_mod_bias[layer_index * 6 * D : (layer_index + 1) * 6 * D])
    pieces += [
        own_mod_bias[LAYERS * 6 * D :],
        grad_patch_bias,
        spread(grad_first_bias, D),
        spread(grad_second_bias, D),
        grad_head_bias,
    ]
    ends = sum_all(jnp.concatenate([grad_patch, grad_head], axis=0), count)
    own_ends = lax.dynamic_slice(ends, (0, me * rows), (2 * PD, rows))
    shard_tables = jnp.concatenate(
        [own_ends[:PD], grad_first, grad_second, grad_class, own_ends[PD:]], axis=0
    )
    shard_squares = jnp.sum(shard_mod * shard_mod) + jnp.sum(shard_tables * shard_tables)
    for layer_index in range(LAYERS):
        for item in shards[layer_index]:
            shard_squares = shard_squares + jnp.sum(item * item)
    bias_length = biases.shape[0]
    pieces += [shard_squares[None], loss_local[None]]
    summed = sum_all(jnp.concatenate(pieces), count)
    bias_grad = summed[:bias_length]
    square_total = summed[bias_length]
    loss_value = summed[bias_length + 1]
    grad_norm = jnp.sqrt(square_total + jnp.sum(bias_grad * bias_grad))
    factor = jnp.minimum(1.0, clip_limit / (grad_norm + 1e-06))
    shard_qkv, shard_proj, shard_up, shard_down = [
        jnp.stack([shards[layer_index][part] for layer_index in range(LAYERS)]) for part in range(4)
    ]
    qkv_update, qkv_first_new, qkv_second_new = adam_step(
        qkv_weight, shard_qkv, qkv_first, qkv_second, factor
    )
    proj_update, proj_first_new, proj_second_new = adam_step(
        proj_weight, shard_proj, proj_first, proj_second, factor
    )
    up_update, up_first_new, up_second_new = adam_step(
        up_weight, shard_up, up_first, up_second, factor
    )
    down_update, down_first_new, down_second_new = adam_step(
        down_weight, shard_down, down_first, down_second, factor
    )
    mod_update, mod_first_new, mod_second_new = adam_step(
        mod_weight, shard_mod, mod_first, mod_second, factor
    )
    tables_update, tables_first_new, tables_second_new = adam_step(
        tables, shard_tables, tables_first, tables_second, factor
    )
    biases_update, biases_first_new, biases_second_new = adam_step(
        biases, bias_grad, biases_first, biases_second, factor
    )
    return (
        loss_value,
        grad_norm,
        qkv_update,
        qkv_first_new,
        qkv_second_new,
        proj_update,
        proj_first_new,
        proj_second_new,
        up_update,
        up_first_new,
        up_second_new,
        down_update,
        down_first_new,
        down_second_new,
        mod_update,
        mod_first_new,
        mod_second_new,
        tables_update,
        tables_first_new,
        tables_second_new,
        biases_update,
        biases_first_new,
        biases_second_new,
    )


def solution(mesh):
    in_specs = (
        P("fsdp", None, None),
        P("fsdp", None, None),
        P("fsdp"),
        P("fsdp"),
        P(None, "fsdp", None),
        P(None, "fsdp", None),
        P(None, "fsdp", None),
        P(None, "fsdp", None),
        P("fsdp", None),
        P(None, "fsdp"),
        P(),
        P(None, "fsdp", None),
        P(None, "fsdp", None),
        P(None, "fsdp", None),
        P(None, "fsdp", None),
        P("fsdp", None),
        P(None, "fsdp"),
        P(),
        P(None, "fsdp", None),
        P(None, "fsdp", None),
        P(None, "fsdp", None),
        P(None, "fsdp", None),
        P("fsdp", None),
        P(None, "fsdp"),
        P(),
    )
    out_specs = (
        P(),
        P(),
        P(None, "fsdp", None),
        P(None, "fsdp", None),
        P(None, "fsdp", None),
        P(None, "fsdp", None),
        P(None, "fsdp", None),
        P(None, "fsdp", None),
        P(None, "fsdp", None),
        P(None, "fsdp", None),
        P(None, "fsdp", None),
        P(None, "fsdp", None),
        P(None, "fsdp", None),
        P(None, "fsdp", None),
        P("fsdp", None),
        P("fsdp", None),
        P("fsdp", None),
        P(None, "fsdp"),
        P(None, "fsdp"),
        P(None, "fsdp"),
        P(),
        P(),
        P(),
    )
    return jax.shard_map(body, mesh=mesh, in_specs=in_specs, out_specs=out_specs, check_vma=False)
```

```python
import math

import jax
import jax.numpy as jnp
from jax import lax
from jax.experimental import pallas as pl
from jax.sharding import PartitionSpec as P

D = 768
HEADS = 12
HD = 64
FF = 3072
FREQ = 256
CLASSES = 1000
DIFF_STEPS = 1000
LAYERS = 2
TOK = 256
PD = 16
MODW = 10752


norm_eps = 1e-06
clip_limit = 2.5
learn_rate = 0.01
beta_first = 0.9
beta_second = 0.95
adam_eps = 1e-08
weight_decay = 0.01
first_fix = 1.0 - 0.9**10
second_fix = 1.0 - 0.95**10


def modulate(residual, shift_term, scale_term):
    centred = residual - jnp.mean(residual, axis=-1, keepdims=True)
    spread = jnp.mean(centred * centred, axis=-1, keepdims=True)
    normed = centred * lax.rsqrt(spread + norm_eps)
    return normed * (1.0 + scale_term[:, None, :]) + shift_term[:, None, :]


def gelu_tanh(values):
    return jax.nn.gelu(values, approximate=True)


def product(left_side, right_side):
    return jnp.dot(left_side, right_side, preferred_element_type=jnp.float32)


def left_product(left_side, right_side):
    return lax.dot_general(
        left_side, right_side, (((0,), (0,)), ((), ())), preferred_element_type=jnp.float32
    )


def right_product(left_side, right_side):
    return lax.dot_general(
        left_side, right_side, (((1,), (1,)), ((), ())), preferred_element_type=jnp.float32
    )


def time_features(steps_in):
    half_count = FREQ // 2
    frequencies = jnp.exp(
        -math.log(10000.0) * jnp.arange(half_count, dtype=jnp.float32) / half_count
    )
    angles = steps_in.astype(jnp.float32)[:, None] * frequencies[None, :]
    return jnp.concatenate([jnp.cos(angles), jnp.sin(angles)], axis=1)


def noise_share(steps_in):
    beta_values = jnp.linspace(0.0001, 0.02, DIFF_STEPS, dtype=jnp.float32)
    log_keep = jnp.log(1.0 - beta_values)
    taken = jnp.arange(DIFF_STEPS, dtype=jnp.int32)[None, :] <= steps_in[:, None]
    return jnp.exp(jnp.sum(jnp.where(taken, log_keep[None, :], 0.0), axis=1))


def bias_parts(biases):
    per_layer = 10 * D + FF
    layer_parts = []
    for layer_index in range(LAYERS):
        anchor = layer_index * per_layer
        layer_parts.append(
            (
                biases[anchor : anchor + D],
                biases[anchor + D : anchor + 2 * D],
                biases[anchor + 2 * D : anchor + 3 * D],
                biases[anchor + 3 * D : anchor + 3 * D + FF],
                biases[anchor + 3 * D + FF : anchor + 4 * D + FF],
                biases[anchor + 4 * D + FF : anchor + per_layer],
            )
        )
    anchor = LAYERS * per_layer
    global_parts = (
        biases[anchor : anchor + 2 * D],
        biases[anchor + 2 * D : anchor + 3 * D],
        biases[anchor + 3 * D : anchor + 4 * D],
        biases[anchor + 4 * D : anchor + 5 * D],
        biases[anchor + 5 * D : anchor + 5 * D + PD],
    )
    return (layer_parts, global_parts)


def hop_plan(count):
    if count == 32:
        return [(8, 4), (2, 2), (4, 2), (1, 2)]
    plan = []
    stride = 1
    while stride < count:
        plan.append((stride, 2))
        stride *= 2
    return plan


def shifted(index, stride, size, amount):
    coord = (index // stride) % size
    return index + ((coord + amount) % size - coord) * stride


def send(value, count, stride, size, amount=1):
    pairs = [(index, shifted(index, stride, size, amount)) for index in range(count)]
    return lax.ppermute(value, "fsdp", pairs)


def gather_near(value, count):
    gathered = value[None]
    for stride, size in hop_plan(count):
        pieces = [gathered]
        for unused in range(size - 1):
            pieces.append(send(pieces[-1], count, stride, size))
        gathered = jnp.concatenate(pieces, axis=0)
    return gathered


def near_places(count):
    me = lax.axis_index("fsdp")
    others = jnp.arange(count, dtype=jnp.int32)
    places = jnp.zeros((count,), jnp.int32)
    weight = 1
    for stride, size in hop_plan(count):
        steps = ((me // stride) % size - (others // stride) % size) % size
        places = places + steps * weight
        weight *= size
    return places


def mesh_dims(count):
    if count == 32:
        return (4, 2, 2, 2)
    return (2,) * (count.bit_length() - 1)


def fold(parts, axis, stride, count):
    size = parts[0].shape[axis]
    mine = (lax.axis_index("fsdp") // stride) % size

    def entry(index):
        picked = [lax.dynamic_index_in_dim(part, index, axis, keepdims=False) for part in parts]
        return picked[0] if len(picked) == 1 else jnp.concatenate(picked, axis=-2)

    arrived = [
        send(entry((mine + step) % size), count, stride, size, step) for step in range(1, size)
    ]
    total = entry(mine).astype(jnp.float32)
    for piece in arrived:
        total = total + piece.astype(jnp.float32)
    return total


def scatter_sum(parts, count, after):
    dims = mesh_dims(count)
    strides = [1]
    for size in reversed(dims[1:]):
        strides.insert(0, strides[0] * size)
    last = len(dims) - 1
    shaped = [part.reshape(dims + part.shape[1:]) for part in parts]
    paired = fold(shaped, last, strides[last], count).astype(jnp.bfloat16)
    paired, after = lax.optimization_barrier((paired, after))
    half = paired.shape[-2] // 2
    results = []
    for lane, order in enumerate((range(last - 1, -1, -1), range(last - 1, -1, -1))):
        axes = list(range(last))
        chosen_axes = list(order)
        if lane == 1 and last >= 2:
            chosen_axes[0], chosen_axes[1] = chosen_axes[1], chosen_axes[0]
        value = paired[..., :half, :] if lane == 0 else paired[..., half:, :]
        for step, axis in enumerate(chosen_axes):
            place = axes.index(axis)
            value = fold([value], place, strides[axis], count)
            axes.remove(axis)
            if step + 1 < last:
                value = value.astype(jnp.bfloat16)
        results.append(value)
    return jnp.concatenate(results, axis=0), after


def sum_all(value, count):
    stride = 1
    while stride < count:
        value = value + send(value, count, stride, 2)
        stride *= 2
    return value


def pair_scores(queries, keys_all, first_half):
    only = jnp.where(first_half, queries, jnp.zeros_like(queries))
    return only, right_product(only, keys_all) * HD ** (-0.5)


def attention_forward_kernel(queries_ref, keys_ref, values_ref, mixed_ref, total_ref):
    lanes = lax.broadcasted_iota(jnp.int32, (TOK, 2 * HD), 1)
    totals = jnp.zeros((TOK, 2 * HD), jnp.float32)
    for pair in range(HEADS // 2):
        span = slice(pair * 2 * HD, (pair + 1) * 2 * HD)
        queries, keys_all, values_all = queries_ref[:, span], keys_ref[:, span], values_ref[:, span]
        halves = []
        for half in range(2):
            mine = (lanes < HD) if half == 0 else (lanes >= HD)
            unused, scores = pair_scores(queries, keys_all, mine)
            row_max = jnp.max(scores, axis=1, keepdims=True)
            raised = jnp.exp(scores - row_max)
            row_sum = jnp.sum(raised, axis=1, keepdims=True)
            soft_low = (raised / row_sum).astype(jnp.bfloat16)
            halves.append(product(soft_low, values_all))
            totals = jnp.where(lanes == 2 * pair + half, row_max + jnp.log(row_sum), totals)
        mixed_ref[:, span] = jnp.where(lanes < HD, halves[0], halves[1]).astype(jnp.bfloat16)
    total_ref[...] = totals


def attention_backward_kernel(
    queries_ref, keys_ref, values_ref, total_ref, grad_ref, dqueries_ref, dkeys_ref, dvalues_ref
):
    lanes = lax.broadcasted_iota(jnp.int32, (TOK, 2 * HD), 1)
    for pair in range(HEADS // 2):
        span = slice(pair * 2 * HD, (pair + 1) * 2 * HD)
        queries, keys_all, values_all = queries_ref[:, span], keys_ref[:, span], values_ref[:, span]
        grads = grad_ref[:, span]
        made = []
        for half in range(2):
            mine = (lanes < HD) if half == 0 else (lanes >= HD)
            unused, scores = pair_scores(queries, keys_all, mine)
            head = 2 * pair + half
            soft_weights = jnp.exp(scores - total_ref[:, head : head + 1])
            grad_values = left_product(soft_weights.astype(jnp.bfloat16), grads)
            grad_soft = right_product(jnp.where(mine, grads, jnp.zeros_like(grads)), values_all)
            spread = jnp.sum(soft_weights * grad_soft, axis=1, keepdims=True)
            score_low = (soft_weights * (grad_soft - spread)).astype(jnp.bfloat16)
            made.append(
                (
                    product(score_low, keys_all) * HD ** (-0.5),
                    left_product(score_low, queries) * HD ** (-0.5),
                    grad_values,
                )
            )
        for part, target in enumerate((dqueries_ref, dkeys_ref, dvalues_ref)):
            target[:, span] = jnp.where(lanes < HD, made[0][part], made[1][part]).astype(
                jnp.bfloat16
            )


def token_block(width):
    return pl.BlockSpec((TOK, width), lambda sample: (sample, 0))


def attention_forward(packed_low, sample_count):
    row_count = sample_count * TOK
    return pl.pallas_call(
        attention_forward_kernel,
        grid=(sample_count,),
        in_specs=[token_block(D)] * 3,
        out_specs=[token_block(D), token_block(2 * HD)],
        out_shape=[
            jax.ShapeDtypeStruct((row_count, D), jnp.bfloat16),
            jax.ShapeDtypeStruct((row_count, 2 * HD), jnp.float32),
        ],
        name="attention_forward",
    )(*packed_low)


def attention_backward(packed_low, log_total, grad_mixed_low, sample_count):
    row_count = sample_count * TOK
    return pl.pallas_call(
        attention_backward_kernel,
        grid=(sample_count,),
        in_specs=[token_block(D)] * 3 + [token_block(2 * HD), token_block(D)],
        out_specs=[token_block(D)] * 3,
        out_shape=[jax.ShapeDtypeStruct((row_count, D), jnp.bfloat16)] * 3,
        name="attention_backward",
    )(*packed_low, log_total, grad_mixed_low)


def adam_step(weight_now, grad_now, first_old, second_old, factor):
    clipped = grad_now * factor
    first_new = beta_first * first_old + (1.0 - beta_first) * clipped
    second_new = beta_second * second_old + (1.0 - beta_second) * clipped * clipped
    step_size = -learn_rate * (
        first_new / first_fix / (jnp.sqrt(second_new / second_fix) + adam_eps)
        + weight_decay * weight_now
    )
    return (step_size, first_new, second_new)


def body(
    latents,
    noise,
    timesteps,
    labels,
    qkv_weight,
    proj_weight,
    up_weight,
    down_weight,
    mod_weight,
    tables,
    biases,
    qkv_first,
    proj_first,
    up_first,
    down_first,
    mod_first,
    tables_first,
    biases_first,
    qkv_second,
    proj_second,
    up_second,
    down_second,
    mod_second,
    tables_second,
    biases_second,
):
    count = lax.axis_size("fsdp")
    me = lax.axis_index("fsdp")
    local = latents.shape[0]
    samples = local * count
    rows = D // count
    row_count = local * TOK
    total_count = samples * TOK * PD
    low = jnp.bfloat16
    f32 = jnp.float32
    layer_parts, global_parts = bias_parts(biases)
    final_bias, patch_bias, first_bias, second_bias, head_bias = global_parts
    mod_bias = jnp.concatenate([part_item[5] for part_item in layer_parts] + [final_bias])

    gathered = []
    for layer_index in range(LAYERS):
        pieces = [qkv_weight[layer_index][:, part * D : (part + 1) * D] for part in range(3)]
        pieces.append(proj_weight[layer_index])
        pieces += [up_weight[layer_index][:, part * D : (part + 1) * D] for part in range(4)]
        pieces.append(down_weight[layer_index])
        packed = jnp.concatenate(pieces, axis=0).astype(low)
        gathered.append(
            lax.all_gather(packed, "fsdp", axis=0, tiled=True).reshape(count, 12 * rows, D)
        )

    mod_low = mod_weight.astype(low)
    mod_columns = lax.all_to_all(mod_low, "fsdp", split_axis=1, concat_axis=0, tiled=True)
    digits = jnp.concatenate([timesteps // 32, timesteps % 32, labels // 32, labels % 32]).astype(low)
    table_low = tables.astype(low).T
    room = -(-CLASSES // 128) * 128
    first_at, class_at, patch_at = D, D + FREQ, D + FREQ + room
    head_at, digit_at = patch_at + PD, patch_at + 2 * PD
    tables_low = jnp.concatenate(
        [
            table_low[:, PD + FREQ : PD + FREQ + D],
            table_low[:, PD : PD + FREQ],
            table_low[:, PD + FREQ + D : PD + FREQ + D + CLASSES],
            jnp.zeros((rows, room - CLASSES), low),
            table_low[:, :PD],
            table_low[:, PD + FREQ + D + CLASSES :],
            jnp.broadcast_to(digits[None, :], (rows, 4 * local)),
        ],
        axis=1,
    )
    tables_near = gather_near(tables_low, count)
    places = near_places(count)
    tables_far = jnp.take(tables_near, places, axis=0, mode="clip")
    tables_full = tables_far.reshape(D, digit_at + 4 * local)

    numbers = tables_far[:, 0, digit_at:].astype(jnp.int32).reshape(count, 4, local)
    steps_all = (numbers[:, 0] * 32 + numbers[:, 1]).reshape(samples)
    labels_all = (numbers[:, 2] * 32 + numbers[:, 3]).reshape(samples)
    features_low = time_features(steps_all).astype(low)
    first_pre = right_product(features_low, tables_full[:, first_at:class_at]) + first_bias
    first_low = jax.nn.silu(first_pre).astype(low)
    class_rows = (labels_all[:, None] == jnp.arange(room, dtype=jnp.int32)[None, :]).astype(low)
    condition = (
        right_product(first_low, tables_full[:, :D])
        + second_bias
        + right_product(class_rows, tables_full[:, class_at:patch_at])
    )
    cond_low = jax.nn.silu(condition).astype(low)
    mods_columns = product(cond_low, mod_columns)
    modulations = (
        lax.all_to_all(mods_columns, "fsdp", split_axis=0, concat_axis=1, tiled=True) + mod_bias
    )

    keep_share = noise_share(timesteps)
    noised = (
        jnp.sqrt(keep_share)[:, None, None] * latents
        + jnp.sqrt(1.0 - keep_share)[:, None, None] * noise
    )
    noised_low = noised.reshape(row_count, PD).astype(low)
    patch_columns = tables_full[:, patch_at:head_at]
    head_columns = tables_full[:, head_at:digit_at]
    residual = (right_product(noised_low, patch_columns) + patch_bias).reshape(local, TOK, D)

    def weights_of(layer_index):
        whole = gathered[layer_index]
        square = [
            whole[:, part * rows : (part + 1) * rows].reshape(D, D) for part in range(8)
        ]
        up_full = jnp.concatenate(square[4:], axis=1)
        down_full = whole[:, 8 * rows :].reshape(FF, D)
        return square[:3], square[3], up_full, down_full

    stored = []
    for layer_index in range(LAYERS):
        gathered[layer_index], residual = lax.optimization_barrier(
            (gathered[layer_index], residual)
        )
        qkv_full, proj_full, up_full, down_full = weights_of(layer_index)
        query_bias, value_bias, proj_bias, up_bias, down_bias, unused = layer_parts[layer_index]
        segment = modulations[:, layer_index * 6 * D : (layer_index + 1) * 6 * D]
        mod_terms = [segment[:, part_index * D : (part_index + 1) * D] for part_index in range(6)]
        shift_attn, scale_attn, gate_attn, shift_mlp, scale_mlp, gate_mlp = mod_terms
        residual_in = residual
        hidden_low = modulate(residual_in, shift_attn, scale_attn).reshape(row_count, D).astype(low)
        packed_low = [
            (product(hidden_low, qkv_full[0]) + query_bias).astype(low),
            product(hidden_low, qkv_full[1]).astype(low),
            (product(hidden_low, qkv_full[2]) + value_bias).astype(low),
        ]
        mixed, log_total = attention_forward(packed_low, local)
        mixed_low = mixed.astype(low)
        attn_out = (product(mixed_low, proj_full) + proj_bias).reshape(local, TOK, D)
        residual_mid = residual_in + gate_attn[:, None, :] * attn_out
        hidden_two_low = modulate(residual_mid, shift_mlp, scale_mlp).reshape(row_count, D).astype(low)
        pre_act = product(hidden_two_low, up_full) + up_bias
        act_low = lax.optimization_barrier(gelu_tanh(pre_act).astype(low))
        mlp_out = (product(act_low, down_full) + down_bias).reshape(local, TOK, D)
        residual = residual_mid + gate_mlp[:, None, :] * mlp_out
        stored.append(
            (
                residual_in,
                hidden_low,
                packed_low,
                log_total,
                mixed_low,
                attn_out,
                residual_mid,
                hidden_two_low,
                pre_act,
                act_low,
                mlp_out,
            )
        )
    final_mods = modulations[:, LAYERS * 6 * D :]
    final_hidden = modulate(residual, final_mods[:, :D], final_mods[:, D:])
    final_low = final_hidden.reshape(row_count, D).astype(low)
    predicted = product(final_low, head_columns) + head_bias
    errors = predicted - noise.reshape(row_count, PD)
    loss_local = jnp.sum(errors * errors) / total_count
    grad_pred_low = (2.0 * errors / total_count).astype(low)
    grad_head_bias = jnp.sum(grad_pred_low.astype(f32), axis=0)
    grad_head = left_product(grad_pred_low, final_low)
    grad_final = right_product(grad_pred_low, head_columns).reshape(local, TOK, D)
    unused, final_pull = jax.vjp(modulate, residual, final_mods[:, :D], final_mods[:, D:])
    grad_residual, grad_shift_final, grad_scale_final = final_pull(grad_final)
    mod_grads = [None] * LAYERS
    shards = [None] * LAYERS
    bias_pieces = [None] * LAYERS
    for layer_index in reversed(range(LAYERS)):
        qkv_full, proj_full, up_full, down_full = weights_of(layer_index)
        (
            residual_in,
            hidden_low,
            packed_low,
            log_total,
            mixed_low,
            attn_out,
            residual_mid,
            hidden_two_low,
            pre_act,
            act_low,
            mlp_out,
        ) = stored[layer_index]
        segment = modulations[:, layer_index * 6 * D : (layer_index + 1) * 6 * D]
        mod_terms = [segment[:, part_index * D : (part_index + 1) * D] for part_index in range(6)]
        shift_attn, scale_attn, gate_attn, shift_mlp, scale_mlp, gate_mlp = mod_terms
        grad_gate_mlp = jnp.sum(grad_residual * mlp_out, axis=1)
        grad_mlp_low = (grad_residual * gate_mlp[:, None, :]).reshape(row_count, D).astype(low)
        grad_down_bias = jnp.sum(grad_mlp_low.astype(f32), axis=0)
        grad_down = left_product(act_low, grad_mlp_low)
        grad_act = right_product(grad_mlp_low, down_full)
        unused, gelu_pull = jax.vjp(gelu_tanh, pre_act)
        grad_pre_low = gelu_pull(grad_act)[0].astype(low)
        grad_up_bias = jnp.sum(grad_pre_low.astype(f32), axis=0)
        grad_up = left_product(hidden_two_low, grad_pre_low)
        grad_hidden_two = right_product(grad_pre_low, up_full).reshape(local, TOK, D)
        unused, mlp_pull = jax.vjp(modulate, residual_mid, shift_mlp, scale_mlp)
        part_residual, grad_shift_mlp, grad_scale_mlp = mlp_pull(grad_hidden_two)
        grad_residual = grad_residual + part_residual
        grad_gate_attn = jnp.sum(grad_residual * attn_out, axis=1)
        grad_attn_low = (grad_residual * gate_attn[:, None, :]).reshape(row_count, D).astype(low)
        grad_proj_bias = jnp.sum(grad_attn_low.astype(f32), axis=0)
        grad_proj = left_product(mixed_low, grad_attn_low)
        grad_mixed_low = right_product(grad_attn_low, proj_full).astype(low)
        grad_packed_low = attention_backward(packed_low, log_total, grad_mixed_low, local)
        grad_query_bias = jnp.sum(grad_packed_low[0].astype(f32), axis=0)
        grad_value_bias = jnp.sum(grad_packed_low[2].astype(f32), axis=0)
        grad_qkv = [left_product(hidden_low, item) for item in grad_packed_low]
        grad_hidden = (
            right_product(grad_packed_low[0], qkv_full[0])
            + right_product(grad_packed_low[1], qkv_full[1])
            + right_product(grad_packed_low[2], qkv_full[2])
        ).reshape(local, TOK, D)
        unused, attn_pull = jax.vjp(modulate, residual_in, shift_attn, scale_attn)
        part_residual, grad_shift_attn, grad_scale_attn = attn_pull(grad_hidden)
        grad_residual = grad_residual + part_residual
        mod_grads[layer_index] = jnp.concatenate(
            [
                grad_shift_attn,
                grad_scale_attn,
                grad_gate_attn,
                grad_shift_mlp,
                grad_scale_mlp,
                grad_gate_mlp,
            ],
            axis=1,
        )
        sent = [item.astype(low).reshape(count, rows, D) for item in grad_qkv + [grad_proj]]
        sent += [
            grad_up[:, part * D : (part + 1) * D].astype(low).reshape(count, rows, D)
            for part in range(4)
        ]
        sent.append(grad_down.astype(low).reshape(count, 4 * rows, D))
        if layer_index > 0:
            sent = jnp.concatenate(sent, axis=1).reshape(count * 12 * rows, D)
            sent, grad_residual = lax.optimization_barrier((sent, grad_residual))
            shard = lax.psum_scatter(sent, "fsdp", scatter_dimension=0, tiled=True).astype(f32)
        else:
            mod_grads[0], grad_residual = lax.optimization_barrier((mod_grads[0], grad_residual))
            shard, mod_grads[0] = scatter_sum(sent, count, mod_grads[0])
        parts = [shard[part * rows : (part + 1) * rows] for part in range(8)]
        shards[layer_index] = (
            jnp.concatenate(parts[:3], axis=1),
            parts[3],
            jnp.concatenate(parts[4:], axis=1),
            shard[8 * rows :],
        )
        bias_pieces[layer_index] = [
            grad_query_bias,
            grad_value_bias,
            grad_proj_bias,
            grad_up_bias,
            grad_down_bias,
        ]
    grad_zero_low = grad_residual.reshape(row_count, D).astype(low)
    grad_patch_bias = jnp.sum(grad_zero_low.astype(f32), axis=0)
    grad_patch = left_product(noised_low, grad_zero_low)

    grad_mods_low = jnp.concatenate(mod_grads + [grad_shift_final, grad_scale_final], axis=1)
    grad_mods_columns = lax.all_to_all(
        grad_mods_low.astype(low), "fsdp", split_axis=1, concat_axis=0, tiled=True
    )
    grad_act = lax.all_to_all(
        right_product(mod_columns, grad_mods_columns), "fsdp", split_axis=0, concat_axis=0, tiled=True
    )
    grad_act = jnp.sum(grad_act.reshape(count, rows, samples), axis=0)
    shard_mod = lax.all_to_all(
        left_product(cond_low, grad_mods_columns).astype(low),
        "fsdp",
        split_axis=0,
        concat_axis=1,
        tiled=True,
    ).astype(f32)
    own_bias = lax.dynamic_slice(second_bias, (me * rows,), (rows,))
    condition_own = (
        right_product(tables_low[:, :D], first_low)
        + own_bias[:, None]
        + right_product(tables_low[:, class_at:patch_at], class_rows)
    )
    unused, silu_pull = jax.vjp(jax.nn.silu, condition_own)
    grad_condition = silu_pull(grad_act)[0]
    grad_class = lax.dot_general(
        grad_condition,
        class_rows.astype(f32),
        (((1,), (0,)), ((), ())),
        precision=lax.Precision.HIGHEST,
        preferred_element_type=f32,
    )[:, :CLASSES]
    grad_time_low = grad_condition.astype(low)
    grad_second_bias = jnp.sum(grad_time_low.astype(f32), axis=1)
    grad_second = product(grad_time_low, first_low)
    grad_time_all = lax.all_to_all(
        jnp.broadcast_to(grad_time_low[None], (count, rows, samples)).reshape(D, samples),
        "fsdp",
        split_axis=0,
        concat_axis=0,
        tiled=True,
    )
    grad_first_act = lax.dynamic_slice(
        left_product(tables_full[:, :D], grad_time_all), (me * rows, 0), (rows, samples)
    )
    own_bias = lax.dynamic_slice(first_bias, (me * rows,), (rows,))
    first_pre_own = right_product(tables_low[:, first_at:class_at], features_low) + own_bias[:, None]
    unused, first_pull = jax.vjp(jax.nn.silu, first_pre_own)
    grad_first_low = first_pull(grad_first_act)[0].astype(low)
    grad_first_bias = jnp.sum(grad_first_low.astype(f32), axis=1)
    grad_first = product(grad_first_low, features_low)
    grad_middle = jnp.concatenate([grad_first, grad_second, grad_class], axis=1).T

    def spread(piece, length):
        return lax.dynamic_update_slice(jnp.zeros((length,), f32), piece, (me * piece.shape[0],))

    own_mod_bias = spread(jnp.sum(grad_mods_columns.astype(f32), axis=0), MODW)
    pieces = []
    for layer_index in range(LAYERS):
        pieces += bias_pieces[layer_index]
        pieces.append(own_mod_bias[layer_index * 6 * D : (layer_index + 1) * 6 * D])
    pieces += [
        own_mod_bias[LAYERS * 6 * D :],
        grad_patch_bias,
        spread(grad_first_bias, D),
        spread(grad_second_bias, D),
        grad_head_bias,
    ]
    pieces += [grad_patch.reshape(-1), grad_head.reshape(-1)]
    summed = sum_all(jnp.concatenate(pieces), count)
    bias_length = biases.shape[0]
    bias_grad = summed[:bias_length]
    ends = summed[bias_length:].reshape(2 * PD, D)
    own_ends = lax.dynamic_slice(ends, (0, me * rows), (2 * PD, rows))
    shard_tables = jnp.concatenate([own_ends[:PD], grad_middle, own_ends[PD:]], axis=0)
    shard_squares = jnp.sum(shard_mod * shard_mod) + jnp.sum(shard_tables * shard_tables)
    for layer_index in range(LAYERS):
        for item in shards[layer_index]:
            shard_squares = shard_squares + jnp.sum(item * item)
    square_total, loss_value = sum_all(jnp.stack([shard_squares, loss_local]), count)
    grad_norm = jnp.sqrt(square_total + jnp.sum(bias_grad * bias_grad))
    factor = jnp.minimum(1.0, clip_limit / (grad_norm + 1e-06))
    shard_qkv, shard_proj, shard_up, shard_down = [
        jnp.stack([shards[layer_index][part] for layer_index in range(LAYERS)]) for part in range(4)
    ]
    qkv_update, qkv_first_new, qkv_second_new = adam_step(
        qkv_weight, shard_qkv, qkv_first, qkv_second, factor
    )
    proj_update, proj_first_new, proj_second_new = adam_step(
        proj_weight, shard_proj, proj_first, proj_second, factor
    )
    up_update, up_first_new, up_second_new = adam_step(
        up_weight, shard_up, up_first, up_second, factor
    )
    down_update, down_first_new, down_second_new = adam_step(
        down_weight, shard_down, down_first, down_second, factor
    )
    mod_update, mod_first_new, mod_second_new = adam_step(
        mod_weight, shard_mod, mod_first, mod_second, factor
    )
    tables_update, tables_first_new, tables_second_new = adam_step(
        tables, shard_tables, tables_first, tables_second, factor
    )
    biases_update, biases_first_new, biases_second_new = adam_step(
        biases, bias_grad, biases_first, biases_second, factor
    )
    return (
        loss_value,
        grad_norm,
        qkv_update,
        qkv_first_new,
        qkv_second_new,
        proj_update,
        proj_first_new,
        proj_second_new,
        up_update,
        up_first_new,
        up_second_new,
        down_update,
        down_first_new,
        down_second_new,
        mod_update,
        mod_first_new,
        mod_second_new,
        tables_update,
        tables_first_new,
        tables_second_new,
        biases_update,
        biases_first_new,
        biases_second_new,
    )


def solution(mesh):
    in_specs = (
        P("fsdp", None, None),
        P("fsdp", None, None),
        P("fsdp"),
        P("fsdp"),
        P(None, "fsdp", None),
        P(None, "fsdp", None),
        P(None, "fsdp", None),
        P(None, "fsdp", None),
        P("fsdp", None),
        P(None, "fsdp"),
        P(),
        P(None, "fsdp", None),
        P(None, "fsdp", None),
        P(None, "fsdp", None),
        P(None, "fsdp", None),
        P("fsdp", None),
        P(None, "fsdp"),
        P(),
        P(None, "fsdp", None),
        P(None, "fsdp", None),
        P(None, "fsdp", None),
        P(None, "fsdp", None),
        P("fsdp", None),
        P(None, "fsdp"),
        P(),
    )
    out_specs = (
        P(),
        P(),
        P(None, "fsdp", None),
        P(None, "fsdp", None),
        P(None, "fsdp", None),
        P(None, "fsdp", None),
        P(None, "fsdp", None),
        P(None, "fsdp", None),
        P(None, "fsdp", None),
        P(None, "fsdp", None),
        P(None, "fsdp", None),
        P(None, "fsdp", None),
        P(None, "fsdp", None),
        P(None, "fsdp", None),
        P("fsdp", None),
        P("fsdp", None),
        P("fsdp", None),
        P(None, "fsdp"),
        P(None, "fsdp"),
        P(None, "fsdp"),
        P(),
        P(),
        P(),
    )
    return jax.shard_map(body, mesh=mesh, in_specs=in_specs, out_specs=out_specs, check_vma=False)
```

```python
import math

import jax
import jax.numpy as jnp
from jax import lax
from jax.experimental import pallas as pl
from jax.sharding import PartitionSpec as P

D = 768
HEADS = 12
HD = 64
FF = 3072
FREQ = 256
CLASSES = 1000
DIFF_STEPS = 1000
LAYERS = 2
TOK = 256
PD = 16
MODW = 10752


norm_eps = 1e-06
clip_limit = 2.5
learn_rate = 0.01
beta_first = 0.9
beta_second = 0.95
adam_eps = 1e-08
weight_decay = 0.01
first_fix = 1.0 - 0.9**10
second_fix = 1.0 - 0.95**10


def modulate(residual, shift_term, scale_term):
    centred = residual - jnp.mean(residual, axis=-1, keepdims=True)
    spread = jnp.mean(centred * centred, axis=-1, keepdims=True)
    normed = centred * lax.rsqrt(spread + norm_eps)
    return normed * (1.0 + scale_term[:, None, :]) + shift_term[:, None, :]


gelu_rate = math.sqrt(2.0 / math.pi)
gelu_cubic = 0.044715 * gelu_rate


def gelu_tanh(values):
    raised = jnp.tanh(values * (gelu_rate + gelu_cubic * (values * values)))
    return (0.5 * values) * (1.0 + raised)


def gelu_pull(values, grad):
    square = values * values
    raised = jnp.tanh(values * (gelu_rate + gelu_cubic * square))
    slope = (1.0 - raised) * (values * (gelu_rate + 3.0 * gelu_cubic * square))
    return (0.5 * grad) * ((1.0 + raised) * (1.0 + slope))


def product(left_side, right_side):
    return jnp.dot(left_side, right_side, preferred_element_type=jnp.float32)


def left_product(left_side, right_side):
    return lax.dot_general(
        left_side, right_side, (((0,), (0,)), ((), ())), preferred_element_type=jnp.float32
    )


def right_product(left_side, right_side):
    return lax.dot_general(
        left_side, right_side, (((1,), (1,)), ((), ())), preferred_element_type=jnp.float32
    )


def time_features(steps_in):
    half_count = FREQ // 2
    frequencies = jnp.exp(
        -math.log(10000.0) * jnp.arange(half_count, dtype=jnp.float32) / half_count
    )
    angles = steps_in.astype(jnp.float32)[:, None] * frequencies[None, :]
    return jnp.concatenate([jnp.cos(angles), jnp.sin(angles)], axis=1)


def noise_share(steps_in):
    beta_values = jnp.linspace(0.0001, 0.02, DIFF_STEPS, dtype=jnp.float32)
    log_keep = jnp.log(1.0 - beta_values)
    taken = jnp.arange(DIFF_STEPS, dtype=jnp.int32)[None, :] <= steps_in[:, None]
    return jnp.exp(jnp.sum(jnp.where(taken, log_keep[None, :], 0.0), axis=1))


def bias_parts(biases):
    per_layer = 10 * D + FF
    layer_parts = []
    for layer_index in range(LAYERS):
        anchor = layer_index * per_layer
        layer_parts.append(
            (
                biases[anchor : anchor + D],
                biases[anchor + D : anchor + 2 * D],
                biases[anchor + 2 * D : anchor + 3 * D],
                biases[anchor + 3 * D : anchor + 3 * D + FF],
                biases[anchor + 3 * D + FF : anchor + 4 * D + FF],
                biases[anchor + 4 * D + FF : anchor + per_layer],
            )
        )
    anchor = LAYERS * per_layer
    global_parts = (
        biases[anchor : anchor + 2 * D],
        biases[anchor + 2 * D : anchor + 3 * D],
        biases[anchor + 3 * D : anchor + 4 * D],
        biases[anchor + 4 * D : anchor + 5 * D],
        biases[anchor + 5 * D : anchor + 5 * D + PD],
    )
    return (layer_parts, global_parts)


def hop_plan(count):
    if count == 32:
        return [(8, 4), (2, 2), (4, 2), (1, 2)]
    plan = []
    stride = 1
    while stride < count:
        plan.append((stride, 2))
        stride *= 2
    return plan


def shifted(index, stride, size, amount):
    coord = (index // stride) % size
    return index + ((coord + amount) % size - coord) * stride


def send(value, count, stride, size, amount=1):
    pairs = [(index, shifted(index, stride, size, amount)) for index in range(count)]
    return lax.ppermute(value, "fsdp", pairs)


def gather_near(value, count):
    gathered = value[None]
    for stride, size in hop_plan(count):
        pieces = [gathered]
        for unused in range(size - 1):
            pieces.append(send(pieces[-1], count, stride, size))
        gathered = jnp.concatenate(pieces, axis=0)
    return gathered


def near_places(count):
    me = lax.axis_index("fsdp")
    others = jnp.arange(count, dtype=jnp.int32)
    places = jnp.zeros((count,), jnp.int32)
    weight = 1
    for stride, size in hop_plan(count):
        steps = ((me // stride) % size - (others // stride) % size) % size
        places = places + steps * weight
        weight *= size
    return places


def mesh_dims(count):
    if count == 32:
        return (4, 2, 2, 2)
    return (2,) * (count.bit_length() - 1)


def fold(parts, axis, stride, count):
    size = parts[0].shape[axis]
    mine = (lax.axis_index("fsdp") // stride) % size

    def entry(index):
        picked = [lax.dynamic_index_in_dim(part, index, axis, keepdims=False) for part in parts]
        return picked[0] if len(picked) == 1 else jnp.concatenate(picked, axis=-2)

    arrived = [
        send(entry((mine + step) % size), count, stride, size, step) for step in range(1, size)
    ]
    total = entry(mine).astype(jnp.float32)
    for piece in arrived:
        total = total + piece.astype(jnp.float32)
    return total


class ScatterSum:
    def __init__(self, parts, count, swap):
        dims = mesh_dims(count)
        self.count = count
        self.strides = [1]
        for size in reversed(dims[1:]):
            self.strides.insert(0, self.strides[0] * size)
        self.value = [part.reshape(dims + part.shape[1:]) for part in parts]
        self.axes = list(range(len(dims)))
        self.order = list(reversed(self.axes))
        if swap:
            self.order[1], self.order[2] = self.order[2], self.order[1]

    def step(self):
        if not self.order:
            return
        axis = self.order.pop(0)
        place = self.axes.index(axis)
        total = fold(self.value, place, self.strides[axis], self.count)
        self.axes.remove(axis)
        self.value = [total.astype(jnp.bfloat16) if self.order else total]

    def before(self, values):
        self.value[0], values = lax.optimization_barrier((self.value[0], values))
        return values

    def finish(self):
        while self.order:
            self.step()
        return self.value[0]


def sum_all(value, count):
    stride = 1
    while stride < count:
        value = value + send(value, count, stride, 2)
        stride *= 2
    return value


def pair_scores(queries, keys_all, first_half):
    only = jnp.where(first_half, queries, jnp.zeros_like(queries))
    return only, right_product(only, keys_all) * HD ** (-0.5)


def attention_forward_kernel(queries_ref, keys_ref, values_ref, mixed_ref, total_ref):
    lanes = lax.broadcasted_iota(jnp.int32, (TOK, 2 * HD), 1)
    totals = jnp.zeros((TOK, 2 * HD), jnp.float32)
    for pair in range(HEADS // 2):
        span = slice(pair * 2 * HD, (pair + 1) * 2 * HD)
        queries, keys_all, values_all = queries_ref[:, span], keys_ref[:, span], values_ref[:, span]
        halves = []
        for half in range(2):
            mine = (lanes < HD) if half == 0 else (lanes >= HD)
            unused, scores = pair_scores(queries, keys_all, mine)
            row_max = jnp.max(scores, axis=1, keepdims=True)
            raised = jnp.exp(scores - row_max)
            row_sum = jnp.sum(raised, axis=1, keepdims=True)
            soft_low = (raised / row_sum).astype(jnp.bfloat16)
            halves.append(product(soft_low, values_all))
            totals = jnp.where(lanes == 2 * pair + half, row_max + jnp.log(row_sum), totals)
        mixed_ref[:, span] = jnp.where(lanes < HD, halves[0], halves[1]).astype(jnp.bfloat16)
    total_ref[...] = totals


def attention_backward_kernel(
    queries_ref, keys_ref, values_ref, total_ref, grad_ref, dqueries_ref, dkeys_ref, dvalues_ref
):
    lanes = lax.broadcasted_iota(jnp.int32, (TOK, 2 * HD), 1)
    for pair in range(HEADS // 2):
        span = slice(pair * 2 * HD, (pair + 1) * 2 * HD)
        queries, keys_all, values_all = queries_ref[:, span], keys_ref[:, span], values_ref[:, span]
        grads = grad_ref[:, span]
        made = []
        for half in range(2):
            mine = (lanes < HD) if half == 0 else (lanes >= HD)
            unused, scores = pair_scores(queries, keys_all, mine)
            head = 2 * pair + half
            soft_weights = jnp.exp(scores - total_ref[:, head : head + 1])
            grad_values = left_product(soft_weights.astype(jnp.bfloat16), grads)
            grad_soft = right_product(jnp.where(mine, grads, jnp.zeros_like(grads)), values_all)
            spread = jnp.sum(soft_weights * grad_soft, axis=1, keepdims=True)
            score_low = (soft_weights * (grad_soft - spread)).astype(jnp.bfloat16)
            made.append(
                (
                    product(score_low, keys_all) * HD ** (-0.5),
                    left_product(score_low, queries) * HD ** (-0.5),
                    grad_values,
                )
            )
        for part, target in enumerate((dqueries_ref, dkeys_ref, dvalues_ref)):
            target[:, span] = jnp.where(lanes < HD, made[0][part], made[1][part]).astype(
                jnp.bfloat16
            )


def token_block(width):
    return pl.BlockSpec((TOK, width), lambda sample: (sample, 0))


def attention_forward(packed_low, sample_count):
    row_count = sample_count * TOK
    return pl.pallas_call(
        attention_forward_kernel,
        grid=(sample_count,),
        in_specs=[token_block(D)] * 3,
        out_specs=[token_block(D), token_block(2 * HD)],
        out_shape=[
            jax.ShapeDtypeStruct((row_count, D), jnp.bfloat16),
            jax.ShapeDtypeStruct((row_count, 2 * HD), jnp.float32),
        ],
        name="attention_forward",
    )(*packed_low)


def attention_backward(packed_low, log_total, grad_mixed_low, sample_count):
    row_count = sample_count * TOK
    return pl.pallas_call(
        attention_backward_kernel,
        grid=(sample_count,),
        in_specs=[token_block(D)] * 3 + [token_block(2 * HD), token_block(D)],
        out_specs=[token_block(D)] * 3,
        out_shape=[jax.ShapeDtypeStruct((row_count, D), jnp.bfloat16)] * 3,
        name="attention_backward",
    )(*packed_low, log_total, grad_mixed_low)


def adam_step(weight_now, grad_now, first_old, second_old, factor):
    clipped = grad_now * factor
    first_new = beta_first * first_old + (1.0 - beta_first) * clipped
    second_new = beta_second * second_old + (1.0 - beta_second) * clipped * clipped
    step_size = -learn_rate * (
        first_new / first_fix / (jnp.sqrt(second_new / second_fix) + adam_eps)
        + weight_decay * weight_now
    )
    return (step_size, first_new, second_new)


def body(
    latents,
    noise,
    timesteps,
    labels,
    qkv_weight,
    proj_weight,
    up_weight,
    down_weight,
    mod_weight,
    tables,
    biases,
    qkv_first,
    proj_first,
    up_first,
    down_first,
    mod_first,
    tables_first,
    biases_first,
    qkv_second,
    proj_second,
    up_second,
    down_second,
    mod_second,
    tables_second,
    biases_second,
):
    count = lax.axis_size("fsdp")
    me = lax.axis_index("fsdp")
    local = latents.shape[0]
    samples = local * count
    rows = D // count
    row_count = local * TOK
    total_count = samples * TOK * PD
    low = jnp.bfloat16
    f32 = jnp.float32
    layer_parts, global_parts = bias_parts(biases)
    final_bias, patch_bias, first_bias, second_bias, head_bias = global_parts
    mod_bias = jnp.concatenate([part_item[5] for part_item in layer_parts] + [final_bias])

    gathered = []
    for layer_index in range(LAYERS):
        pieces = [qkv_weight[layer_index][:, part * D : (part + 1) * D] for part in range(3)]
        pieces.append(proj_weight[layer_index])
        pieces += [up_weight[layer_index][:, part * D : (part + 1) * D] for part in range(4)]
        pieces.append(down_weight[layer_index])
        packed = jnp.concatenate(pieces, axis=0).astype(low).reshape(12, rows, D)
        gathered.append(lax.all_gather(packed, "fsdp", axis=1, tiled=True))

    mod_low = mod_weight.astype(low)
    mod_columns = lax.all_to_all(mod_low, "fsdp", split_axis=1, concat_axis=0, tiled=True)
    digits = jnp.concatenate([timesteps // 32, timesteps % 32, labels // 32, labels % 32]).astype(low)
    table_low = tables.astype(low).T
    room = -(-CLASSES // 128) * 128
    first_at, class_at, patch_at = D, D + FREQ, D + FREQ + room
    head_at, digit_at = patch_at + PD, patch_at + 2 * PD
    tables_low = jnp.concatenate(
        [
            table_low[:, PD + FREQ : PD + FREQ + D],
            table_low[:, PD : PD + FREQ],
            table_low[:, PD + FREQ + D : PD + FREQ + D + CLASSES],
            jnp.zeros((rows, room - CLASSES), low),
            table_low[:, :PD],
            table_low[:, PD + FREQ + D + CLASSES :],
            jnp.broadcast_to(digits[None, :], (rows, 4 * local)),
        ],
        axis=1,
    )
    tables_near = gather_near(tables_low, count)
    places = near_places(count)
    tables_far = jnp.take(tables_near, places, axis=0, mode="clip")
    tables_full = tables_far.reshape(D, digit_at + 4 * local)

    numbers = tables_far[:, 0, digit_at:].astype(jnp.int32).reshape(count, 4, local)
    steps_all = (numbers[:, 0] * 32 + numbers[:, 1]).reshape(samples)
    labels_all = (numbers[:, 2] * 32 + numbers[:, 3]).reshape(samples)
    features_low = time_features(steps_all).astype(low)
    first_pre = right_product(features_low, tables_full[:, first_at:class_at]) + first_bias
    first_low = jax.nn.silu(first_pre).astype(low)
    class_rows = (labels_all[:, None] == jnp.arange(room, dtype=jnp.int32)[None, :]).astype(low)
    condition = (
        right_product(first_low, tables_full[:, :D])
        + second_bias
        + right_product(class_rows, tables_full[:, class_at:patch_at])
    )
    cond_low = jax.nn.silu(condition).astype(low)
    mods_columns = product(cond_low, mod_columns)
    modulations = (
        lax.all_to_all(mods_columns, "fsdp", split_axis=0, concat_axis=1, tiled=True) + mod_bias
    )

    keep_share = noise_share(timesteps)
    noised = (
        jnp.sqrt(keep_share)[:, None, None] * latents
        + jnp.sqrt(1.0 - keep_share)[:, None, None] * noise
    )
    noised_low = noised.reshape(row_count, PD).astype(low)
    patch_columns = tables_full[:, patch_at:head_at]
    head_columns = tables_full[:, head_at:digit_at]
    residual = (right_product(noised_low, patch_columns) + patch_bias).reshape(local, TOK, D)

    def weights_of(layer_index):
        whole = gathered[layer_index]
        square = [whole[part] for part in range(8)]
        up_full = jnp.concatenate(square[4:], axis=1)
        down_full = whole[8:].reshape(4, count, rows, D).transpose(1, 0, 2, 3).reshape(FF, D)
        return square[:3], square[3], up_full, down_full

    stored = []
    for layer_index in range(LAYERS):
        gathered[layer_index], residual = lax.optimization_barrier(
            (gathered[layer_index], residual)
        )
        qkv_full, proj_full, up_full, down_full = weights_of(layer_index)
        query_bias, value_bias, proj_bias, up_bias, down_bias, unused = layer_parts[layer_index]
        segment = modulations[:, layer_index * 6 * D : (layer_index + 1) * 6 * D]
        mod_terms = [segment[:, part_index * D : (part_index + 1) * D] for part_index in range(6)]
        shift_attn, scale_attn, gate_attn, shift_mlp, scale_mlp, gate_mlp = mod_terms
        residual_in = residual
        hidden_low = modulate(residual_in, shift_attn, scale_attn).reshape(row_count, D).astype(low)
        packed_low = [
            (product(hidden_low, qkv_full[0]) + query_bias).astype(low),
            product(hidden_low, qkv_full[1]).astype(low),
            (product(hidden_low, qkv_full[2]) + value_bias).astype(low),
        ]
        mixed, log_total = attention_forward(packed_low, local)
        mixed_low = mixed.astype(low)
        attn_out = (product(mixed_low, proj_full) + proj_bias).reshape(local, TOK, D)
        residual_mid = residual_in + gate_attn[:, None, :] * attn_out
        hidden_two_low = modulate(residual_mid, shift_mlp, scale_mlp).reshape(row_count, D).astype(low)
        pre_act = product(hidden_two_low, up_full) + up_bias
        act_low = lax.optimization_barrier(gelu_tanh(pre_act).astype(low))
        mlp_out = (product(act_low, down_full) + down_bias).reshape(local, TOK, D)
        residual = residual_mid + gate_mlp[:, None, :] * mlp_out
        stored.append(
            (
                residual_in,
                hidden_low,
                packed_low,
                log_total,
                mixed_low,
                attn_out,
                residual_mid,
                hidden_two_low,
                pre_act,
                act_low,
                mlp_out,
            )
        )
    final_mods = modulations[:, LAYERS * 6 * D :]
    final_hidden = modulate(residual, final_mods[:, :D], final_mods[:, D:])
    final_low = final_hidden.reshape(row_count, D).astype(low)
    predicted = product(final_low, head_columns) + head_bias
    errors = predicted - noise.reshape(row_count, PD)
    loss_local = jnp.sum(errors * errors) / total_count
    grad_pred_low = (2.0 * errors / total_count).astype(low)
    grad_head_bias = jnp.sum(grad_pred_low.astype(f32), axis=0)
    grad_head = left_product(grad_pred_low, final_low)
    grad_final = right_product(grad_pred_low, head_columns).reshape(local, TOK, D)
    unused, final_pull = jax.vjp(modulate, residual, final_mods[:, :D], final_mods[:, D:])
    grad_residual, grad_shift_final, grad_scale_final = final_pull(grad_final)
    mod_grads = [None] * LAYERS
    shards = [None] * LAYERS
    bias_pieces = [None] * LAYERS
    for layer_index in reversed(range(LAYERS)):
        qkv_full, proj_full, up_full, down_full = weights_of(layer_index)
        (
            residual_in,
            hidden_low,
            packed_low,
            log_total,
            mixed_low,
            attn_out,
            residual_mid,
            hidden_two_low,
            pre_act,
            act_low,
            mlp_out,
        ) = stored[layer_index]
        segment = modulations[:, layer_index * 6 * D : (layer_index + 1) * 6 * D]
        mod_terms = [segment[:, part_index * D : (part_index + 1) * D] for part_index in range(6)]
        shift_attn, scale_attn, gate_attn, shift_mlp, scale_mlp, gate_mlp = mod_terms
        grad_gate_mlp = jnp.sum(grad_residual * mlp_out, axis=1)
        grad_mlp_low = (grad_residual * gate_mlp[:, None, :]).reshape(row_count, D).astype(low)
        grad_down_bias = jnp.sum(grad_mlp_low.astype(f32), axis=0)
        grad_down = left_product(act_low, grad_mlp_low)
        grad_act = right_product(grad_mlp_low, down_full)
        grad_pre_low = gelu_pull(pre_act, grad_act).astype(low)
        grad_up_bias = jnp.sum(grad_pre_low.astype(f32), axis=0)
        grad_up = left_product(hidden_two_low, grad_pre_low)
        grad_hidden_two = right_product(grad_pre_low, up_full).reshape(local, TOK, D)
        unused, mlp_pull = jax.vjp(modulate, residual_mid, shift_mlp, scale_mlp)
        part_residual, grad_shift_mlp, grad_scale_mlp = mlp_pull(grad_hidden_two)
        grad_residual = grad_residual + part_residual
        grad_gate_attn = jnp.sum(grad_residual * attn_out, axis=1)
        grad_attn_low = (grad_residual * gate_attn[:, None, :]).reshape(row_count, D).astype(low)
        grad_proj_bias = jnp.sum(grad_attn_low.astype(f32), axis=0)
        grad_proj = left_product(mixed_low, grad_attn_low)
        grad_mixed_low = right_product(grad_attn_low, proj_full).astype(low)
        sent_mlp = [
            grad_up[:, part * D : (part + 1) * D].astype(low).reshape(count, rows, D)
            for part in range(4)
        ]
        sent_mlp.append(grad_down.astype(low).reshape(count, 4 * rows, D))
        if layer_index == 0:
            sent_mlp, grad_mixed_low = lax.optimization_barrier((sent_mlp, grad_mixed_low))
            mlp_sum = ScatterSum(sent_mlp, count, False)
            mlp_sum.step()
        grad_packed_low = attention_backward(packed_low, log_total, grad_mixed_low, local)
        if layer_index == 0:
            grad_packed_low = mlp_sum.before(grad_packed_low)
            mlp_sum.step()
        grad_query_bias = jnp.sum(grad_packed_low[0].astype(f32), axis=0)
        grad_value_bias = jnp.sum(grad_packed_low[2].astype(f32), axis=0)
        grad_qkv = [left_product(hidden_low, item) for item in grad_packed_low]
        grad_hidden = (
            right_product(grad_packed_low[0], qkv_full[0])
            + right_product(grad_packed_low[1], qkv_full[1])
            + right_product(grad_packed_low[2], qkv_full[2])
        ).reshape(local, TOK, D)
        unused, attn_pull = jax.vjp(modulate, residual_in, shift_attn, scale_attn)
        part_residual, grad_shift_attn, grad_scale_attn = attn_pull(grad_hidden)
        grad_residual = grad_residual + part_residual
        mod_grads[layer_index] = jnp.concatenate(
            [
                grad_shift_attn,
                grad_scale_attn,
                grad_gate_attn,
                grad_shift_mlp,
                grad_scale_mlp,
                grad_gate_mlp,
            ],
            axis=1,
        )
        sent = [item.astype(low).reshape(count, rows, D) for item in grad_qkv + [grad_proj]]
        if layer_index > 0:
            sent = jnp.concatenate(sent + sent_mlp, axis=1).reshape(count * 12 * rows, D)
            sent, grad_residual = lax.optimization_barrier((sent, grad_residual))
            shard = lax.psum_scatter(sent, "fsdp", scatter_dimension=0, tiled=True).astype(f32)
        else:
            attn_sum = ScatterSum(sent, count, True)
            attn_sum.step()
            mod_grads[0] = mlp_sum.before(mod_grads[0])
            mlp_sum.step()
            mod_grads[0] = attn_sum.before(mod_grads[0])
            attn_sum.step()
            shard = None
        shards[layer_index] = shard
        bias_pieces[layer_index] = [
            grad_query_bias,
            grad_value_bias,
            grad_proj_bias,
            grad_up_bias,
            grad_down_bias,
        ]
    grad_zero_low = grad_residual.reshape(row_count, D).astype(low)
    grad_patch_bias = jnp.sum(grad_zero_low.astype(f32), axis=0)
    grad_patch = left_product(noised_low, grad_zero_low)

    grad_mods_low = jnp.concatenate(mod_grads + [grad_shift_final, grad_scale_final], axis=1)
    grad_mods_columns = lax.all_to_all(
        grad_mods_low.astype(low), "fsdp", split_axis=1, concat_axis=0, tiled=True
    )
    grad_act = lax.all_to_all(
        right_product(mod_columns, grad_mods_columns), "fsdp", split_axis=0, concat_axis=0, tiled=True
    )
    grad_act = jnp.sum(grad_act.reshape(count, rows, samples), axis=0)
    grad_act = mlp_sum.before(grad_act)
    mlp_sum.step()
    grad_act = attn_sum.before(grad_act)
    attn_sum.step()
    shard_mod = lax.all_to_all(
        left_product(cond_low, grad_mods_columns).astype(low),
        "fsdp",
        split_axis=0,
        concat_axis=1,
        tiled=True,
    ).astype(f32)
    own_bias = lax.dynamic_slice(second_bias, (me * rows,), (rows,))
    condition_own = (
        right_product(tables_low[:, :D], first_low)
        + own_bias[:, None]
        + right_product(tables_low[:, class_at:patch_at], class_rows)
    )
    unused, silu_pull = jax.vjp(jax.nn.silu, condition_own)
    grad_condition = silu_pull(grad_act)[0]
    grad_class = lax.dot_general(
        grad_condition,
        class_rows.astype(f32),
        (((1,), (0,)), ((), ())),
        precision=lax.Precision.HIGHEST,
        preferred_element_type=f32,
    )[:, :CLASSES]
    grad_time_low = grad_condition.astype(low)
    grad_second_bias = jnp.sum(grad_time_low.astype(f32), axis=1)
    grad_second = product(grad_time_low, first_low)
    grad_time_all = lax.all_to_all(
        jnp.broadcast_to(grad_time_low[None], (count, rows, samples)).reshape(D, samples),
        "fsdp",
        split_axis=0,
        concat_axis=0,
        tiled=True,
    )
    grad_first_act = lax.dynamic_slice(
        left_product(tables_full[:, :D], grad_time_all), (me * rows, 0), (rows, samples)
    )
    own_bias = lax.dynamic_slice(first_bias, (me * rows,), (rows,))
    first_pre_own = right_product(tables_low[:, first_at:class_at], features_low) + own_bias[:, None]
    unused, first_pull = jax.vjp(jax.nn.silu, first_pre_own)
    grad_first_low = first_pull(grad_first_act)[0].astype(low)
    grad_first_bias = jnp.sum(grad_first_low.astype(f32), axis=1)
    grad_first = product(grad_first_low, features_low)
    grad_middle = jnp.concatenate([grad_first, grad_second, grad_class], axis=1).T

    def spread(piece, length):
        return lax.dynamic_update_slice(jnp.zeros((length,), f32), piece, (me * piece.shape[0],))

    own_mod_bias = spread(jnp.sum(grad_mods_columns.astype(f32), axis=0), MODW)
    pieces = []
    for layer_index in range(LAYERS):
        pieces += bias_pieces[layer_index]
        pieces.append(own_mod_bias[layer_index * 6 * D : (layer_index + 1) * 6 * D])
    pieces += [
        own_mod_bias[LAYERS * 6 * D :],
        grad_patch_bias,
        spread(grad_first_bias, D),
        spread(grad_second_bias, D),
        grad_head_bias,
    ]
    pieces += [grad_patch.reshape(-1), grad_head.reshape(-1)]
    summed = sum_all(jnp.concatenate(pieces), count)
    bias_length = biases.shape[0]
    bias_grad = summed[:bias_length]
    ends = summed[bias_length:].reshape(2 * PD, D)
    own_ends = lax.dynamic_slice(ends, (0, me * rows), (2 * PD, rows))
    shard_tables = jnp.concatenate([own_ends[:PD], grad_middle, own_ends[PD:]], axis=0)
    shards[0] = jnp.concatenate([attn_sum.finish(), mlp_sum.finish()], axis=0)
    for layer_index in range(LAYERS):
        shard = shards[layer_index]
        parts = [shard[part * rows : (part + 1) * rows] for part in range(8)]
        shards[layer_index] = (
            jnp.concatenate(parts[:3], axis=1),
            parts[3],
            jnp.concatenate(parts[4:], axis=1),
            shard[8 * rows :],
        )
    shard_squares = jnp.sum(shard_mod * shard_mod) + jnp.sum(shard_tables * shard_tables)
    for layer_index in range(LAYERS):
        for item in shards[layer_index]:
            shard_squares = shard_squares + jnp.sum(item * item)
    square_total, loss_value = sum_all(jnp.stack([shard_squares, loss_local]), count)
    grad_norm = jnp.sqrt(square_total + jnp.sum(bias_grad * bias_grad))
    factor = jnp.minimum(1.0, clip_limit / (grad_norm + 1e-06))
    shard_qkv, shard_proj, shard_up, shard_down = [
        jnp.stack([shards[layer_index][part] for layer_index in range(LAYERS)]) for part in range(4)
    ]
    qkv_update, qkv_first_new, qkv_second_new = adam_step(
        qkv_weight, shard_qkv, qkv_first, qkv_second, factor
    )
    proj_update, proj_first_new, proj_second_new = adam_step(
        proj_weight, shard_proj, proj_first, proj_second, factor
    )
    up_update, up_first_new, up_second_new = adam_step(
        up_weight, shard_up, up_first, up_second, factor
    )
    down_update, down_first_new, down_second_new = adam_step(
        down_weight, shard_down, down_first, down_second, factor
    )
    mod_update, mod_first_new, mod_second_new = adam_step(
        mod_weight, shard_mod, mod_first, mod_second, factor
    )
    tables_update, tables_first_new, tables_second_new = adam_step(
        tables, shard_tables, tables_first, tables_second, factor
    )
    biases_update, biases_first_new, biases_second_new = adam_step(
        biases, bias_grad, biases_first, biases_second, factor
    )
    return (
        loss_value,
        grad_norm,
        qkv_update,
        qkv_first_new,
        qkv_second_new,
        proj_update,
        proj_first_new,
        proj_second_new,
        up_update,
        up_first_new,
        up_second_new,
        down_update,
        down_first_new,
        down_second_new,
        mod_update,
        mod_first_new,
        mod_second_new,
        tables_update,
        tables_first_new,
        tables_second_new,
        biases_update,
        biases_first_new,
        biases_second_new,
    )


def solution(mesh):
    in_specs = (
        P("fsdp", None, None),
        P("fsdp", None, None),
        P("fsdp"),
        P("fsdp"),
        P(None, "fsdp", None),
        P(None, "fsdp", None),
        P(None, "fsdp", None),
        P(None, "fsdp", None),
        P("fsdp", None),
        P(None, "fsdp"),
        P(),
        P(None, "fsdp", None),
        P(None, "fsdp", None),
        P(None, "fsdp", None),
        P(None, "fsdp", None),
        P("fsdp", None),
        P(None, "fsdp"),
        P(),
        P(None, "fsdp", None),
        P(None, "fsdp", None),
        P(None, "fsdp", None),
        P(None, "fsdp", None),
        P("fsdp", None),
        P(None, "fsdp"),
        P(),
    )
    out_specs = (
        P(),
        P(),
        P(None, "fsdp", None),
        P(None, "fsdp", None),
        P(None, "fsdp", None),
        P(None, "fsdp", None),
        P(None, "fsdp", None),
        P(None, "fsdp", None),
        P(None, "fsdp", None),
        P(None, "fsdp", None),
        P(None, "fsdp", None),
        P(None, "fsdp", None),
        P(None, "fsdp", None),
        P(None, "fsdp", None),
        P("fsdp", None),
        P("fsdp", None),
        P("fsdp", None),
        P(None, "fsdp"),
        P(None, "fsdp"),
        P(None, "fsdp"),
        P(),
        P(),
        P(),
    )
    return jax.shard_map(body, mesh=mesh, in_specs=in_specs, out_specs=out_specs, check_vma=False)
```

```python
import math

import jax
import jax.numpy as jnp
from jax import lax
from jax.experimental import pallas as pl
from jax.sharding import PartitionSpec as P

D = 768
HEADS = 12
HD = 64
FF = 3072
FREQ = 256
CLASSES = 1000
DIFF_STEPS = 1000
LAYERS = 2
TOK = 256
PD = 16
MODW = 10752


norm_eps = 1e-06
clip_limit = 2.5
learn_rate = 0.01
beta_first = 0.9
beta_second = 0.95
adam_eps = 1e-08
weight_decay = 0.01
first_fix = 1.0 - 0.9**10
second_fix = 1.0 - 0.95**10


def modulate(residual, shift_term, scale_term):
    centred = residual - jnp.mean(residual, axis=-1, keepdims=True)
    spread = jnp.mean(centred * centred, axis=-1, keepdims=True)
    normed = centred * lax.rsqrt(spread + norm_eps)
    return normed * (1.0 + scale_term[:, None, :]) + shift_term[:, None, :]


gelu_rate = math.sqrt(2.0 / math.pi)
gelu_cubic = 0.044715 * gelu_rate


def gelu_tanh(values):
    raised = jnp.tanh(values * (gelu_rate + gelu_cubic * (values * values)))
    return (0.5 * values) * (1.0 + raised)


def gelu_pull(values, grad):
    square = values * values
    raised = jnp.tanh(values * (gelu_rate + gelu_cubic * square))
    slope = (1.0 - raised) * (values * (gelu_rate + 3.0 * gelu_cubic * square))
    return (0.5 * grad) * ((1.0 + raised) * (1.0 + slope))


def product(left_side, right_side):
    return jnp.dot(left_side, right_side, preferred_element_type=jnp.float32)


def left_product(left_side, right_side):
    return lax.dot_general(
        left_side, right_side, (((0,), (0,)), ((), ())), preferred_element_type=jnp.float32
    )


def right_product(left_side, right_side):
    return lax.dot_general(
        left_side, right_side, (((1,), (1,)), ((), ())), preferred_element_type=jnp.float32
    )


def time_features(steps_in):
    half_count = FREQ // 2
    frequencies = jnp.exp(
        -math.log(10000.0) * jnp.arange(half_count, dtype=jnp.float32) / half_count
    )
    angles = steps_in.astype(jnp.float32)[:, None] * frequencies[None, :]
    return jnp.concatenate([jnp.cos(angles), jnp.sin(angles)], axis=1)


def noise_share(steps_in):
    beta_values = jnp.linspace(0.0001, 0.02, DIFF_STEPS, dtype=jnp.float32)
    log_keep = jnp.log(1.0 - beta_values)
    taken = jnp.arange(DIFF_STEPS, dtype=jnp.int32)[None, :] <= steps_in[:, None]
    return jnp.exp(jnp.sum(jnp.where(taken, log_keep[None, :], 0.0), axis=1))


def bias_parts(biases):
    per_layer = 10 * D + FF
    layer_parts = []
    for layer_index in range(LAYERS):
        anchor = layer_index * per_layer
        layer_parts.append(
            (
                biases[anchor : anchor + D],
                biases[anchor + D : anchor + 2 * D],
                biases[anchor + 2 * D : anchor + 3 * D],
                biases[anchor + 3 * D : anchor + 3 * D + FF],
                biases[anchor + 3 * D + FF : anchor + 4 * D + FF],
                biases[anchor + 4 * D + FF : anchor + per_layer],
            )
        )
    anchor = LAYERS * per_layer
    global_parts = (
        biases[anchor : anchor + 2 * D],
        biases[anchor + 2 * D : anchor + 3 * D],
        biases[anchor + 3 * D : anchor + 4 * D],
        biases[anchor + 4 * D : anchor + 5 * D],
        biases[anchor + 5 * D : anchor + 5 * D + PD],
    )
    return (layer_parts, global_parts)


def hop_plan(count):
    if count == 32:
        return [(8, 4), (2, 2), (4, 2), (1, 2)]
    plan = []
    stride = 1
    while stride < count:
        plan.append((stride, 2))
        stride *= 2
    return plan


def shifted(index, stride, size, amount):
    coord = (index // stride) % size
    return index + ((coord + amount) % size - coord) * stride


def send(value, count, stride, size, amount=1):
    pairs = [(index, shifted(index, stride, size, amount)) for index in range(count)]
    return lax.ppermute(value, "fsdp", pairs)


def gather_near(value, count):
    gathered = value[None]
    for stride, size in hop_plan(count):
        pieces = [gathered]
        for unused in range(size - 1):
            pieces.append(send(pieces[-1], count, stride, size))
        gathered = jnp.concatenate(pieces, axis=0)
    return gathered


def near_places(count):
    me = lax.axis_index("fsdp")
    others = jnp.arange(count, dtype=jnp.int32)
    places = jnp.zeros((count,), jnp.int32)
    weight = 1
    for stride, size in hop_plan(count):
        steps = ((me // stride) % size - (others // stride) % size) % size
        places = places + steps * weight
        weight *= size
    return places


def mesh_dims(count):
    if count == 32:
        return (4, 2, 2, 2)
    return (2,) * (count.bit_length() - 1)


def fold(parts, axis, stride, count):
    size = parts[0].shape[axis]
    mine = (lax.axis_index("fsdp") // stride) % size

    def entry(index):
        picked = [lax.dynamic_index_in_dim(part, index, axis, keepdims=False) for part in parts]
        return picked[0] if len(picked) == 1 else jnp.concatenate(picked, axis=-2)

    arrived = [
        send(entry((mine + step) % size), count, stride, size, step) for step in range(1, size)
    ]
    total = entry(mine).astype(jnp.float32)
    for piece in arrived:
        total = total + piece.astype(jnp.float32)
    return total


class ScatterSum:
    def __init__(self, parts, count, swap):
        dims = mesh_dims(count)
        self.count = count
        self.strides = [1]
        for size in reversed(dims[1:]):
            self.strides.insert(0, self.strides[0] * size)
        self.value = [part.reshape(dims + part.shape[1:]) for part in parts]
        self.axes = list(range(len(dims)))
        self.order = list(reversed(self.axes))
        if swap:
            self.order[1], self.order[2] = self.order[2], self.order[1]

    def step(self):
        if not self.order:
            return
        axis = self.order.pop(0)
        place = self.axes.index(axis)
        total = fold(self.value, place, self.strides[axis], self.count)
        self.axes.remove(axis)
        self.value = [total.astype(jnp.bfloat16) if self.order else total]

    def before(self, values):
        self.value[0], values = lax.optimization_barrier((self.value[0], values))
        return values

    def finish(self):
        while self.order:
            self.step()
        return self.value[0]


def sum_all(value, count):
    stride = 1
    while stride < count:
        value = value + send(value, count, stride, 2)
        stride *= 2
    return value


def pair_scores(queries, keys_all, first_half):
    only = jnp.where(first_half, queries, jnp.zeros_like(queries))
    return only, right_product(only, keys_all) * HD ** (-0.5)


def attention_forward_kernel(queries_ref, keys_ref, values_ref, mixed_ref, total_ref):
    lanes = lax.broadcasted_iota(jnp.int32, (TOK, 2 * HD), 1)
    totals = jnp.zeros((TOK, 2 * HD), jnp.float32)
    for pair in range(HEADS // 2):
        span = slice(pair * 2 * HD, (pair + 1) * 2 * HD)
        queries, keys_all, values_all = queries_ref[:, span], keys_ref[:, span], values_ref[:, span]
        halves = []
        for half in range(2):
            mine = (lanes < HD) if half == 0 else (lanes >= HD)
            unused, scores = pair_scores(queries, keys_all, mine)
            row_max = jnp.max(scores, axis=1, keepdims=True)
            raised = jnp.exp(scores - row_max)
            row_sum = jnp.sum(raised, axis=1, keepdims=True)
            soft_low = (raised / row_sum).astype(jnp.bfloat16)
            halves.append(product(soft_low, values_all))
            totals = jnp.where(lanes == 2 * pair + half, row_max + jnp.log(row_sum), totals)
        mixed_ref[:, span] = jnp.where(lanes < HD, halves[0], halves[1]).astype(jnp.bfloat16)
    total_ref[...] = totals


def attention_backward_kernel(
    queries_ref, keys_ref, values_ref, total_ref, grad_ref, dqueries_ref, dkeys_ref, dvalues_ref
):
    lanes = lax.broadcasted_iota(jnp.int32, (TOK, 2 * HD), 1)
    for pair in range(HEADS // 2):
        span = slice(pair * 2 * HD, (pair + 1) * 2 * HD)
        queries, keys_all, values_all = queries_ref[:, span], keys_ref[:, span], values_ref[:, span]
        grads = grad_ref[:, span]
        made = []
        for half in range(2):
            mine = (lanes < HD) if half == 0 else (lanes >= HD)
            unused, scores = pair_scores(queries, keys_all, mine)
            head = 2 * pair + half
            soft_weights = jnp.exp(scores - total_ref[:, head : head + 1])
            grad_values = left_product(soft_weights.astype(jnp.bfloat16), grads)
            grad_soft = right_product(jnp.where(mine, grads, jnp.zeros_like(grads)), values_all)
            spread = jnp.sum(soft_weights * grad_soft, axis=1, keepdims=True)
            score_low = (soft_weights * (grad_soft - spread)).astype(jnp.bfloat16)
            made.append(
                (
                    product(score_low, keys_all) * HD ** (-0.5),
                    left_product(score_low, queries) * HD ** (-0.5),
                    grad_values,
                )
            )
        for part, target in enumerate((dqueries_ref, dkeys_ref, dvalues_ref)):
            target[:, span] = jnp.where(lanes < HD, made[0][part], made[1][part]).astype(
                jnp.bfloat16
            )


def token_block(width):
    return pl.BlockSpec((TOK, width), lambda sample: (sample, 0))


def attention_forward(packed_low, sample_count):
    row_count = sample_count * TOK
    return pl.pallas_call(
        attention_forward_kernel,
        grid=(sample_count,),
        in_specs=[token_block(D)] * 3,
        out_specs=[token_block(D), token_block(2 * HD)],
        out_shape=[
            jax.ShapeDtypeStruct((row_count, D), jnp.bfloat16),
            jax.ShapeDtypeStruct((row_count, 2 * HD), jnp.float32),
        ],
        name="attention_forward",
    )(*packed_low)


def attention_backward(packed_low, log_total, grad_mixed_low, sample_count):
    row_count = sample_count * TOK
    return pl.pallas_call(
        attention_backward_kernel,
        grid=(sample_count,),
        in_specs=[token_block(D)] * 3 + [token_block(2 * HD), token_block(D)],
        out_specs=[token_block(D)] * 3,
        out_shape=[jax.ShapeDtypeStruct((row_count, D), jnp.bfloat16)] * 3,
        name="attention_backward",
    )(*packed_low, log_total, grad_mixed_low)


def adam_step(weight_now, grad_now, first_old, second_old, factor):
    clipped = grad_now * factor
    first_new = beta_first * first_old + (1.0 - beta_first) * clipped
    second_new = beta_second * second_old + (1.0 - beta_second) * clipped * clipped
    step_size = -learn_rate * (
        first_new / first_fix / (jnp.sqrt(second_new / second_fix) + adam_eps)
        + weight_decay * weight_now
    )
    return (step_size, first_new, second_new)


def body(
    latents,
    noise,
    timesteps,
    labels,
    qkv_weight,
    proj_weight,
    up_weight,
    down_weight,
    mod_weight,
    tables,
    biases,
    qkv_first,
    proj_first,
    up_first,
    down_first,
    mod_first,
    tables_first,
    biases_first,
    qkv_second,
    proj_second,
    up_second,
    down_second,
    mod_second,
    tables_second,
    biases_second,
):
    count = lax.axis_size("fsdp")
    me = lax.axis_index("fsdp")
    local = latents.shape[0]
    samples = local * count
    rows = D // count
    row_count = local * TOK
    total_count = samples * TOK * PD
    low = jnp.bfloat16
    f32 = jnp.float32
    layer_parts, global_parts = bias_parts(biases)
    final_bias, patch_bias, first_bias, second_bias, head_bias = global_parts
    mod_bias = jnp.concatenate([part_item[5] for part_item in layer_parts] + [final_bias])

    gathered = []
    for layer_index in range(LAYERS):
        pieces = [qkv_weight[layer_index][:, part * D : (part + 1) * D] for part in range(3)]
        pieces.append(proj_weight[layer_index])
        pieces += [up_weight[layer_index][:, part * D : (part + 1) * D] for part in range(4)]
        pieces.append(down_weight[layer_index])
        packed = jnp.concatenate(pieces, axis=0).astype(low).reshape(12, rows, D)
        gathered.append(lax.all_gather(packed, "fsdp", axis=1, tiled=True))

    mod_low = mod_weight.astype(low)
    mod_columns = lax.all_to_all(mod_low, "fsdp", split_axis=1, concat_axis=0, tiled=True)
    digits = jnp.concatenate([timesteps // 32, timesteps % 32, labels // 32, labels % 32]).astype(low)
    table_low = tables.astype(low).T
    room = -(-CLASSES // 128) * 128
    first_at, class_at, patch_at = D, D + FREQ, D + FREQ + room
    head_at, digit_at = patch_at + PD, patch_at + 2 * PD
    tables_low = jnp.concatenate(
        [
            table_low[:, PD + FREQ : PD + FREQ + D],
            table_low[:, PD : PD + FREQ],
            table_low[:, PD + FREQ + D : PD + FREQ + D + CLASSES],
            jnp.zeros((rows, room - CLASSES), low),
            table_low[:, :PD],
            table_low[:, PD + FREQ + D + CLASSES :],
            jnp.broadcast_to(digits[None, :], (rows, 4 * local)),
        ],
        axis=1,
    )
    tables_near = gather_near(tables_low, count)
    places = near_places(count)
    tables_far = jnp.take(tables_near, places, axis=0, mode="clip")
    tables_full = tables_far.reshape(D, digit_at + 4 * local)

    numbers = tables_far[:, 0, digit_at:].astype(jnp.int32).reshape(count, 4, local)
    steps_all = (numbers[:, 0] * 32 + numbers[:, 1]).reshape(samples)
    labels_all = (numbers[:, 2] * 32 + numbers[:, 3]).reshape(samples)
    features_low = time_features(steps_all).astype(low)
    first_pre = right_product(features_low, tables_full[:, first_at:class_at]) + first_bias
    first_low = jax.nn.silu(first_pre).astype(low)
    class_rows = (labels_all[:, None] == jnp.arange(room, dtype=jnp.int32)[None, :]).astype(low)
    condition = (
        right_product(first_low, tables_full[:, :D])
        + second_bias
        + right_product(class_rows, tables_full[:, class_at:patch_at])
    )
    cond_low = jax.nn.silu(condition).astype(low)
    mods_columns = product(cond_low, mod_columns)
    modulations = (
        lax.all_to_all(mods_columns, "fsdp", split_axis=0, concat_axis=1, tiled=True) + mod_bias
    )

    keep_share = noise_share(timesteps)
    noised = (
        jnp.sqrt(keep_share)[:, None, None] * latents
        + jnp.sqrt(1.0 - keep_share)[:, None, None] * noise
    )
    noised_low = noised.reshape(row_count, PD).astype(low)
    patch_columns = tables_full[:, patch_at:head_at]
    head_columns = tables_full[:, head_at:digit_at]
    residual = (right_product(noised_low, patch_columns) + patch_bias).reshape(local, TOK, D)

    def weights_of(layer_index):
        whole = gathered[layer_index]
        square = [whole[part] for part in range(8)]
        up_full = jnp.concatenate(square[4:], axis=1)
        down_full = whole[8:].reshape(4, count, rows, D).transpose(1, 0, 2, 3).reshape(FF, D)
        return square[:3], square[3], up_full, down_full

    stored = []
    for layer_index in range(LAYERS):
        gathered[layer_index], residual = lax.optimization_barrier(
            (gathered[layer_index], residual)
        )
        qkv_full, proj_full, up_full, down_full = weights_of(layer_index)
        query_bias, value_bias, proj_bias, up_bias, down_bias, unused = layer_parts[layer_index]
        segment = modulations[:, layer_index * 6 * D : (layer_index + 1) * 6 * D]
        mod_terms = [segment[:, part_index * D : (part_index + 1) * D] for part_index in range(6)]
        shift_attn, scale_attn, gate_attn, shift_mlp, scale_mlp, gate_mlp = mod_terms
        residual_in = residual
        hidden_low = modulate(residual_in, shift_attn, scale_attn).reshape(row_count, D).astype(low)
        packed_low = [
            (product(hidden_low, qkv_full[0]) + query_bias).astype(low),
            product(hidden_low, qkv_full[1]).astype(low),
            (product(hidden_low, qkv_full[2]) + value_bias).astype(low),
        ]
        mixed, log_total = attention_forward(packed_low, local)
        mixed_low = mixed.astype(low)
        attn_out = (product(mixed_low, proj_full) + proj_bias).reshape(local, TOK, D)
        residual_mid = residual_in + gate_attn[:, None, :] * attn_out
        hidden_two_low = modulate(residual_mid, shift_mlp, scale_mlp).reshape(row_count, D).astype(low)
        pre_act = product(hidden_two_low, up_full) + up_bias
        act_low = lax.optimization_barrier(gelu_tanh(pre_act).astype(low))
        mlp_out = (product(act_low, down_full) + down_bias).reshape(local, TOK, D)
        residual = residual_mid + gate_mlp[:, None, :] * mlp_out
        stored.append(
            (
                residual_in,
                hidden_low,
                packed_low,
                log_total,
                mixed_low,
                attn_out,
                residual_mid,
                hidden_two_low,
                pre_act,
                act_low,
                mlp_out,
            )
        )
    final_mods = modulations[:, LAYERS * 6 * D :]
    final_hidden = modulate(residual, final_mods[:, :D], final_mods[:, D:])
    final_low = final_hidden.reshape(row_count, D).astype(low)
    predicted = product(final_low, head_columns) + head_bias
    errors = predicted - noise.reshape(row_count, PD)
    loss_local = jnp.sum(errors * errors) / total_count
    grad_pred_low = (2.0 * errors / total_count).astype(low)
    grad_head_bias = jnp.sum(grad_pred_low.astype(f32), axis=0)
    grad_head = left_product(grad_pred_low, final_low)
    grad_final = right_product(grad_pred_low, head_columns).reshape(local, TOK, D)
    unused, final_pull = jax.vjp(modulate, residual, final_mods[:, :D], final_mods[:, D:])
    grad_residual, grad_shift_final, grad_scale_final = final_pull(grad_final)
    mod_grads = [None] * LAYERS
    attn_sums = [None] * LAYERS
    mlp_shards = [None] * LAYERS
    shards = [None] * LAYERS
    bias_pieces = [None] * LAYERS
    for layer_index in reversed(range(LAYERS)):
        qkv_full, proj_full, up_full, down_full = weights_of(layer_index)
        (
            residual_in,
            hidden_low,
            packed_low,
            log_total,
            mixed_low,
            attn_out,
            residual_mid,
            hidden_two_low,
            pre_act,
            act_low,
            mlp_out,
        ) = stored[layer_index]
        segment = modulations[:, layer_index * 6 * D : (layer_index + 1) * 6 * D]
        mod_terms = [segment[:, part_index * D : (part_index + 1) * D] for part_index in range(6)]
        shift_attn, scale_attn, gate_attn, shift_mlp, scale_mlp, gate_mlp = mod_terms
        grad_gate_mlp = jnp.sum(grad_residual * mlp_out, axis=1)
        grad_mlp_low = (grad_residual * gate_mlp[:, None, :]).reshape(row_count, D).astype(low)
        grad_down_bias = jnp.sum(grad_mlp_low.astype(f32), axis=0)
        grad_down = left_product(act_low, grad_mlp_low)
        grad_act = right_product(grad_mlp_low, down_full)
        grad_pre_low = gelu_pull(pre_act, grad_act).astype(low)
        grad_up_bias = jnp.sum(grad_pre_low.astype(f32), axis=0)
        grad_up = left_product(hidden_two_low, grad_pre_low)
        grad_hidden_two = right_product(grad_pre_low, up_full).reshape(local, TOK, D)
        unused, mlp_pull = jax.vjp(modulate, residual_mid, shift_mlp, scale_mlp)
        part_residual, grad_shift_mlp, grad_scale_mlp = mlp_pull(grad_hidden_two)
        grad_residual = grad_residual + part_residual
        grad_gate_attn = jnp.sum(grad_residual * attn_out, axis=1)
        grad_attn_low = (grad_residual * gate_attn[:, None, :]).reshape(row_count, D).astype(low)
        grad_proj_bias = jnp.sum(grad_attn_low.astype(f32), axis=0)
        grad_proj = left_product(mixed_low, grad_attn_low)
        grad_mixed_low = right_product(grad_attn_low, proj_full).astype(low)
        sent_mlp = [
            grad_up[:, part * D : (part + 1) * D].astype(low).reshape(count, rows, D)
            for part in range(4)
        ]
        sent_mlp.append(grad_down.astype(low).reshape(count, 4 * rows, D))
        sent_mlp = jnp.concatenate(sent_mlp, axis=1).reshape(count * 8 * rows, D)
        sent_mlp, grad_mixed_low = lax.optimization_barrier((sent_mlp, grad_mixed_low))
        mlp_shards[layer_index] = lax.psum_scatter(
            sent_mlp, "fsdp", scatter_dimension=0, tiled=True
        ).astype(f32)
        if layer_index + 1 < LAYERS:
            grad_mixed_low = attn_sums[layer_index + 1].before(grad_mixed_low)
            attn_sums[layer_index + 1].step()
        grad_packed_low = attention_backward(packed_low, log_total, grad_mixed_low, local)
        if layer_index + 1 < LAYERS:
            grad_packed_low = attn_sums[layer_index + 1].before(grad_packed_low)
            attn_sums[layer_index + 1].step()
        grad_query_bias = jnp.sum(grad_packed_low[0].astype(f32), axis=0)
        grad_value_bias = jnp.sum(grad_packed_low[2].astype(f32), axis=0)
        grad_qkv = [left_product(hidden_low, item) for item in grad_packed_low]
        grad_hidden = (
            right_product(grad_packed_low[0], qkv_full[0])
            + right_product(grad_packed_low[1], qkv_full[1])
            + right_product(grad_packed_low[2], qkv_full[2])
        ).reshape(local, TOK, D)
        unused, attn_pull = jax.vjp(modulate, residual_in, shift_attn, scale_attn)
        part_residual, grad_shift_attn, grad_scale_attn = attn_pull(grad_hidden)
        grad_residual = grad_residual + part_residual
        mod_grads[layer_index] = jnp.concatenate(
            [
                grad_shift_attn,
                grad_scale_attn,
                grad_gate_attn,
                grad_shift_mlp,
                grad_scale_mlp,
                grad_gate_mlp,
            ],
            axis=1,
        )
        sent = [item.astype(low).reshape(count, rows, D) for item in grad_qkv + [grad_proj]]
        attn_sums[layer_index] = ScatterSum(sent, count, layer_index % 2 == 0)
        attn_sums[layer_index].step()
        (grad_residual, mod_grads[layer_index]) = attn_sums[layer_index].before(
            (grad_residual, mod_grads[layer_index])
        )
        attn_sums[layer_index].step()
        bias_pieces[layer_index] = [
            grad_query_bias,
            grad_value_bias,
            grad_proj_bias,
            grad_up_bias,
            grad_down_bias,
        ]
    grad_zero_low = grad_residual.reshape(row_count, D).astype(low)
    grad_patch_bias = jnp.sum(grad_zero_low.astype(f32), axis=0)
    grad_patch = left_product(noised_low, grad_zero_low)

    grad_mods_low = jnp.concatenate(mod_grads + [grad_shift_final, grad_scale_final], axis=1)
    grad_mods_columns = lax.all_to_all(
        grad_mods_low.astype(low), "fsdp", split_axis=1, concat_axis=0, tiled=True
    )
    grad_act = lax.all_to_all(
        right_product(mod_columns, grad_mods_columns), "fsdp", split_axis=0, concat_axis=0, tiled=True
    )
    grad_act = jnp.sum(grad_act.reshape(count, rows, samples), axis=0)
    grad_act = attn_sums[0].before(grad_act)
    attn_sums[0].step()
    grad_act, grad_mods_later = lax.optimization_barrier((grad_act, grad_mods_columns))
    shard_mod = lax.all_to_all(
        left_product(cond_low, grad_mods_later).astype(low),
        "fsdp",
        split_axis=0,
        concat_axis=1,
        tiled=True,
    ).astype(f32)
    own_bias = lax.dynamic_slice(second_bias, (me * rows,), (rows,))
    condition_own = (
        right_product(tables_low[:, :D], first_low)
        + own_bias[:, None]
        + right_product(tables_low[:, class_at:patch_at], class_rows)
    )
    unused, silu_pull = jax.vjp(jax.nn.silu, condition_own)
    grad_condition = silu_pull(grad_act)[0]
    grad_class = lax.dot_general(
        grad_condition,
        class_rows.astype(f32),
        (((1,), (0,)), ((), ())),
        precision=lax.Precision.HIGHEST,
        preferred_element_type=f32,
    )[:, :CLASSES]
    grad_time_low = grad_condition.astype(low)
    grad_second_bias = jnp.sum(grad_time_low.astype(f32), axis=1)
    grad_second = product(grad_time_low, first_low)
    grad_time_all = lax.all_to_all(
        jnp.broadcast_to(grad_time_low[None], (count, rows, samples)).reshape(D, samples),
        "fsdp",
        split_axis=0,
        concat_axis=0,
        tiled=True,
    )
    grad_time_all = attn_sums[0].before(grad_time_all)
    attn_sums[0].step()
    grad_first_act = lax.dynamic_slice(
        left_product(tables_full[:, :D], grad_time_all), (me * rows, 0), (rows, samples)
    )
    own_bias = lax.dynamic_slice(first_bias, (me * rows,), (rows,))
    first_pre_own = right_product(tables_low[:, first_at:class_at], features_low) + own_bias[:, None]
    unused, first_pull = jax.vjp(jax.nn.silu, first_pre_own)
    grad_first_low = first_pull(grad_first_act)[0].astype(low)
    grad_first_bias = jnp.sum(grad_first_low.astype(f32), axis=1)
    grad_first = product(grad_first_low, features_low)
    grad_middle = jnp.concatenate([grad_first, grad_second, grad_class], axis=1).T

    def spread(piece, length):
        return lax.dynamic_update_slice(jnp.zeros((length,), f32), piece, (me * piece.shape[0],))

    own_mod_bias = spread(jnp.sum(grad_mods_columns.astype(f32), axis=0), MODW)
    pieces = []
    for layer_index in range(LAYERS):
        pieces += bias_pieces[layer_index]
        pieces.append(own_mod_bias[layer_index * 6 * D : (layer_index + 1) * 6 * D])
    pieces += [
        own_mod_bias[LAYERS * 6 * D :],
        grad_patch_bias,
        spread(grad_first_bias, D),
        spread(grad_second_bias, D),
        grad_head_bias,
    ]
    pieces += [grad_patch.reshape(-1), grad_head.reshape(-1)]
    summed = sum_all(jnp.concatenate(pieces), count)
    bias_length = biases.shape[0]
    bias_grad = summed[:bias_length]
    ends = summed[bias_length:].reshape(2 * PD, D)
    own_ends = lax.dynamic_slice(ends, (0, me * rows), (2 * PD, rows))
    shard_tables = jnp.concatenate([own_ends[:PD], grad_middle, own_ends[PD:]], axis=0)
    for layer_index in range(LAYERS):
        shard = mlp_shards[layer_index]
        parts = [attn_sums[layer_index].finish()[part * rows : (part + 1) * rows] for part in range(4)]
        parts += [shard[part * rows : (part + 1) * rows] for part in range(4)]
        shards[layer_index] = (
            jnp.concatenate(parts[:3], axis=1),
            parts[3],
            jnp.concatenate(parts[4:], axis=1),
            shard[4 * rows :],
        )
    shard_squares = jnp.sum(shard_mod * shard_mod) + jnp.sum(shard_tables * shard_tables)
    for layer_index in range(LAYERS):
        for item in shards[layer_index]:
            shard_squares = shard_squares + jnp.sum(item * item)
    square_total, loss_value = sum_all(jnp.stack([shard_squares, loss_local]), count)
    grad_norm = jnp.sqrt(square_total + jnp.sum(bias_grad * bias_grad))
    factor = jnp.minimum(1.0, clip_limit / (grad_norm + 1e-06))
    shard_qkv, shard_proj, shard_up, shard_down = [
        jnp.stack([shards[layer_index][part] for layer_index in range(LAYERS)]) for part in range(4)
    ]
    qkv_update, qkv_first_new, qkv_second_new = adam_step(
        qkv_weight, shard_qkv, qkv_first, qkv_second, factor
    )
    proj_update, proj_first_new, proj_second_new = adam_step(
        proj_weight, shard_proj, proj_first, proj_second, factor
    )
    up_update, up_first_new, up_second_new = adam_step(
        up_weight, shard_up, up_first, up_second, factor
    )
    down_update, down_first_new, down_second_new = adam_step(
        down_weight, shard_down, down_first, down_second, factor
    )
    mod_update, mod_first_new, mod_second_new = adam_step(
        mod_weight, shard_mod, mod_first, mod_second, factor
    )
    tables_update, tables_first_new, tables_second_new = adam_step(
        tables, shard_tables, tables_first, tables_second, factor
    )
    biases_update, biases_first_new, biases_second_new = adam_step(
        biases, bias_grad, biases_first, biases_second, factor
    )
    return (
        loss_value,
        grad_norm,
        qkv_update,
        qkv_first_new,
        qkv_second_new,
        proj_update,
        proj_first_new,
        proj_second_new,
        up_update,
        up_first_new,
        up_second_new,
        down_update,
        down_first_new,
        down_second_new,
        mod_update,
        mod_first_new,
        mod_second_new,
        tables_update,
        tables_first_new,
        tables_second_new,
        biases_update,
        biases_first_new,
        biases_second_new,
    )


def solution(mesh):
    in_specs = (
        P("fsdp", None, None),
        P("fsdp", None, None),
        P("fsdp"),
        P("fsdp"),
        P(None, "fsdp", None),
        P(None, "fsdp", None),
        P(None, "fsdp", None),
        P(None, "fsdp", None),
        P("fsdp", None),
        P(None, "fsdp"),
        P(),
        P(None, "fsdp", None),
        P(None, "fsdp", None),
        P(None, "fsdp", None),
        P(None, "fsdp", None),
        P("fsdp", None),
        P(None, "fsdp"),
        P(),
        P(None, "fsdp", None),
        P(None, "fsdp", None),
        P(None, "fsdp", None),
        P(None, "fsdp", None),
        P("fsdp", None),
        P(None, "fsdp"),
        P(),
    )
    out_specs = (
        P(),
        P(),
        P(None, "fsdp", None),
        P(None, "fsdp", None),
        P(None, "fsdp", None),
        P(None, "fsdp", None),
        P(None, "fsdp", None),
        P(None, "fsdp", None),
        P(None, "fsdp", None),
        P(None, "fsdp", None),
        P(None, "fsdp", None),
        P(None, "fsdp", None),
        P(None, "fsdp", None),
        P(None, "fsdp", None),
        P("fsdp", None),
        P("fsdp", None),
        P("fsdp", None),
        P(None, "fsdp"),
        P(None, "fsdp"),
        P(None, "fsdp"),
        P(),
        P(),
        P(),
    )
    return jax.shard_map(body, mesh=mesh, in_specs=in_specs, out_specs=out_specs, check_vma=False)
```

```python
import math

import jax
import jax.numpy as jnp
from jax import lax
from jax.experimental import pallas as pl
from jax.sharding import PartitionSpec as P

D = 768
HEADS = 12
HD = 64
FF = 3072
FREQ = 256
CLASSES = 1000
DIFF_STEPS = 1000
LAYERS = 2
TOK = 256
PD = 16
MODW = 10752


norm_eps = 1e-06
clip_limit = 2.5
learn_rate = 0.01
beta_first = 0.9
beta_second = 0.95
adam_eps = 1e-08
weight_decay = 0.01
first_fix = 1.0 - 0.9**10
second_fix = 1.0 - 0.95**10


def modulate(residual, shift_term, scale_term):
    centred = residual - jnp.mean(residual, axis=-1, keepdims=True)
    spread = jnp.mean(centred * centred, axis=-1, keepdims=True)
    normed = centred * lax.rsqrt(spread + norm_eps)
    return normed * (1.0 + scale_term[:, None, :]) + shift_term[:, None, :]


gelu_rate = math.sqrt(2.0 / math.pi)
gelu_cubic = 0.044715 * gelu_rate


def gelu_tanh(values):
    raised = jnp.tanh(values * (gelu_rate + gelu_cubic * (values * values)))
    return (0.5 * values) * (1.0 + raised)


def gelu_pull(values, grad):
    square = values * values
    raised = jnp.tanh(values * (gelu_rate + gelu_cubic * square))
    slope = (1.0 - raised) * (values * (gelu_rate + 3.0 * gelu_cubic * square))
    return (0.5 * grad) * ((1.0 + raised) * (1.0 + slope))


def product(left_side, right_side):
    return jnp.dot(left_side, right_side, preferred_element_type=jnp.float32)


def left_product(left_side, right_side):
    return lax.dot_general(
        left_side, right_side, (((0,), (0,)), ((), ())), preferred_element_type=jnp.float32
    )


def right_product(left_side, right_side):
    return lax.dot_general(
        left_side, right_side, (((1,), (1,)), ((), ())), preferred_element_type=jnp.float32
    )


def time_features(steps_in):
    half_count = FREQ // 2
    frequencies = jnp.exp(
        -math.log(10000.0) * jnp.arange(half_count, dtype=jnp.float32) / half_count
    )
    angles = steps_in.astype(jnp.float32)[:, None] * frequencies[None, :]
    return jnp.concatenate([jnp.cos(angles), jnp.sin(angles)], axis=1)


def noise_share(steps_in):
    beta_values = jnp.linspace(0.0001, 0.02, DIFF_STEPS, dtype=jnp.float32)
    log_keep = jnp.log(1.0 - beta_values)
    taken = jnp.arange(DIFF_STEPS, dtype=jnp.int32)[None, :] <= steps_in[:, None]
    return jnp.exp(jnp.sum(jnp.where(taken, log_keep[None, :], 0.0), axis=1))


def bias_parts(biases):
    per_layer = 10 * D + FF
    layer_parts = []
    for layer_index in range(LAYERS):
        anchor = layer_index * per_layer
        layer_parts.append(
            (
                biases[anchor : anchor + D],
                biases[anchor + D : anchor + 2 * D],
                biases[anchor + 2 * D : anchor + 3 * D],
                biases[anchor + 3 * D : anchor + 3 * D + FF],
                biases[anchor + 3 * D + FF : anchor + 4 * D + FF],
                biases[anchor + 4 * D + FF : anchor + per_layer],
            )
        )
    anchor = LAYERS * per_layer
    global_parts = (
        biases[anchor : anchor + 2 * D],
        biases[anchor + 2 * D : anchor + 3 * D],
        biases[anchor + 3 * D : anchor + 4 * D],
        biases[anchor + 4 * D : anchor + 5 * D],
        biases[anchor + 5 * D : anchor + 5 * D + PD],
    )
    return (layer_parts, global_parts)


def hop_plan(count):
    if count == 32:
        return [(8, 4), (2, 2), (4, 2), (1, 2)]
    plan = []
    stride = 1
    while stride < count:
        plan.append((stride, 2))
        stride *= 2
    return plan


def shifted(index, stride, size, amount):
    coord = (index // stride) % size
    return index + ((coord + amount) % size - coord) * stride


def send(value, count, stride, size, amount=1):
    pairs = [(index, shifted(index, stride, size, amount)) for index in range(count)]
    return lax.ppermute(value, "fsdp", pairs)


def gather_near(value, count):
    gathered = value[None]
    for stride, size in hop_plan(count):
        pieces = [gathered]
        for unused in range(size - 1):
            pieces.append(send(pieces[-1], count, stride, size))
        gathered = jnp.concatenate(pieces, axis=0)
    return gathered


def near_places(count):
    me = lax.axis_index("fsdp")
    others = jnp.arange(count, dtype=jnp.int32)
    places = jnp.zeros((count,), jnp.int32)
    weight = 1
    for stride, size in hop_plan(count):
        steps = ((me // stride) % size - (others // stride) % size) % size
        places = places + steps * weight
        weight *= size
    return places


def mesh_dims(count):
    if count == 32:
        return (4, 2, 2, 2)
    return (2,) * (count.bit_length() - 1)


def fold(parts, axis, stride, count):
    size = parts[0].shape[axis]
    mine = (lax.axis_index("fsdp") // stride) % size

    def entry(index):
        picked = [lax.dynamic_index_in_dim(part, index, axis, keepdims=False) for part in parts]
        return picked[0] if len(picked) == 1 else jnp.concatenate(picked, axis=-2)

    arrived = [
        send(entry((mine + step) % size), count, stride, size, step) for step in range(1, size)
    ]
    total = entry(mine).astype(jnp.float32)
    for piece in arrived:
        total = total + piece.astype(jnp.float32)
    return total


class ScatterSum:
    def __init__(self, parts, count, swap):
        dims = mesh_dims(count)
        self.count = count
        self.strides = [1]
        for size in reversed(dims[1:]):
            self.strides.insert(0, self.strides[0] * size)
        self.value = [part.reshape(dims + part.shape[1:]) for part in parts]
        self.axes = list(range(len(dims)))
        self.order = list(reversed(self.axes))
        if swap:
            self.order[1], self.order[2] = self.order[2], self.order[1]

    def step(self):
        if not self.order:
            return
        axis = self.order.pop(0)
        place = self.axes.index(axis)
        total = fold(self.value, place, self.strides[axis], self.count)
        self.axes.remove(axis)
        self.value = [total.astype(jnp.bfloat16) if self.order else total]

    def before(self, values):
        self.value[0], values = lax.optimization_barrier((self.value[0], values))
        return values

    def finish(self):
        while self.order:
            self.step()
        return self.value[0]


def sum_all(value, count):
    stride = 1
    while stride < count:
        value = value + send(value, count, stride, 2)
        stride *= 2
    return value


def pair_scores(queries, keys_all, first_half):
    only = jnp.where(first_half, queries, jnp.zeros_like(queries))
    return only, right_product(only, keys_all) * HD ** (-0.5)


def attention_forward_kernel(queries_ref, keys_ref, values_ref, mixed_ref, total_ref):
    lanes = lax.broadcasted_iota(jnp.int32, (TOK, 2 * HD), 1)
    totals = jnp.zeros((TOK, 2 * HD), jnp.float32)
    for pair in range(HEADS // 2):
        span = slice(pair * 2 * HD, (pair + 1) * 2 * HD)
        queries, keys_all, values_all = queries_ref[:, span], keys_ref[:, span], values_ref[:, span]
        halves = []
        for half in range(2):
            mine = (lanes < HD) if half == 0 else (lanes >= HD)
            unused, scores = pair_scores(queries, keys_all, mine)
            row_max = jnp.max(scores, axis=1, keepdims=True)
            raised = jnp.exp(scores - row_max)
            row_sum = jnp.sum(raised, axis=1, keepdims=True)
            soft_low = (raised / row_sum).astype(jnp.bfloat16)
            halves.append(product(soft_low, values_all))
            totals = jnp.where(lanes == 2 * pair + half, row_max + jnp.log(row_sum), totals)
        mixed_ref[:, span] = jnp.where(lanes < HD, halves[0], halves[1]).astype(jnp.bfloat16)
    total_ref[...] = totals


def attention_backward_kernel(
    queries_ref, keys_ref, values_ref, total_ref, grad_ref, dqueries_ref, dkeys_ref, dvalues_ref
):
    lanes = lax.broadcasted_iota(jnp.int32, (TOK, 2 * HD), 1)
    for pair in range(HEADS // 2):
        span = slice(pair * 2 * HD, (pair + 1) * 2 * HD)
        queries, keys_all, values_all = queries_ref[:, span], keys_ref[:, span], values_ref[:, span]
        grads = grad_ref[:, span]
        made = []
        for half in range(2):
            mine = (lanes < HD) if half == 0 else (lanes >= HD)
            unused, scores = pair_scores(queries, keys_all, mine)
            head = 2 * pair + half
            soft_weights = jnp.exp(scores - total_ref[:, head : head + 1])
            grad_values = left_product(soft_weights.astype(jnp.bfloat16), grads)
            grad_soft = right_product(jnp.where(mine, grads, jnp.zeros_like(grads)), values_all)
            spread = jnp.sum(soft_weights * grad_soft, axis=1, keepdims=True)
            score_low = (soft_weights * (grad_soft - spread)).astype(jnp.bfloat16)
            made.append(
                (
                    product(score_low, keys_all) * HD ** (-0.5),
                    left_product(score_low, queries) * HD ** (-0.5),
                    grad_values,
                )
            )
        for part, target in enumerate((dqueries_ref, dkeys_ref, dvalues_ref)):
            target[:, span] = jnp.where(lanes < HD, made[0][part], made[1][part]).astype(
                jnp.bfloat16
            )


def token_block(width):
    return pl.BlockSpec((TOK, width), lambda sample: (sample, 0))


def attention_forward(packed_low, sample_count):
    row_count = sample_count * TOK
    return pl.pallas_call(
        attention_forward_kernel,
        grid=(sample_count,),
        in_specs=[token_block(D)] * 3,
        out_specs=[token_block(D), token_block(2 * HD)],
        out_shape=[
            jax.ShapeDtypeStruct((row_count, D), jnp.bfloat16),
            jax.ShapeDtypeStruct((row_count, 2 * HD), jnp.float32),
        ],
        cost_estimate=pl.CostEstimate(
            flops=8 * 10**9, bytes_accessed=8 * row_count * D, transcendentals=row_count * TOK * HEADS
        ),
        name="attention_forward",
    )(*packed_low)


def attention_backward(packed_low, log_total, grad_mixed_low, sample_count):
    row_count = sample_count * TOK
    return pl.pallas_call(
        attention_backward_kernel,
        grid=(sample_count,),
        in_specs=[token_block(D)] * 3 + [token_block(2 * HD), token_block(D)],
        out_specs=[token_block(D)] * 3,
        out_shape=[jax.ShapeDtypeStruct((row_count, D), jnp.bfloat16)] * 3,
        cost_estimate=pl.CostEstimate(
            flops=20 * 10**9, bytes_accessed=14 * row_count * D, transcendentals=row_count * TOK * HEADS
        ),
        name="attention_backward",
    )(*packed_low, log_total, grad_mixed_low)


def adam_step(weight_now, grad_now, first_old, second_old, factor):
    clipped = grad_now * factor
    first_new = beta_first * first_old + (1.0 - beta_first) * clipped
    second_new = beta_second * second_old + (1.0 - beta_second) * clipped * clipped
    step_size = -learn_rate * (
        first_new / first_fix / (jnp.sqrt(second_new / second_fix) + adam_eps)
        + weight_decay * weight_now
    )
    return (step_size, first_new, second_new)


def body(
    latents,
    noise,
    timesteps,
    labels,
    qkv_weight,
    proj_weight,
    up_weight,
    down_weight,
    mod_weight,
    tables,
    biases,
    qkv_first,
    proj_first,
    up_first,
    down_first,
    mod_first,
    tables_first,
    biases_first,
    qkv_second,
    proj_second,
    up_second,
    down_second,
    mod_second,
    tables_second,
    biases_second,
):
    count = lax.axis_size("fsdp")
    me = lax.axis_index("fsdp")
    local = latents.shape[0]
    samples = local * count
    rows = D // count
    row_count = local * TOK
    total_count = samples * TOK * PD
    low = jnp.bfloat16
    f32 = jnp.float32
    layer_parts, global_parts = bias_parts(biases)
    final_bias, patch_bias, first_bias, second_bias, head_bias = global_parts
    mod_bias = jnp.concatenate([part_item[5] for part_item in layer_parts] + [final_bias])

    gathered = []
    for layer_index in range(LAYERS):
        pieces = [qkv_weight[layer_index][:, part * D : (part + 1) * D] for part in range(3)]
        pieces.append(proj_weight[layer_index])
        pieces += [up_weight[layer_index][:, part * D : (part + 1) * D] for part in range(4)]
        pieces.append(down_weight[layer_index])
        packed = jnp.concatenate(pieces, axis=0).astype(low).reshape(12, rows, D)
        gathered.append(lax.all_gather(packed, "fsdp", axis=1, tiled=True))

    mod_low = mod_weight.astype(low)
    mod_columns = lax.all_to_all(mod_low, "fsdp", split_axis=1, concat_axis=0, tiled=True)
    digits = jnp.concatenate([timesteps // 32, timesteps % 32, labels // 32, labels % 32]).astype(low)
    table_low = tables.astype(low).T
    room = -(-CLASSES // 128) * 128
    first_at, class_at, patch_at = D, D + FREQ, D + FREQ + room
    head_at, digit_at = patch_at + PD, patch_at + 2 * PD
    tables_low = jnp.concatenate(
        [
            table_low[:, PD + FREQ : PD + FREQ + D],
            table_low[:, PD : PD + FREQ],
            table_low[:, PD + FREQ + D : PD + FREQ + D + CLASSES],
            jnp.zeros((rows, room - CLASSES), low),
            table_low[:, :PD],
            table_low[:, PD + FREQ + D + CLASSES :],
            jnp.broadcast_to(digits[None, :], (rows, 4 * local)),
        ],
        axis=1,
    )
    tables_near = gather_near(tables_low, count)
    places = near_places(count)
    tables_far = jnp.take(tables_near, places, axis=0, mode="clip")
    tables_full = tables_far.reshape(D, digit_at + 4 * local)

    numbers = tables_far[:, 0, digit_at:].astype(jnp.int32).reshape(count, 4, local)
    steps_all = (numbers[:, 0] * 32 + numbers[:, 1]).reshape(samples)
    labels_all = (numbers[:, 2] * 32 + numbers[:, 3]).reshape(samples)
    features_low = time_features(steps_all).astype(low)
    first_pre = right_product(features_low, tables_full[:, first_at:class_at]) + first_bias
    first_low = jax.nn.silu(first_pre).astype(low)
    class_rows = (labels_all[:, None] == jnp.arange(room, dtype=jnp.int32)[None, :]).astype(low)
    condition = (
        right_product(first_low, tables_full[:, :D])
        + second_bias
        + right_product(class_rows, tables_full[:, class_at:patch_at])
    )
    cond_low = jax.nn.silu(condition).astype(low)
    mods_columns = product(cond_low, mod_columns)
    modulations = (
        lax.all_to_all(mods_columns, "fsdp", split_axis=0, concat_axis=1, tiled=True) + mod_bias
    )

    keep_share = noise_share(timesteps)
    noised = (
        jnp.sqrt(keep_share)[:, None, None] * latents
        + jnp.sqrt(1.0 - keep_share)[:, None, None] * noise
    )
    noised_low = noised.reshape(row_count, PD).astype(low)
    patch_columns = tables_full[:, patch_at:head_at]
    head_columns = tables_full[:, head_at:digit_at]
    residual = (right_product(noised_low, patch_columns) + patch_bias).reshape(local, TOK, D)

    def weights_of(layer_index):
        whole = gathered[layer_index]
        square = [whole[part] for part in range(8)]
        up_full = jnp.concatenate(square[4:], axis=1)
        down_full = whole[8:].reshape(4, count, rows, D).transpose(1, 0, 2, 3).reshape(FF, D)
        return square[:3], square[3], up_full, down_full

    stored = []
    for layer_index in range(LAYERS):
        gathered[layer_index], residual = lax.optimization_barrier(
            (gathered[layer_index], residual)
        )
        qkv_full, proj_full, up_full, down_full = weights_of(layer_index)
        query_bias, value_bias, proj_bias, up_bias, down_bias, unused = layer_parts[layer_index]
        segment = modulations[:, layer_index * 6 * D : (layer_index + 1) * 6 * D]
        mod_terms = [segment[:, part_index * D : (part_index + 1) * D] for part_index in range(6)]
        shift_attn, scale_attn, gate_attn, shift_mlp, scale_mlp, gate_mlp = mod_terms
        residual_in = residual
        hidden_low = modulate(residual_in, shift_attn, scale_attn).reshape(row_count, D).astype(low)
        packed_low = [
            (product(hidden_low, qkv_full[0]) + query_bias).astype(low),
            product(hidden_low, qkv_full[1]).astype(low),
            (product(hidden_low, qkv_full[2]) + value_bias).astype(low),
        ]
        mixed, log_total = attention_forward(packed_low, local)
        mixed_low = mixed.astype(low)
        attn_out = (product(mixed_low, proj_full) + proj_bias).reshape(local, TOK, D)
        residual_mid = residual_in + gate_attn[:, None, :] * attn_out
        hidden_two_low = modulate(residual_mid, shift_mlp, scale_mlp).reshape(row_count, D).astype(low)
        pre_act = product(hidden_two_low, up_full) + up_bias
        act_low = lax.optimization_barrier(gelu_tanh(pre_act).astype(low))
        mlp_out = (product(act_low, down_full) + down_bias).reshape(local, TOK, D)
        residual = residual_mid + gate_mlp[:, None, :] * mlp_out
        stored.append(
            (
                residual_in,
                hidden_low,
                packed_low,
                log_total,
                mixed_low,
                attn_out,
                residual_mid,
                hidden_two_low,
                pre_act,
                act_low,
                mlp_out,
            )
        )
    final_mods = modulations[:, LAYERS * 6 * D :]
    final_hidden = modulate(residual, final_mods[:, :D], final_mods[:, D:])
    final_low = final_hidden.reshape(row_count, D).astype(low)
    predicted = product(final_low, head_columns) + head_bias
    errors = predicted - noise.reshape(row_count, PD)
    loss_local = jnp.sum(errors * errors) / total_count
    grad_pred_low = (2.0 * errors / total_count).astype(low)
    grad_head_bias = jnp.sum(grad_pred_low.astype(f32), axis=0)
    grad_head = left_product(grad_pred_low, final_low)
    grad_final = right_product(grad_pred_low, head_columns).reshape(local, TOK, D)
    unused, final_pull = jax.vjp(modulate, residual, final_mods[:, :D], final_mods[:, D:])
    grad_residual, grad_shift_final, grad_scale_final = final_pull(grad_final)
    mod_grads = [None] * LAYERS
    attn_sums = [None] * LAYERS
    mlp_shards = [None] * LAYERS
    shards = [None] * LAYERS
    bias_pieces = [None] * LAYERS
    for layer_index in reversed(range(LAYERS)):
        qkv_full, proj_full, up_full, down_full = weights_of(layer_index)
        (
            residual_in,
            hidden_low,
            packed_low,
            log_total,
            mixed_low,
            attn_out,
            residual_mid,
            hidden_two_low,
            pre_act,
            act_low,
            mlp_out,
        ) = stored[layer_index]
        segment = modulations[:, layer_index * 6 * D : (layer_index + 1) * 6 * D]
        mod_terms = [segment[:, part_index * D : (part_index + 1) * D] for part_index in range(6)]
        shift_attn, scale_attn, gate_attn, shift_mlp, scale_mlp, gate_mlp = mod_terms
        grad_gate_mlp = jnp.sum(grad_residual * mlp_out, axis=1)
        grad_mlp_low = (grad_residual * gate_mlp[:, None, :]).reshape(row_count, D).astype(low)
        grad_down_bias = jnp.sum(grad_mlp_low.astype(f32), axis=0)
        grad_down = left_product(act_low, grad_mlp_low)
        grad_act = right_product(grad_mlp_low, down_full)
        grad_pre_low = gelu_pull(pre_act, grad_act).astype(low)
        grad_up_bias = jnp.sum(grad_pre_low.astype(f32), axis=0)
        grad_up = left_product(hidden_two_low, grad_pre_low)
        grad_hidden_two = right_product(grad_pre_low, up_full).reshape(local, TOK, D)
        unused, mlp_pull = jax.vjp(modulate, residual_mid, shift_mlp, scale_mlp)
        part_residual, grad_shift_mlp, grad_scale_mlp = mlp_pull(grad_hidden_two)
        grad_residual = grad_residual + part_residual
        grad_gate_attn = jnp.sum(grad_residual * attn_out, axis=1)
        grad_attn_low = (grad_residual * gate_attn[:, None, :]).reshape(row_count, D).astype(low)
        grad_proj_bias = jnp.sum(grad_attn_low.astype(f32), axis=0)
        grad_proj = left_product(mixed_low, grad_attn_low)
        grad_mixed_low = right_product(grad_attn_low, proj_full).astype(low)
        sent_mlp = [
            grad_up[:, part * D : (part + 1) * D].astype(low).reshape(count, rows, D)
            for part in range(4)
        ]
        sent_mlp.append(grad_down.astype(low).reshape(count, 4 * rows, D))
        sent_mlp = jnp.concatenate(sent_mlp, axis=1).reshape(count * 8 * rows, D)
        sent_mlp, grad_mixed_low = lax.optimization_barrier((sent_mlp, grad_mixed_low))
        mlp_shards[layer_index] = lax.psum_scatter(
            sent_mlp, "fsdp", scatter_dimension=0, tiled=True
        ).astype(f32)
        grad_packed_low = attention_backward(packed_low, log_total, grad_mixed_low, local)
        if layer_index + 1 < LAYERS:
            grad_packed_low = attn_sums[layer_index + 1].before(grad_packed_low)
            attn_sums[layer_index + 1].step()
        grad_query_bias = jnp.sum(grad_packed_low[0].astype(f32), axis=0)
        grad_value_bias = jnp.sum(grad_packed_low[2].astype(f32), axis=0)
        grad_qkv = [left_product(hidden_low, item) for item in grad_packed_low]
        grad_hidden = (
            right_product(grad_packed_low[0], qkv_full[0])
            + right_product(grad_packed_low[1], qkv_full[1])
            + right_product(grad_packed_low[2], qkv_full[2])
        ).reshape(local, TOK, D)
        unused, attn_pull = jax.vjp(modulate, residual_in, shift_attn, scale_attn)
        part_residual, grad_shift_attn, grad_scale_attn = attn_pull(grad_hidden)
        grad_residual = grad_residual + part_residual
        mod_grads[layer_index] = jnp.concatenate(
            [
                grad_shift_attn,
                grad_scale_attn,
                grad_gate_attn,
                grad_shift_mlp,
                grad_scale_mlp,
                grad_gate_mlp,
            ],
            axis=1,
        )
        sent = [item.astype(low).reshape(count, rows, D) for item in grad_qkv + [grad_proj]]
        attn_sums[layer_index] = ScatterSum(sent, count, layer_index % 2 == 0)
        attn_sums[layer_index].step()
        if layer_index + 1 < LAYERS:
            grad_residual, mod_grads[layer_index] = attn_sums[layer_index + 1].before(
                (grad_residual, mod_grads[layer_index])
            )
            attn_sums[layer_index + 1].step()
        (grad_residual, mod_grads[layer_index]) = attn_sums[layer_index].before(
            (grad_residual, mod_grads[layer_index])
        )
        attn_sums[layer_index].step()
        bias_pieces[layer_index] = [
            grad_query_bias,
            grad_value_bias,
            grad_proj_bias,
            grad_up_bias,
            grad_down_bias,
        ]
    grad_zero_low = grad_residual.reshape(row_count, D).astype(low)
    grad_patch_bias = jnp.sum(grad_zero_low.astype(f32), axis=0)
    grad_patch = left_product(noised_low, grad_zero_low)

    grad_mods_low = jnp.concatenate(
        mod_grads + [grad_shift_final, grad_scale_final], axis=1
    ).astype(low)
    grad_mods_columns = lax.all_to_all(
        grad_mods_low, "fsdp", split_axis=1, concat_axis=0, tiled=True
    )
    grad_mods_columns = attn_sums[0].before(grad_mods_columns)
    attn_sums[0].step()
    grad_act_sent = right_product(mod_columns, grad_mods_columns).astype(low)
    grad_act = lax.all_to_all(
        grad_act_sent,
        "fsdp",
        split_axis=0,
        concat_axis=0,
        tiled=True,
    )
    grad_act = jnp.sum(grad_act.reshape(count, rows, samples).astype(f32), axis=0)
    grad_act = attn_sums[0].before(grad_act)
    attn_sums[0].step()
    grad_act, grad_mods_later = lax.optimization_barrier((grad_act, grad_mods_columns))
    shard_mod = lax.all_to_all(
        left_product(cond_low, grad_mods_later).astype(low),
        "fsdp",
        split_axis=0,
        concat_axis=1,
        tiled=True,
    ).astype(f32)
    own_bias = lax.dynamic_slice(second_bias, (me * rows,), (rows,))
    condition_own = (
        right_product(tables_low[:, :D], first_low)
        + own_bias[:, None]
        + right_product(tables_low[:, class_at:patch_at], class_rows)
    )
    unused, silu_pull = jax.vjp(jax.nn.silu, condition_own)
    grad_condition = silu_pull(grad_act)[0]
    grad_class = lax.dot_general(
        grad_condition,
        class_rows.astype(f32),
        (((1,), (0,)), ((), ())),
        precision=lax.Precision.HIGHEST,
        preferred_element_type=f32,
    )[:, :CLASSES]
    grad_time_low = grad_condition.astype(low)
    grad_second_bias = jnp.sum(grad_time_low.astype(f32), axis=1)
    grad_second = product(grad_time_low, first_low)
    grad_time_all = lax.all_to_all(
        jnp.broadcast_to(grad_time_low[None], (count, rows, samples)).reshape(D, samples),
        "fsdp",
        split_axis=0,
        concat_axis=0,
        tiled=True,
    )
    grad_first_act = lax.dynamic_slice(
        left_product(tables_full[:, :D], grad_time_all), (me * rows, 0), (rows, samples)
    )
    own_bias = lax.dynamic_slice(first_bias, (me * rows,), (rows,))
    first_pre_own = right_product(tables_low[:, first_at:class_at], features_low) + own_bias[:, None]
    unused, first_pull = jax.vjp(jax.nn.silu, first_pre_own)
    grad_first_low = first_pull(grad_first_act)[0].astype(low)
    grad_first_bias = jnp.sum(grad_first_low.astype(f32), axis=1)
    grad_first = product(grad_first_low, features_low)
    grad_middle = jnp.concatenate([grad_first, grad_second, grad_class], axis=1).T

    def spread(piece, length):
        return lax.dynamic_update_slice(jnp.zeros((length,), f32), piece, (me * piece.shape[0],))

    own_mod_bias = jnp.sum(grad_mods_low.astype(f32), axis=0)
    pieces = []
    for layer_index in range(LAYERS):
        pieces += bias_pieces[layer_index]
        pieces.append(own_mod_bias[layer_index * 6 * D : (layer_index + 1) * 6 * D])
    pieces += [
        own_mod_bias[LAYERS * 6 * D :],
        grad_patch_bias,
        grad_head_bias,
    ]
    pieces += [grad_patch.reshape(-1), grad_head.reshape(-1)]
    pieces, unused = lax.optimization_barrier((pieces, grad_act_sent))
    summed = sum_all(jnp.concatenate(pieces), count)
    bias_length = biases.shape[0] - 2 * D
    ends = summed[bias_length:].reshape(2 * PD, D)
    own_ends = lax.dynamic_slice(ends, (0, me * rows), (2 * PD, rows))
    shard_tables = jnp.concatenate([own_ends[:PD], grad_middle, own_ends[PD:]], axis=0)
    for layer_index in range(LAYERS):
        shard = mlp_shards[layer_index]
        parts = [attn_sums[layer_index].finish()[part * rows : (part + 1) * rows] for part in range(4)]
        parts += [shard[part * rows : (part + 1) * rows] for part in range(4)]
        shards[layer_index] = (
            jnp.concatenate(parts[:3], axis=1),
            parts[3],
            jnp.concatenate(parts[4:], axis=1),
            shard[4 * rows :],
        )
    shard_squares = jnp.sum(shard_mod * shard_mod) + jnp.sum(shard_tables * shard_tables)
    for layer_index in range(LAYERS):
        for item in shards[layer_index]:
            shard_squares = shard_squares + jnp.sum(item * item)
    last_sums = sum_all(
        jnp.concatenate(
            [
                spread(grad_first_bias, D),
                spread(grad_second_bias, D),
                shard_squares[None],
                loss_local[None],
            ]
        ),
        count,
    )
    square_total, loss_value = last_sums[2 * D], last_sums[2 * D + 1]
    bias_grad = jnp.concatenate(
        [summed[: bias_length - PD], last_sums[: 2 * D], summed[bias_length - PD : bias_length]]
    )
    grad_norm = jnp.sqrt(square_total + jnp.sum(bias_grad * bias_grad))
    factor = jnp.minimum(1.0, clip_limit / (grad_norm + 1e-06))
    shard_qkv, shard_proj, shard_up, shard_down = [
        jnp.stack([shards[layer_index][part] for layer_index in range(LAYERS)]) for part in range(4)
    ]
    qkv_update, qkv_first_new, qkv_second_new = adam_step(
        qkv_weight, shard_qkv, qkv_first, qkv_second, factor
    )
    proj_update, proj_first_new, proj_second_new = adam_step(
        proj_weight, shard_proj, proj_first, proj_second, factor
    )
    up_update, up_first_new, up_second_new = adam_step(
        up_weight, shard_up, up_first, up_second, factor
    )
    down_update, down_first_new, down_second_new = adam_step(
        down_weight, shard_down, down_first, down_second, factor
    )
    mod_update, mod_first_new, mod_second_new = adam_step(
        mod_weight, shard_mod, mod_first, mod_second, factor
    )
    tables_update, tables_first_new, tables_second_new = adam_step(
        tables, shard_tables, tables_first, tables_second, factor
    )
    biases_update, biases_first_new, biases_second_new = adam_step(
        biases, bias_grad, biases_first, biases_second, factor
    )
    return (
        loss_value,
        grad_norm,
        qkv_update,
        qkv_first_new,
        qkv_second_new,
        proj_update,
        proj_first_new,
        proj_second_new,
        up_update,
        up_first_new,
        up_second_new,
        down_update,
        down_first_new,
        down_second_new,
        mod_update,
        mod_first_new,
        mod_second_new,
        tables_update,
        tables_first_new,
        tables_second_new,
        biases_update,
        biases_first_new,
        biases_second_new,
    )


def solution(mesh):
    in_specs = (
        P("fsdp", None, None),
        P("fsdp", None, None),
        P("fsdp"),
        P("fsdp"),
        P(None, "fsdp", None),
        P(None, "fsdp", None),
        P(None, "fsdp", None),
        P(None, "fsdp", None),
        P("fsdp", None),
        P(None, "fsdp"),
        P(),
        P(None, "fsdp", None),
        P(None, "fsdp", None),
        P(None, "fsdp", None),
        P(None, "fsdp", None),
        P("fsdp", None),
        P(None, "fsdp"),
        P(),
        P(None, "fsdp", None),
        P(None, "fsdp", None),
        P(None, "fsdp", None),
        P(None, "fsdp", None),
        P("fsdp", None),
        P(None, "fsdp"),
        P(),
    )
    out_specs = (
        P(),
        P(),
        P(None, "fsdp", None),
        P(None, "fsdp", None),
        P(None, "fsdp", None),
        P(None, "fsdp", None),
        P(None, "fsdp", None),
        P(None, "fsdp", None),
        P(None, "fsdp", None),
        P(None, "fsdp", None),
        P(None, "fsdp", None),
        P(None, "fsdp", None),
        P(None, "fsdp", None),
        P(None, "fsdp", None),
        P("fsdp", None),
        P("fsdp", None),
        P("fsdp", None),
        P(None, "fsdp"),
        P(None, "fsdp"),
        P(None, "fsdp"),
        P(),
        P(),
        P(),
    )
    return jax.shard_map(body, mesh=mesh, in_specs=in_specs, out_specs=out_specs, check_vma=False)
```

```python
import math

import jax
import jax.numpy as jnp
from jax import lax
from jax.experimental import pallas as pl
from jax.sharding import PartitionSpec as P

D = 768
HEADS = 12
HD = 64
FF = 3072
FREQ = 256
CLASSES = 1000
DIFF_STEPS = 1000
LAYERS = 2
TOK = 256
PD = 16
MODW = 10752


norm_eps = 1e-06
clip_limit = 2.5
learn_rate = 0.01
beta_first = 0.9
beta_second = 0.95
adam_eps = 1e-08
weight_decay = 0.01
first_fix = 1.0 - 0.9**10
second_fix = 1.0 - 0.95**10


def modulate(residual, shift_term, scale_term):
    centred = residual - jnp.mean(residual, axis=-1, keepdims=True)
    spread = jnp.mean(centred * centred, axis=-1, keepdims=True)
    normed = centred * lax.rsqrt(spread + norm_eps)
    return normed * (1.0 + scale_term[:, None, :]) + shift_term[:, None, :]


gelu_rate = math.sqrt(2.0 / math.pi)
gelu_cubic = 0.044715 * gelu_rate


def gelu_tanh(values):
    raised = jnp.tanh(values * (gelu_rate + gelu_cubic * (values * values)))
    return (0.5 * values) * (1.0 + raised)


def gelu_pull(values, grad):
    square = values * values
    raised = jnp.tanh(values * (gelu_rate + gelu_cubic * square))
    slope = (1.0 - raised) * (values * (gelu_rate + 3.0 * gelu_cubic * square))
    return (0.5 * grad) * ((1.0 + raised) * (1.0 + slope))


def product(left_side, right_side):
    return jnp.dot(left_side, right_side, preferred_element_type=jnp.float32)


def left_product(left_side, right_side):
    return lax.dot_general(
        left_side, right_side, (((0,), (0,)), ((), ())), preferred_element_type=jnp.float32
    )


def right_product(left_side, right_side):
    return lax.dot_general(
        left_side, right_side, (((1,), (1,)), ((), ())), preferred_element_type=jnp.float32
    )


def time_features(steps_in):
    half_count = FREQ // 2
    frequencies = jnp.exp(
        -math.log(10000.0) * jnp.arange(half_count, dtype=jnp.float32) / half_count
    )
    angles = steps_in.astype(jnp.float32)[:, None] * frequencies[None, :]
    return jnp.concatenate([jnp.cos(angles), jnp.sin(angles)], axis=1)


def noise_share(steps_in):
    beta_values = jnp.linspace(0.0001, 0.02, DIFF_STEPS, dtype=jnp.float32)
    log_keep = jnp.log(1.0 - beta_values)
    taken = jnp.arange(DIFF_STEPS, dtype=jnp.int32)[None, :] <= steps_in[:, None]
    return jnp.exp(jnp.sum(jnp.where(taken, log_keep[None, :], 0.0), axis=1))


def bias_parts(biases):
    per_layer = 10 * D + FF
    layer_parts = []
    for layer_index in range(LAYERS):
        anchor = layer_index * per_layer
        layer_parts.append(
            (
                biases[anchor : anchor + D],
                biases[anchor + D : anchor + 2 * D],
                biases[anchor + 2 * D : anchor + 3 * D],
                biases[anchor + 3 * D : anchor + 3 * D + FF],
                biases[anchor + 3 * D + FF : anchor + 4 * D + FF],
                biases[anchor + 4 * D + FF : anchor + per_layer],
            )
        )
    anchor = LAYERS * per_layer
    global_parts = (
        biases[anchor : anchor + 2 * D],
        biases[anchor + 2 * D : anchor + 3 * D],
        biases[anchor + 3 * D : anchor + 4 * D],
        biases[anchor + 4 * D : anchor + 5 * D],
        biases[anchor + 5 * D : anchor + 5 * D + PD],
    )
    return (layer_parts, global_parts)


def hop_plan(count):
    if count == 32:
        return [(8, 4), (2, 2), (4, 2), (1, 2)]
    plan = []
    stride = 1
    while stride < count:
        plan.append((stride, 2))
        stride *= 2
    return plan


def shifted(index, stride, size, amount):
    coord = (index // stride) % size
    return index + ((coord + amount) % size - coord) * stride


def send(value, count, stride, size, amount=1):
    pairs = [(index, shifted(index, stride, size, amount)) for index in range(count)]
    return lax.ppermute(value, "fsdp", pairs)


def gather_near(value, count):
    gathered = value[None]
    for stride, size in hop_plan(count):
        pieces = [gathered]
        for unused in range(size - 1):
            pieces.append(send(pieces[-1], count, stride, size))
        gathered = jnp.concatenate(pieces, axis=0)
    return gathered


def near_places(count):
    me = lax.axis_index("fsdp")
    others = jnp.arange(count, dtype=jnp.int32)
    places = jnp.zeros((count,), jnp.int32)
    weight = 1
    for stride, size in hop_plan(count):
        steps = ((me // stride) % size - (others // stride) % size) % size
        places = places + steps * weight
        weight *= size
    return places


def mesh_dims(count):
    if count == 32:
        return (4, 2, 2, 2)
    return (2,) * (count.bit_length() - 1)


def fold(parts, axis, stride, count):
    size = parts[0].shape[axis]
    mine = (lax.axis_index("fsdp") // stride) % size

    def entry(index):
        picked = [lax.dynamic_index_in_dim(part, index, axis, keepdims=False) for part in parts]
        return picked[0] if len(picked) == 1 else jnp.concatenate(picked, axis=-2)

    arrived = [
        send(entry((mine + step) % size), count, stride, size, step) for step in range(1, size)
    ]
    total = entry(mine).astype(jnp.float32)
    for piece in arrived:
        total = total + piece.astype(jnp.float32)
    return total


class ScatterSum:
    def __init__(self, parts, count, swap):
        dims = mesh_dims(count)
        self.count = count
        self.strides = [1]
        for size in reversed(dims[1:]):
            self.strides.insert(0, self.strides[0] * size)
        self.value = [part.reshape(dims + part.shape[1:]) for part in parts]
        self.axes = list(range(len(dims)))
        self.order = list(reversed(self.axes))
        if swap:
            self.order[1], self.order[2] = self.order[2], self.order[1]

    def step(self):
        if not self.order:
            return
        axis = self.order.pop(0)
        place = self.axes.index(axis)
        total = fold(self.value, place, self.strides[axis], self.count)
        self.axes.remove(axis)
        self.value = [total.astype(jnp.bfloat16) if self.order else total]

    def before(self, values):
        self.value[0], values = lax.optimization_barrier((self.value[0], values))
        return values

    def finish(self):
        while self.order:
            self.step()
        return self.value[0]


def sum_all(value, count):
    stride = 1
    while stride < count:
        value = value + send(value, count, stride, 2)
        stride *= 2
    return value


def pair_scores(queries, keys_all, first_half):
    only = jnp.where(first_half, queries, jnp.zeros_like(queries))
    return only, right_product(only, keys_all) * HD ** (-0.5)


def attention_forward_kernel(queries_ref, keys_ref, values_ref, mixed_ref, total_ref):
    lanes = lax.broadcasted_iota(jnp.int32, (TOK, 2 * HD), 1)
    totals = jnp.zeros((TOK, 2 * HD), jnp.float32)
    for pair in range(HEADS // 2):
        span = slice(pair * 2 * HD, (pair + 1) * 2 * HD)
        queries, keys_all, values_all = queries_ref[:, span], keys_ref[:, span], values_ref[:, span]
        halves = []
        for half in range(2):
            mine = (lanes < HD) if half == 0 else (lanes >= HD)
            unused, scores = pair_scores(queries, keys_all, mine)
            row_max = jnp.max(scores, axis=1, keepdims=True)
            raised = jnp.exp(scores - row_max)
            row_sum = jnp.sum(raised, axis=1, keepdims=True)
            soft_low = (raised / row_sum).astype(jnp.bfloat16)
            halves.append(product(soft_low, values_all))
            totals = jnp.where(lanes == 2 * pair + half, row_max + jnp.log(row_sum), totals)
        mixed_ref[:, span] = jnp.where(lanes < HD, halves[0], halves[1]).astype(jnp.bfloat16)
    total_ref[...] = totals


def attention_backward_kernel(
    queries_ref, keys_ref, values_ref, total_ref, grad_ref, dqueries_ref, dkeys_ref, dvalues_ref
):
    lanes = lax.broadcasted_iota(jnp.int32, (TOK, 2 * HD), 1)
    for pair in range(HEADS // 2):
        span = slice(pair * 2 * HD, (pair + 1) * 2 * HD)
        queries, keys_all, values_all = queries_ref[:, span], keys_ref[:, span], values_ref[:, span]
        grads = grad_ref[:, span]
        made = []
        for half in range(2):
            mine = (lanes < HD) if half == 0 else (lanes >= HD)
            unused, scores = pair_scores(queries, keys_all, mine)
            head = 2 * pair + half
            soft_weights = jnp.exp(scores - total_ref[:, head : head + 1])
            grad_values = left_product(soft_weights.astype(jnp.bfloat16), grads)
            grad_soft = right_product(jnp.where(mine, grads, jnp.zeros_like(grads)), values_all)
            spread = jnp.sum(soft_weights * grad_soft, axis=1, keepdims=True)
            score_low = (soft_weights * (grad_soft - spread)).astype(jnp.bfloat16)
            made.append(
                (
                    product(score_low, keys_all) * HD ** (-0.5),
                    left_product(score_low, queries) * HD ** (-0.5),
                    grad_values,
                )
            )
        for part, target in enumerate((dqueries_ref, dkeys_ref, dvalues_ref)):
            target[:, span] = jnp.where(lanes < HD, made[0][part], made[1][part]).astype(
                jnp.bfloat16
            )


def token_block(width):
    return pl.BlockSpec((TOK, width), lambda sample: (sample, 0))


def attention_forward(packed_low, sample_count):
    row_count = sample_count * TOK
    return pl.pallas_call(
        attention_forward_kernel,
        grid=(sample_count,),
        in_specs=[token_block(D)] * 3,
        out_specs=[token_block(D), token_block(2 * HD)],
        out_shape=[
            jax.ShapeDtypeStruct((row_count, D), jnp.bfloat16),
            jax.ShapeDtypeStruct((row_count, 2 * HD), jnp.float32),
        ],
        cost_estimate=pl.CostEstimate(
            flops=8 * 10**9, bytes_accessed=8 * row_count * D, transcendentals=row_count * TOK * HEADS
        ),
        name="attention_forward",
    )(*packed_low)


def attention_backward(packed_low, log_total, grad_mixed_low, sample_count):
    row_count = sample_count * TOK
    return pl.pallas_call(
        attention_backward_kernel,
        grid=(sample_count,),
        in_specs=[token_block(D)] * 3 + [token_block(2 * HD), token_block(D)],
        out_specs=[token_block(D)] * 3,
        out_shape=[jax.ShapeDtypeStruct((row_count, D), jnp.bfloat16)] * 3,
        cost_estimate=pl.CostEstimate(
            flops=20 * 10**9, bytes_accessed=14 * row_count * D, transcendentals=row_count * TOK * HEADS
        ),
        name="attention_backward",
    )(*packed_low, log_total, grad_mixed_low)


def adam_step(weight_now, grad_now, first_old, second_old, factor):
    clipped = grad_now * factor
    first_new = beta_first * first_old + (1.0 - beta_first) * clipped
    second_new = beta_second * second_old + (1.0 - beta_second) * clipped * clipped
    step_size = -learn_rate * (
        first_new / first_fix / (jnp.sqrt(second_new / second_fix) + adam_eps)
        + weight_decay * weight_now
    )
    return (step_size, first_new, second_new)


def body(
    latents,
    noise,
    timesteps,
    labels,
    qkv_weight,
    proj_weight,
    up_weight,
    down_weight,
    mod_weight,
    tables,
    biases,
    qkv_first,
    proj_first,
    up_first,
    down_first,
    mod_first,
    tables_first,
    biases_first,
    qkv_second,
    proj_second,
    up_second,
    down_second,
    mod_second,
    tables_second,
    biases_second,
):
    count = lax.axis_size("fsdp")
    me = lax.axis_index("fsdp")
    local = latents.shape[0]
    samples = local * count
    rows = D // count
    row_count = local * TOK
    total_count = samples * TOK * PD
    low = jnp.bfloat16
    f32 = jnp.float32
    layer_parts, global_parts = bias_parts(biases)
    final_bias, patch_bias, first_bias, second_bias, head_bias = global_parts
    mod_bias = jnp.concatenate([part_item[5] for part_item in layer_parts] + [final_bias])

    attn_pieces, mlp_pieces = [], []
    for layer_index in range(LAYERS):
        pieces = [qkv_weight[layer_index][:, part * D : (part + 1) * D] for part in range(3)]
        attn_pieces.append(pieces + [proj_weight[layer_index]])
        pieces = [up_weight[layer_index][:, part * D : (part + 1) * D] for part in range(4)]
        mlp_pieces.append(pieces + [down_weight[layer_index]])

    def gather(pieces):
        packed = jnp.concatenate(pieces, axis=0).astype(low).reshape(-1, rows, D)
        return lax.all_gather(packed, "fsdp", axis=1, tiled=True)

    early = gather(attn_pieces[0] + mlp_pieces[0] + attn_pieces[1])
    late = gather(mlp_pieces[1])

    mod_low = mod_weight.astype(low)
    mod_columns = lax.all_to_all(mod_low, "fsdp", split_axis=1, concat_axis=0, tiled=True)
    digits = jnp.concatenate([timesteps // 32, timesteps % 32, labels // 32, labels % 32]).astype(low)
    table_low = tables.astype(low).T
    room = -(-CLASSES // 128) * 128
    first_at, class_at, patch_at = D, D + FREQ, D + FREQ + room
    head_at, digit_at = patch_at + PD, patch_at + 2 * PD
    tables_low = jnp.concatenate(
        [
            table_low[:, PD + FREQ : PD + FREQ + D],
            table_low[:, PD : PD + FREQ],
            table_low[:, PD + FREQ + D : PD + FREQ + D + CLASSES],
            jnp.zeros((rows, room - CLASSES), low),
            table_low[:, :PD],
            table_low[:, PD + FREQ + D + CLASSES :],
            jnp.broadcast_to(digits[None, :], (rows, 4 * local)),
        ],
        axis=1,
    )
    tables_near = gather_near(tables_low, count)
    places = near_places(count)
    tables_far = jnp.take(tables_near, places, axis=0, mode="clip")
    tables_full = tables_far.reshape(D, digit_at + 4 * local)

    numbers = tables_far[:, 0, digit_at:].astype(jnp.int32).reshape(count, 4, local)
    steps_all = (numbers[:, 0] * 32 + numbers[:, 1]).reshape(samples)
    labels_all = (numbers[:, 2] * 32 + numbers[:, 3]).reshape(samples)
    features_low = time_features(steps_all).astype(low)
    first_pre = right_product(features_low, tables_full[:, first_at:class_at]) + first_bias
    first_low = jax.nn.silu(first_pre).astype(low)
    class_rows = (labels_all[:, None] == jnp.arange(room, dtype=jnp.int32)[None, :]).astype(low)
    condition = (
        right_product(first_low, tables_full[:, :D])
        + second_bias
        + right_product(class_rows, tables_full[:, class_at:patch_at])
    )
    cond_low = jax.nn.silu(condition).astype(low)
    mods_columns = product(cond_low, mod_columns)
    modulations = (
        lax.all_to_all(mods_columns, "fsdp", split_axis=0, concat_axis=1, tiled=True) + mod_bias
    )

    keep_share = noise_share(timesteps)
    noised = (
        jnp.sqrt(keep_share)[:, None, None] * latents
        + jnp.sqrt(1.0 - keep_share)[:, None, None] * noise
    )
    noised_low = noised.reshape(row_count, PD).astype(low)
    patch_columns = tables_full[:, patch_at:head_at]
    head_columns = tables_full[:, head_at:digit_at]
    residual = (right_product(noised_low, patch_columns) + patch_bias).reshape(local, TOK, D)

    def weights_of_attn(layer_index):
        whole = attn_whole[layer_index]
        return [whole[part] for part in range(3)], whole[3]

    def weights_of_mlp(layer_index):
        whole = mlp_whole[layer_index]
        up_full = jnp.concatenate([whole[part] for part in range(4)], axis=1)
        down_full = whole[4:].reshape(4, count, rows, D).transpose(1, 0, 2, 3).reshape(FF, D)
        return up_full, down_full

    stored = []
    for layer_index in range(LAYERS):
        if layer_index == 0:
            early, residual = lax.optimization_barrier((early, residual))
            attn_whole = [early[:4], early[12:]]
            mlp_whole = [early[4:12], late]
        qkv_full, proj_full = weights_of_attn(layer_index)
        query_bias, value_bias, proj_bias, up_bias, down_bias, unused = layer_parts[layer_index]
        segment = modulations[:, layer_index * 6 * D : (layer_index + 1) * 6 * D]
        mod_terms = [segment[:, part_index * D : (part_index + 1) * D] for part_index in range(6)]
        shift_attn, scale_attn, gate_attn, shift_mlp, scale_mlp, gate_mlp = mod_terms
        residual_in = residual
        hidden_low = modulate(residual_in, shift_attn, scale_attn).reshape(row_count, D).astype(low)
        packed_low = [
            (product(hidden_low, qkv_full[0]) + query_bias).astype(low),
            product(hidden_low, qkv_full[1]).astype(low),
            (product(hidden_low, qkv_full[2]) + value_bias).astype(low),
        ]
        mixed, log_total = attention_forward(packed_low, local)
        mixed_low = mixed.astype(low)
        attn_out = (product(mixed_low, proj_full) + proj_bias).reshape(local, TOK, D)
        residual_mid = residual_in + gate_attn[:, None, :] * attn_out
        if layer_index == 1:
            mlp_whole[1], residual_mid = lax.optimization_barrier((mlp_whole[1], residual_mid))
        up_full, down_full = weights_of_mlp(layer_index)
        hidden_two_low = modulate(residual_mid, shift_mlp, scale_mlp).reshape(row_count, D).astype(low)
        pre_act = product(hidden_two_low, up_full) + up_bias
        act_low = lax.optimization_barrier(gelu_tanh(pre_act).astype(low))
        mlp_out = (product(act_low, down_full) + down_bias).reshape(local, TOK, D)
        residual = residual_mid + gate_mlp[:, None, :] * mlp_out
        stored.append(
            (
                residual_in,
                hidden_low,
                packed_low,
                log_total,
                mixed_low,
                attn_out,
                residual_mid,
                hidden_two_low,
                pre_act,
                act_low,
                mlp_out,
            )
        )
    final_mods = modulations[:, LAYERS * 6 * D :]
    final_hidden = modulate(residual, final_mods[:, :D], final_mods[:, D:])
    final_low = final_hidden.reshape(row_count, D).astype(low)
    predicted = product(final_low, head_columns) + head_bias
    errors = predicted - noise.reshape(row_count, PD)
    loss_local = jnp.sum(errors * errors) / total_count
    grad_pred_low = (2.0 * errors / total_count).astype(low)
    grad_head_bias = jnp.sum(grad_pred_low.astype(f32), axis=0)
    grad_head = left_product(grad_pred_low, final_low)
    grad_final = right_product(grad_pred_low, head_columns).reshape(local, TOK, D)
    unused, final_pull = jax.vjp(modulate, residual, final_mods[:, :D], final_mods[:, D:])
    grad_residual, grad_shift_final, grad_scale_final = final_pull(grad_final)
    mod_grads = [None] * LAYERS
    attn_sums = [None] * LAYERS
    mlp_shards = [None] * LAYERS
    shards = [None] * LAYERS
    bias_pieces = [None] * LAYERS
    for layer_index in reversed(range(LAYERS)):
        qkv_full, proj_full = weights_of_attn(layer_index)
        up_full, down_full = weights_of_mlp(layer_index)
        (
            residual_in,
            hidden_low,
            packed_low,
            log_total,
            mixed_low,
            attn_out,
            residual_mid,
            hidden_two_low,
            pre_act,
            act_low,
            mlp_out,
        ) = stored[layer_index]
        segment = modulations[:, layer_index * 6 * D : (layer_index + 1) * 6 * D]
        mod_terms = [segment[:, part_index * D : (part_index + 1) * D] for part_index in range(6)]
        shift_attn, scale_attn, gate_attn, shift_mlp, scale_mlp, gate_mlp = mod_terms
        grad_gate_mlp = jnp.sum(grad_residual * mlp_out, axis=1)
        grad_mlp_low = (grad_residual * gate_mlp[:, None, :]).reshape(row_count, D).astype(low)
        grad_down_bias = jnp.sum(grad_mlp_low.astype(f32), axis=0)
        grad_down = left_product(act_low, grad_mlp_low)
        grad_act = right_product(grad_mlp_low, down_full)
        grad_pre_low = gelu_pull(pre_act, grad_act).astype(low)
        grad_up_bias = jnp.sum(grad_pre_low.astype(f32), axis=0)
        grad_up = left_product(hidden_two_low, grad_pre_low)
        grad_hidden_two = right_product(grad_pre_low, up_full).reshape(local, TOK, D)
        unused, mlp_pull = jax.vjp(modulate, residual_mid, shift_mlp, scale_mlp)
        part_residual, grad_shift_mlp, grad_scale_mlp = mlp_pull(grad_hidden_two)
        grad_residual = grad_residual + part_residual
        grad_gate_attn = jnp.sum(grad_residual * attn_out, axis=1)
        grad_attn_low = (grad_residual * gate_attn[:, None, :]).reshape(row_count, D).astype(low)
        grad_proj_bias = jnp.sum(grad_attn_low.astype(f32), axis=0)
        grad_proj = left_product(mixed_low, grad_attn_low)
        grad_mixed_low = right_product(grad_attn_low, proj_full).astype(low)
        sent_mlp = [
            grad_up[:, part * D : (part + 1) * D].astype(low).reshape(count, rows, D)
            for part in range(4)
        ]
        sent_mlp.append(grad_down.astype(low).reshape(count, 4 * rows, D))
        sent_mlp = jnp.concatenate(sent_mlp, axis=1).reshape(count * 8 * rows, D)
        sent_mlp, grad_mixed_low = lax.optimization_barrier((sent_mlp, grad_mixed_low))
        mlp_shards[layer_index] = lax.psum_scatter(
            sent_mlp, "fsdp", scatter_dimension=0, tiled=True
        ).astype(f32)
        grad_packed_low = attention_backward(packed_low, log_total, grad_mixed_low, local)
        if layer_index + 1 < LAYERS:
            grad_packed_low = attn_sums[layer_index + 1].before(grad_packed_low)
            attn_sums[layer_index + 1].step()
        grad_query_bias = jnp.sum(grad_packed_low[0].astype(f32), axis=0)
        grad_value_bias = jnp.sum(grad_packed_low[2].astype(f32), axis=0)
        grad_qkv = [left_product(hidden_low, item) for item in grad_packed_low]
        grad_hidden = (
            right_product(grad_packed_low[0], qkv_full[0])
            + right_product(grad_packed_low[1], qkv_full[1])
            + right_product(grad_packed_low[2], qkv_full[2])
        ).reshape(local, TOK, D)
        unused, attn_pull = jax.vjp(modulate, residual_in, shift_attn, scale_attn)
        part_residual, grad_shift_attn, grad_scale_attn = attn_pull(grad_hidden)
        grad_residual = grad_residual + part_residual
        mod_grads[layer_index] = jnp.concatenate(
            [
                grad_shift_attn,
                grad_scale_attn,
                grad_gate_attn,
                grad_shift_mlp,
                grad_scale_mlp,
                grad_gate_mlp,
            ],
            axis=1,
        )
        sent = [item.astype(low).reshape(count, rows, D) for item in grad_qkv + [grad_proj]]
        attn_sums[layer_index] = ScatterSum(sent, count, layer_index % 2 == 0)
        attn_sums[layer_index].step()
        if layer_index + 1 < LAYERS:
            grad_residual, mod_grads[layer_index] = attn_sums[layer_index + 1].before(
                (grad_residual, mod_grads[layer_index])
            )
            attn_sums[layer_index + 1].step()
        (grad_residual, mod_grads[layer_index]) = attn_sums[layer_index].before(
            (grad_residual, mod_grads[layer_index])
        )
        attn_sums[layer_index].step()
        bias_pieces[layer_index] = [
            grad_query_bias,
            grad_value_bias,
            grad_proj_bias,
            grad_up_bias,
            grad_down_bias,
        ]
    grad_zero_low = grad_residual.reshape(row_count, D).astype(low)
    grad_patch_bias = jnp.sum(grad_zero_low.astype(f32), axis=0)
    grad_patch = left_product(noised_low, grad_zero_low)

    grad_mods_low = jnp.concatenate(
        mod_grads + [grad_shift_final, grad_scale_final], axis=1
    ).astype(low)
    grad_mods_columns = lax.all_to_all(
        grad_mods_low, "fsdp", split_axis=1, concat_axis=0, tiled=True
    )
    grad_mods_columns = attn_sums[0].before(grad_mods_columns)
    attn_sums[0].step()
    grad_act_sent = right_product(mod_columns, grad_mods_columns).astype(low)
    own_mod_bias = jnp.sum(grad_mods_low.astype(f32), axis=0)
    pieces = []
    for layer_index in range(LAYERS):
        pieces += bias_pieces[layer_index]
        pieces.append(own_mod_bias[layer_index * 6 * D : (layer_index + 1) * 6 * D])
    pieces += [
        own_mod_bias[LAYERS * 6 * D :],
        grad_patch_bias,
        grad_head_bias,
    ]
    pieces += [grad_patch.reshape(-1), grad_head.reshape(-1)]
    pieces, grad_act_sent = lax.optimization_barrier((pieces, grad_act_sent))
    grad_act = lax.all_to_all(
        grad_act_sent,
        "fsdp",
        split_axis=0,
        concat_axis=0,
        tiled=True,
    )
    grad_act = jnp.sum(grad_act.reshape(count, rows, samples).astype(f32), axis=0)
    grad_act = attn_sums[0].before(grad_act)
    attn_sums[0].step()
    grad_act_sent, grad_mods_later = lax.optimization_barrier((grad_act_sent, grad_mods_columns))
    shard_mod = lax.all_to_all(
        left_product(cond_low, grad_mods_later).astype(low),
        "fsdp",
        split_axis=0,
        concat_axis=1,
        tiled=True,
    ).astype(f32)
    own_bias = lax.dynamic_slice(second_bias, (me * rows,), (rows,))
    condition_own = (
        right_product(tables_low[:, :D], first_low)
        + own_bias[:, None]
        + right_product(tables_low[:, class_at:patch_at], class_rows)
    )
    unused, silu_pull = jax.vjp(jax.nn.silu, condition_own)
    grad_condition = silu_pull(grad_act)[0]
    grad_class = lax.dot_general(
        grad_condition,
        class_rows.astype(f32),
        (((1,), (0,)), ((), ())),
        precision=lax.Precision.HIGHEST,
        preferred_element_type=f32,
    )[:, :CLASSES]
    grad_time_low = grad_condition.astype(low)
    grad_second_bias = jnp.sum(grad_time_low.astype(f32), axis=1)
    grad_second = product(grad_time_low, first_low)
    grad_time_sent, shard_mod = lax.optimization_barrier((grad_time_low, shard_mod))
    grad_time_all = lax.all_to_all(
        jnp.broadcast_to(grad_time_sent[None], (count, rows, samples)).reshape(D, samples),
        "fsdp",
        split_axis=0,
        concat_axis=0,
        tiled=True,
    )
    grad_first_act = lax.dynamic_slice(
        left_product(tables_full[:, :D], grad_time_all), (me * rows, 0), (rows, samples)
    )
    own_bias = lax.dynamic_slice(first_bias, (me * rows,), (rows,))
    first_pre_own = right_product(tables_low[:, first_at:class_at], features_low) + own_bias[:, None]
    unused, first_pull = jax.vjp(jax.nn.silu, first_pre_own)
    grad_first_low = first_pull(grad_first_act)[0].astype(low)
    grad_first_bias = jnp.sum(grad_first_low.astype(f32), axis=1)
    grad_first = product(grad_first_low, features_low)
    grad_middle = jnp.concatenate([grad_first, grad_second, grad_class], axis=1).T

    def spread(piece, length):
        return lax.dynamic_update_slice(jnp.zeros((length,), f32), piece, (me * piece.shape[0],))

    summed = sum_all(jnp.concatenate(pieces), count)
    bias_length = biases.shape[0] - 2 * D
    ends = summed[bias_length:].reshape(2 * PD, D)
    own_ends = lax.dynamic_slice(ends, (0, me * rows), (2 * PD, rows))
    shard_tables = jnp.concatenate([own_ends[:PD], grad_middle, own_ends[PD:]], axis=0)
    for layer_index in range(LAYERS):
        shard = mlp_shards[layer_index]
        parts = [attn_sums[layer_index].finish()[part * rows : (part + 1) * rows] for part in range(4)]
        parts += [shard[part * rows : (part + 1) * rows] for part in range(4)]
        shards[layer_index] = (
            jnp.concatenate(parts[:3], axis=1),
            parts[3],
            jnp.concatenate(parts[4:], axis=1),
            shard[4 * rows :],
        )
    shard_squares = jnp.sum(shard_mod * shard_mod) + jnp.sum(shard_tables * shard_tables)
    for layer_index in range(LAYERS):
        for item in shards[layer_index]:
            shard_squares = shard_squares + jnp.sum(item * item)
    last_sums = sum_all(
        jnp.concatenate(
            [
                spread(grad_first_bias, D),
                spread(grad_second_bias, D),
                shard_squares[None],
                loss_local[None],
            ]
        ),
        count,
    )
    square_total, loss_value = last_sums[2 * D], last_sums[2 * D + 1]
    bias_grad = jnp.concatenate(
        [summed[: bias_length - PD], last_sums[: 2 * D], summed[bias_length - PD : bias_length]]
    )
    grad_norm = jnp.sqrt(square_total + jnp.sum(bias_grad * bias_grad))
    factor = jnp.minimum(1.0, clip_limit / (grad_norm + 1e-06))
    shard_qkv, shard_proj, shard_up, shard_down = [
        jnp.stack([shards[layer_index][part] for layer_index in range(LAYERS)]) for part in range(4)
    ]
    qkv_update, qkv_first_new, qkv_second_new = adam_step(
        qkv_weight, shard_qkv, qkv_first, qkv_second, factor
    )
    proj_update, proj_first_new, proj_second_new = adam_step(
        proj_weight, shard_proj, proj_first, proj_second, factor
    )
    up_update, up_first_new, up_second_new = adam_step(
        up_weight, shard_up, up_first, up_second, factor
    )
    down_update, down_first_new, down_second_new = adam_step(
        down_weight, shard_down, down_first, down_second, factor
    )
    mod_update, mod_first_new, mod_second_new = adam_step(
        mod_weight, shard_mod, mod_first, mod_second, factor
    )
    tables_update, tables_first_new, tables_second_new = adam_step(
        tables, shard_tables, tables_first, tables_second, factor
    )
    biases_update, biases_first_new, biases_second_new = adam_step(
        biases, bias_grad, biases_first, biases_second, factor
    )
    return (
        loss_value,
        grad_norm,
        qkv_update,
        qkv_first_new,
        qkv_second_new,
        proj_update,
        proj_first_new,
        proj_second_new,
        up_update,
        up_first_new,
        up_second_new,
        down_update,
        down_first_new,
        down_second_new,
        mod_update,
        mod_first_new,
        mod_second_new,
        tables_update,
        tables_first_new,
        tables_second_new,
        biases_update,
        biases_first_new,
        biases_second_new,
    )


def solution(mesh):
    in_specs = (
        P("fsdp", None, None),
        P("fsdp", None, None),
        P("fsdp"),
        P("fsdp"),
        P(None, "fsdp", None),
        P(None, "fsdp", None),
        P(None, "fsdp", None),
        P(None, "fsdp", None),
        P("fsdp", None),
        P(None, "fsdp"),
        P(),
        P(None, "fsdp", None),
        P(None, "fsdp", None),
        P(None, "fsdp", None),
        P(None, "fsdp", None),
        P("fsdp", None),
        P(None, "fsdp"),
        P(),
        P(None, "fsdp", None),
        P(None, "fsdp", None),
        P(None, "fsdp", None),
        P(None, "fsdp", None),
        P("fsdp", None),
        P(None, "fsdp"),
        P(),
    )
    out_specs = (
        P(),
        P(),
        P(None, "fsdp", None),
        P(None, "fsdp", None),
        P(None, "fsdp", None),
        P(None, "fsdp", None),
        P(None, "fsdp", None),
        P(None, "fsdp", None),
        P(None, "fsdp", None),
        P(None, "fsdp", None),
        P(None, "fsdp", None),
        P(None, "fsdp", None),
        P(None, "fsdp", None),
        P(None, "fsdp", None),
        P("fsdp", None),
        P("fsdp", None),
        P("fsdp", None),
        P(None, "fsdp"),
        P(None, "fsdp"),
        P(None, "fsdp"),
        P(),
        P(),
        P(),
    )
    return jax.shard_map(body, mesh=mesh, in_specs=in_specs, out_specs=out_specs, check_vma=False)
```

```python
import math

import jax
import jax.numpy as jnp
from jax import lax
from jax.experimental import pallas as pl
from jax.sharding import PartitionSpec as P

D = 768
HEADS = 12
HD = 64
FF = 3072
FREQ = 256
CLASSES = 1000
DIFF_STEPS = 1000
LAYERS = 2
TOK = 256
PD = 16
MODW = 10752


norm_eps = 1e-06
clip_limit = 2.5
learn_rate = 0.01
beta_first = 0.9
beta_second = 0.95
adam_eps = 1e-08
weight_decay = 0.01
first_fix = 1.0 - 0.9**10
second_fix = 1.0 - 0.95**10


def modulate(residual, shift_term, scale_term):
    centred = residual - jnp.mean(residual, axis=-1, keepdims=True)
    spread = jnp.mean(centred * centred, axis=-1, keepdims=True)
    normed = centred * lax.rsqrt(spread + norm_eps)
    return normed * (1.0 + scale_term[:, None, :]) + shift_term[:, None, :]


gelu_rate = math.sqrt(2.0 / math.pi)
gelu_cubic = 0.044715 * gelu_rate


def gelu_tanh(values):
    raised = jnp.tanh(values * (gelu_rate + gelu_cubic * (values * values)))
    return (0.5 * values) * (1.0 + raised)


def gelu_pull(values, grad):
    square = values * values
    raised = jnp.tanh(values * (gelu_rate + gelu_cubic * square))
    slope = (1.0 - raised) * (values * (gelu_rate + 3.0 * gelu_cubic * square))
    return (0.5 * grad) * ((1.0 + raised) * (1.0 + slope))


def product(left_side, right_side):
    return jnp.dot(left_side, right_side, preferred_element_type=jnp.float32)


def left_product(left_side, right_side):
    return lax.dot_general(
        left_side, right_side, (((0,), (0,)), ((), ())), preferred_element_type=jnp.float32
    )


def right_product(left_side, right_side):
    return lax.dot_general(
        left_side, right_side, (((1,), (1,)), ((), ())), preferred_element_type=jnp.float32
    )


def time_features(steps_in):
    half_count = FREQ // 2
    frequencies = jnp.exp(
        -math.log(10000.0) * jnp.arange(half_count, dtype=jnp.float32) / half_count
    )
    angles = steps_in.astype(jnp.float32)[:, None] * frequencies[None, :]
    return jnp.concatenate([jnp.cos(angles), jnp.sin(angles)], axis=1)


def noise_share(steps_in):
    beta_values = jnp.linspace(0.0001, 0.02, DIFF_STEPS, dtype=jnp.float32)
    log_keep = jnp.log(1.0 - beta_values)
    taken = jnp.arange(DIFF_STEPS, dtype=jnp.int32)[None, :] <= steps_in[:, None]
    return jnp.exp(jnp.sum(jnp.where(taken, log_keep[None, :], 0.0), axis=1))


def bias_parts(biases):
    per_layer = 10 * D + FF
    layer_parts = []
    for layer_index in range(LAYERS):
        anchor = layer_index * per_layer
        layer_parts.append(
            (
                biases[anchor : anchor + D],
                biases[anchor + D : anchor + 2 * D],
                biases[anchor + 2 * D : anchor + 3 * D],
                biases[anchor + 3 * D : anchor + 3 * D + FF],
                biases[anchor + 3 * D + FF : anchor + 4 * D + FF],
                biases[anchor + 4 * D + FF : anchor + per_layer],
            )
        )
    anchor = LAYERS * per_layer
    global_parts = (
        biases[anchor : anchor + 2 * D],
        biases[anchor + 2 * D : anchor + 3 * D],
        biases[anchor + 3 * D : anchor + 4 * D],
        biases[anchor + 4 * D : anchor + 5 * D],
        biases[anchor + 5 * D : anchor + 5 * D + PD],
    )
    return (layer_parts, global_parts)


def hop_plan(count):
    if count == 32:
        return [(8, 4), (2, 2), (4, 2), (1, 2)]
    plan = []
    stride = 1
    while stride < count:
        plan.append((stride, 2))
        stride *= 2
    return plan


def shifted(index, stride, size, amount):
    coord = (index // stride) % size
    return index + ((coord + amount) % size - coord) * stride


def send(value, count, stride, size, amount=1):
    pairs = [(index, shifted(index, stride, size, amount)) for index in range(count)]
    return lax.ppermute(value, "fsdp", pairs)


def gather_near(value, count):
    gathered = value[None]
    for stride, size in hop_plan(count):
        pieces = [gathered]
        for unused in range(size - 1):
            pieces.append(send(pieces[-1], count, stride, size))
        gathered = jnp.concatenate(pieces, axis=0)
    return gathered


def near_places(count):
    me = lax.axis_index("fsdp")
    others = jnp.arange(count, dtype=jnp.int32)
    places = jnp.zeros((count,), jnp.int32)
    weight = 1
    for stride, size in hop_plan(count):
        steps = ((me // stride) % size - (others // stride) % size) % size
        places = places + steps * weight
        weight *= size
    return places


def mesh_dims(count):
    if count == 32:
        return (4, 2, 2, 2)
    return (2,) * (count.bit_length() - 1)


def fold(parts, axis, stride, count):
    size = parts[0].shape[axis]
    mine = (lax.axis_index("fsdp") // stride) % size

    def entry(index):
        picked = [lax.dynamic_index_in_dim(part, index, axis, keepdims=False) for part in parts]
        return picked[0] if len(picked) == 1 else jnp.concatenate(picked, axis=-2)

    arrived = [
        send(entry((mine + step) % size), count, stride, size, step) for step in range(1, size)
    ]
    total = entry(mine).astype(jnp.float32)
    for piece in arrived:
        total = total + piece.astype(jnp.float32)
    return total


class ScatterSum:
    def __init__(self, parts, count, swap):
        dims = mesh_dims(count)
        self.count = count
        self.strides = [1]
        for size in reversed(dims[1:]):
            self.strides.insert(0, self.strides[0] * size)
        self.value = [part.reshape(dims + part.shape[1:]) for part in parts]
        self.axes = list(range(len(dims)))
        self.order = list(reversed(self.axes))
        if swap:
            self.order[1], self.order[2] = self.order[2], self.order[1]

    def step(self):
        if not self.order:
            return
        axis = self.order.pop(0)
        place = self.axes.index(axis)
        total = fold(self.value, place, self.strides[axis], self.count)
        self.axes.remove(axis)
        self.value = [total.astype(jnp.bfloat16) if self.order else total]

    def before(self, values):
        self.value[0], values = lax.optimization_barrier((self.value[0], values))
        return values

    def finish(self):
        while self.order:
            self.step()
        return self.value[0]


def sum_all(value, count):
    stride = 1
    while stride < count:
        value = value + send(value, count, stride, 2)
        stride *= 2
    return value


def pair_scores(queries, keys_all, first_half):
    only = jnp.where(first_half, queries, jnp.zeros_like(queries))
    return only, right_product(only, keys_all) * HD ** (-0.5)


def attention_forward_kernel(queries_ref, keys_ref, values_ref, mixed_ref, total_ref):
    lanes = lax.broadcasted_iota(jnp.int32, (TOK, 2 * HD), 1)
    totals = jnp.zeros((TOK, 2 * HD), jnp.float32)
    for pair in range(HEADS // 2):
        span = slice(pair * 2 * HD, (pair + 1) * 2 * HD)
        queries, keys_all, values_all = queries_ref[:, span], keys_ref[:, span], values_ref[:, span]
        halves = []
        for half in range(2):
            mine = (lanes < HD) if half == 0 else (lanes >= HD)
            unused, scores = pair_scores(queries, keys_all, mine)
            row_max = jnp.max(scores, axis=1, keepdims=True)
            raised = jnp.exp(scores - row_max)
            row_sum = jnp.sum(raised, axis=1, keepdims=True)
            soft_low = (raised / row_sum).astype(jnp.bfloat16)
            halves.append(product(soft_low, values_all))
            totals = jnp.where(lanes == 2 * pair + half, row_max + jnp.log(row_sum), totals)
        mixed_ref[:, span] = jnp.where(lanes < HD, halves[0], halves[1]).astype(jnp.bfloat16)
    total_ref[...] = totals


def attention_backward_kernel(
    queries_ref, keys_ref, values_ref, total_ref, grad_ref, dqueries_ref, dkeys_ref, dvalues_ref
):
    lanes = lax.broadcasted_iota(jnp.int32, (TOK, 2 * HD), 1)
    for pair in range(HEADS // 2):
        span = slice(pair * 2 * HD, (pair + 1) * 2 * HD)
        queries, keys_all, values_all = queries_ref[:, span], keys_ref[:, span], values_ref[:, span]
        grads = grad_ref[:, span]
        made = []
        for half in range(2):
            mine = (lanes < HD) if half == 0 else (lanes >= HD)
            unused, scores = pair_scores(queries, keys_all, mine)
            head = 2 * pair + half
            soft_weights = jnp.exp(scores - total_ref[:, head : head + 1])
            grad_values = left_product(soft_weights.astype(jnp.bfloat16), grads)
            grad_soft = right_product(jnp.where(mine, grads, jnp.zeros_like(grads)), values_all)
            spread = jnp.sum(soft_weights * grad_soft, axis=1, keepdims=True)
            score_low = (soft_weights * (grad_soft - spread)).astype(jnp.bfloat16)
            made.append(
                (
                    product(score_low, keys_all) * HD ** (-0.5),
                    left_product(score_low, queries) * HD ** (-0.5),
                    grad_values,
                )
            )
        for part, target in enumerate((dqueries_ref, dkeys_ref, dvalues_ref)):
            target[:, span] = jnp.where(lanes < HD, made[0][part], made[1][part]).astype(
                jnp.bfloat16
            )


def token_block(width):
    return pl.BlockSpec((TOK, width), lambda sample: (sample, 0))


def attention_forward(packed_low, sample_count):
    row_count = sample_count * TOK
    return pl.pallas_call(
        attention_forward_kernel,
        grid=(sample_count,),
        in_specs=[token_block(D)] * 3,
        out_specs=[token_block(D), token_block(2 * HD)],
        out_shape=[
            jax.ShapeDtypeStruct((row_count, D), jnp.bfloat16),
            jax.ShapeDtypeStruct((row_count, 2 * HD), jnp.float32),
        ],
        cost_estimate=pl.CostEstimate(
            flops=8 * 10**9, bytes_accessed=8 * row_count * D, transcendentals=row_count * TOK * HEADS
        ),
        name="attention_forward",
    )(*packed_low)


def attention_backward(packed_low, log_total, grad_mixed_low, sample_count):
    row_count = sample_count * TOK
    return pl.pallas_call(
        attention_backward_kernel,
        grid=(sample_count,),
        in_specs=[token_block(D)] * 3 + [token_block(2 * HD), token_block(D)],
        out_specs=[token_block(D)] * 3,
        out_shape=[jax.ShapeDtypeStruct((row_count, D), jnp.bfloat16)] * 3,
        cost_estimate=pl.CostEstimate(
            flops=20 * 10**9, bytes_accessed=14 * row_count * D, transcendentals=row_count * TOK * HEADS
        ),
        name="attention_backward",
    )(*packed_low, log_total, grad_mixed_low)


def adam_step(weight_now, grad_now, first_old, second_old, factor):
    clipped = grad_now * factor
    first_new = beta_first * first_old + (1.0 - beta_first) * clipped
    second_new = beta_second * second_old + (1.0 - beta_second) * clipped * clipped
    step_size = -learn_rate * (
        first_new / first_fix / (jnp.sqrt(second_new / second_fix) + adam_eps)
        + weight_decay * weight_now
    )
    return (step_size, first_new, second_new)


def body(
    latents,
    noise,
    timesteps,
    labels,
    qkv_weight,
    proj_weight,
    up_weight,
    down_weight,
    mod_weight,
    tables,
    biases,
    qkv_first,
    proj_first,
    up_first,
    down_first,
    mod_first,
    tables_first,
    biases_first,
    qkv_second,
    proj_second,
    up_second,
    down_second,
    mod_second,
    tables_second,
    biases_second,
):
    count = lax.axis_size("fsdp")
    me = lax.axis_index("fsdp")
    local = latents.shape[0]
    samples = local * count
    rows = D // count
    row_count = local * TOK
    total_count = samples * TOK * PD
    low = jnp.bfloat16
    f32 = jnp.float32
    layer_parts, global_parts = bias_parts(biases)
    final_bias, patch_bias, first_bias, second_bias, head_bias = global_parts
    mod_bias = jnp.concatenate([part_item[5] for part_item in layer_parts] + [final_bias])

    attn_pieces, mlp_pieces = [], []
    for layer_index in range(LAYERS):
        pieces = [qkv_weight[layer_index][:, part * D : (part + 1) * D] for part in range(3)]
        attn_pieces.append(pieces + [proj_weight[layer_index]])
        pieces = [up_weight[layer_index][:, part * D : (part + 1) * D] for part in range(4)]
        mlp_pieces.append(pieces + [down_weight[layer_index]])

    def gather(pieces):
        packed = jnp.concatenate(pieces, axis=0).astype(low).reshape(-1, rows, D)
        return lax.all_gather(packed, "fsdp", axis=1, tiled=True)

    early = gather(attn_pieces[0] + mlp_pieces[0] + attn_pieces[1])
    late = gather(mlp_pieces[1])

    mod_low = mod_weight.astype(low)
    mod_columns = lax.all_to_all(mod_low, "fsdp", split_axis=1, concat_axis=0, tiled=True)
    digits = jnp.concatenate([timesteps // 32, timesteps % 32, labels // 32, labels % 32]).astype(low)
    table_low = tables.astype(low).T
    room = -(-CLASSES // 128) * 128
    first_at, class_at, patch_at = D, D + FREQ, D + FREQ + room
    head_at, digit_at = patch_at + PD, patch_at + 2 * PD
    tables_low = jnp.concatenate(
        [
            table_low[:, PD + FREQ : PD + FREQ + D],
            table_low[:, PD : PD + FREQ],
            table_low[:, PD + FREQ + D : PD + FREQ + D + CLASSES],
            jnp.zeros((rows, room - CLASSES), low),
            table_low[:, :PD],
            table_low[:, PD + FREQ + D + CLASSES :],
            jnp.broadcast_to(digits[None, :], (rows, 4 * local)),
        ],
        axis=1,
    )
    tables_near = gather_near(tables_low, count)
    places = near_places(count)
    tables_far = jnp.take(tables_near, places, axis=0, mode="clip")
    tables_full = tables_far.reshape(D, digit_at + 4 * local)

    numbers = tables_far[:, 0, digit_at:].astype(jnp.int32).reshape(count, 4, local)
    steps_all = (numbers[:, 0] * 32 + numbers[:, 1]).reshape(samples)
    labels_all = (numbers[:, 2] * 32 + numbers[:, 3]).reshape(samples)
    features_low = time_features(steps_all).astype(low)
    first_pre = right_product(features_low, tables_full[:, first_at:class_at]) + first_bias
    first_low = jax.nn.silu(first_pre).astype(low)
    class_rows = (labels_all[:, None] == jnp.arange(room, dtype=jnp.int32)[None, :]).astype(low)
    condition = (
        right_product(first_low, tables_full[:, :D])
        + second_bias
        + right_product(class_rows, tables_full[:, class_at:patch_at])
    )
    cond_low = jax.nn.silu(condition).astype(low)
    mods_columns = product(cond_low, mod_columns)
    modulations = (
        lax.all_to_all(mods_columns, "fsdp", split_axis=0, concat_axis=1, tiled=True) + mod_bias
    )

    keep_share = noise_share(timesteps)
    noised = (
        jnp.sqrt(keep_share)[:, None, None] * latents
        + jnp.sqrt(1.0 - keep_share)[:, None, None] * noise
    )
    noised_low = noised.reshape(row_count, PD).astype(low)
    patch_columns = tables_full[:, patch_at:head_at]
    head_columns = tables_full[:, head_at:digit_at]
    residual = (right_product(noised_low, patch_columns) + patch_bias).reshape(local, TOK, D)

    def weights_of_attn(layer_index):
        whole = attn_whole[layer_index]
        return [whole[part] for part in range(3)], whole[3]

    def weights_of_mlp(layer_index):
        whole = mlp_whole[layer_index]
        up_full = whole[:4].transpose(1, 0, 2).reshape(D, FF)
        down_full = whole[4:].reshape(4, count, rows, D).transpose(1, 0, 2, 3).reshape(FF, D)
        return lax.optimization_barrier((up_full, down_full))

    mlp_weights = []
    stored = []
    for layer_index in range(LAYERS):
        if layer_index == 0:
            early, residual = lax.optimization_barrier((early, residual))
            attn_whole = [early[:4], early[12:]]
            mlp_whole = [early[4:12], late]
        qkv_full, proj_full = weights_of_attn(layer_index)
        query_bias, value_bias, proj_bias, up_bias, down_bias, unused = layer_parts[layer_index]
        segment = modulations[:, layer_index * 6 * D : (layer_index + 1) * 6 * D]
        mod_terms = [segment[:, part_index * D : (part_index + 1) * D] for part_index in range(6)]
        shift_attn, scale_attn, gate_attn, shift_mlp, scale_mlp, gate_mlp = mod_terms
        residual_in = residual
        hidden_low = modulate(residual_in, shift_attn, scale_attn).reshape(row_count, D).astype(low)
        packed_low = [
            (product(hidden_low, qkv_full[0]) + query_bias).astype(low),
            product(hidden_low, qkv_full[1]).astype(low),
            (product(hidden_low, qkv_full[2]) + value_bias).astype(low),
        ]
        mixed, log_total = attention_forward(packed_low, local)
        mixed_low = mixed.astype(low)
        attn_out = (product(mixed_low, proj_full) + proj_bias).reshape(local, TOK, D)
        residual_mid = residual_in + gate_attn[:, None, :] * attn_out
        if layer_index == 1:
            mlp_whole[1], residual_mid = lax.optimization_barrier((mlp_whole[1], residual_mid))
        up_full, down_full = weights_of_mlp(layer_index)
        mlp_weights.append((up_full, down_full))
        hidden_two_low = modulate(residual_mid, shift_mlp, scale_mlp).reshape(row_count, D).astype(low)
        pre_act = product(hidden_two_low, up_full) + up_bias
        act_low = lax.optimization_barrier(gelu_tanh(pre_act).astype(low))
        mlp_out = (product(act_low, down_full) + down_bias).reshape(local, TOK, D)
        residual = residual_mid + gate_mlp[:, None, :] * mlp_out
        stored.append(
            (
                residual_in,
                hidden_low,
                packed_low,
                log_total,
                mixed_low,
                attn_out,
                residual_mid,
                hidden_two_low,
                pre_act,
                act_low,
                mlp_out,
            )
        )
    final_mods = modulations[:, LAYERS * 6 * D :]
    final_hidden = modulate(residual, final_mods[:, :D], final_mods[:, D:])
    final_low = final_hidden.reshape(row_count, D).astype(low)
    predicted = product(final_low, head_columns) + head_bias
    errors = predicted - noise.reshape(row_count, PD)
    loss_local = jnp.sum(errors * errors) / total_count
    grad_pred_low = (2.0 * errors / total_count).astype(low)
    grad_head_bias = jnp.sum(grad_pred_low.astype(f32), axis=0)
    grad_head = left_product(grad_pred_low, final_low)
    grad_final = right_product(grad_pred_low, head_columns).reshape(local, TOK, D)
    unused, final_pull = jax.vjp(modulate, residual, final_mods[:, :D], final_mods[:, D:])
    grad_residual, grad_shift_final, grad_scale_final = final_pull(grad_final)
    mod_grads = [None] * LAYERS
    attn_sums = [None] * LAYERS
    mlp_shards = [None] * LAYERS
    shards = [None] * LAYERS
    bias_pieces = [None] * LAYERS
    for layer_index in reversed(range(LAYERS)):
        qkv_full, proj_full = weights_of_attn(layer_index)
        up_full, down_full = mlp_weights[layer_index]
        (
            residual_in,
            hidden_low,
            packed_low,
            log_total,
            mixed_low,
            attn_out,
            residual_mid,
            hidden_two_low,
            pre_act,
            act_low,
            mlp_out,
        ) = stored[layer_index]
        segment = modulations[:, layer_index * 6 * D : (layer_index + 1) * 6 * D]
        mod_terms = [segment[:, part_index * D : (part_index + 1) * D] for part_index in range(6)]
        shift_attn, scale_attn, gate_attn, shift_mlp, scale_mlp, gate_mlp = mod_terms
        grad_gate_mlp = jnp.sum(grad_residual * mlp_out, axis=1)
        grad_mlp_low = (grad_residual * gate_mlp[:, None, :]).reshape(row_count, D).astype(low)
        grad_down_bias = jnp.sum(grad_mlp_low.astype(f32), axis=0)
        grad_down = left_product(act_low, grad_mlp_low)
        grad_act = right_product(grad_mlp_low, down_full)
        grad_pre_low = gelu_pull(pre_act, grad_act).astype(low)
        grad_up_bias = jnp.sum(grad_pre_low.astype(f32), axis=0)
        grad_up = left_product(hidden_two_low, grad_pre_low)
        sent_mlp = [
            grad_up[:, part * D : (part + 1) * D].astype(low).reshape(count, rows, D)
            for part in range(4)
        ]
        sent_mlp.append(grad_down.astype(low).reshape(count, 4 * rows, D))
        sent_mlp = jnp.concatenate(sent_mlp, axis=1).reshape(count * 8 * rows, D)
        sent_mlp, grad_pre_low = lax.optimization_barrier((sent_mlp, grad_pre_low))
        mlp_shards[layer_index] = lax.psum_scatter(
            sent_mlp, "fsdp", scatter_dimension=0, tiled=True
        ).astype(f32)
        grad_hidden_two = right_product(grad_pre_low, up_full).reshape(local, TOK, D)
        unused, mlp_pull = jax.vjp(modulate, residual_mid, shift_mlp, scale_mlp)
        part_residual, grad_shift_mlp, grad_scale_mlp = mlp_pull(grad_hidden_two)
        grad_residual = grad_residual + part_residual
        grad_gate_attn = jnp.sum(grad_residual * attn_out, axis=1)
        grad_attn_low = (grad_residual * gate_attn[:, None, :]).reshape(row_count, D).astype(low)
        grad_proj_bias = jnp.sum(grad_attn_low.astype(f32), axis=0)
        grad_proj = left_product(mixed_low, grad_attn_low)
        grad_mixed_low = right_product(grad_attn_low, proj_full).astype(low)
        grad_packed_low = attention_backward(packed_low, log_total, grad_mixed_low, local)
        if layer_index + 1 < LAYERS:
            grad_packed_low = attn_sums[layer_index + 1].before(grad_packed_low)
            attn_sums[layer_index + 1].step()
        grad_query_bias = jnp.sum(grad_packed_low[0].astype(f32), axis=0)
        grad_value_bias = jnp.sum(grad_packed_low[2].astype(f32), axis=0)
        grad_qkv = [left_product(hidden_low, item) for item in grad_packed_low]
        grad_hidden = (
            right_product(grad_packed_low[0], qkv_full[0])
            + right_product(grad_packed_low[1], qkv_full[1])
            + right_product(grad_packed_low[2], qkv_full[2])
        ).reshape(local, TOK, D)
        unused, attn_pull = jax.vjp(modulate, residual_in, shift_attn, scale_attn)
        part_residual, grad_shift_attn, grad_scale_attn = attn_pull(grad_hidden)
        grad_residual = grad_residual + part_residual
        mod_grads[layer_index] = jnp.concatenate(
            [
                grad_shift_attn,
                grad_scale_attn,
                grad_gate_attn,
                grad_shift_mlp,
                grad_scale_mlp,
                grad_gate_mlp,
            ],
            axis=1,
        )
        sent = [item.astype(low).reshape(count, rows, D) for item in grad_qkv + [grad_proj]]
        attn_sums[layer_index] = ScatterSum(sent, count, layer_index % 2 == 0)
        attn_sums[layer_index].step()
        if layer_index + 1 < LAYERS:
            grad_residual, mod_grads[layer_index] = attn_sums[layer_index + 1].before(
                (grad_residual, mod_grads[layer_index])
            )
            attn_sums[layer_index + 1].step()
        (grad_residual, mod_grads[layer_index]) = attn_sums[layer_index].before(
            (grad_residual, mod_grads[layer_index])
        )
        attn_sums[layer_index].step()
        bias_pieces[layer_index] = [
            grad_query_bias,
            grad_value_bias,
            grad_proj_bias,
            grad_up_bias,
            grad_down_bias,
        ]
    grad_zero_low = grad_residual.reshape(row_count, D).astype(low)
    grad_patch_bias = jnp.sum(grad_zero_low.astype(f32), axis=0)
    grad_patch = left_product(noised_low, grad_zero_low)

    grad_mods_low = jnp.concatenate(
        mod_grads + [grad_shift_final, grad_scale_final], axis=1
    ).astype(low)
    grad_mods_columns = lax.all_to_all(
        grad_mods_low, "fsdp", split_axis=1, concat_axis=0, tiled=True
    )
    grad_mods_columns = attn_sums[0].before(grad_mods_columns)
    attn_sums[0].step()
    grad_act_sent = right_product(mod_columns, grad_mods_columns).astype(low)
    own_mod_bias = jnp.sum(grad_mods_low.astype(f32), axis=0)
    pieces = []
    for layer_index in range(LAYERS):
        pieces += bias_pieces[layer_index]
        pieces.append(own_mod_bias[layer_index * 6 * D : (layer_index + 1) * 6 * D])
    pieces += [
        own_mod_bias[LAYERS * 6 * D :],
        grad_patch_bias,
        grad_head_bias,
    ]
    pieces += [grad_patch.reshape(-1), grad_head.reshape(-1)]
    pieces, grad_act_sent = lax.optimization_barrier((pieces, grad_act_sent))
    grad_act = lax.all_to_all(
        grad_act_sent,
        "fsdp",
        split_axis=0,
        concat_axis=0,
        tiled=True,
    )
    grad_act = jnp.sum(grad_act.reshape(count, rows, samples).astype(f32), axis=0)
    grad_act = attn_sums[0].before(grad_act)
    attn_sums[0].step()
    grad_act_sent, grad_mods_later = lax.optimization_barrier((grad_act_sent, grad_mods_columns))
    shard_mod = lax.all_to_all(
        left_product(cond_low, grad_mods_later).astype(low),
        "fsdp",
        split_axis=0,
        concat_axis=1,
        tiled=True,
    ).astype(f32)
    own_bias = lax.dynamic_slice(second_bias, (me * rows,), (rows,))
    condition_own = (
        right_product(tables_low[:, :D], first_low)
        + own_bias[:, None]
        + right_product(tables_low[:, class_at:patch_at], class_rows)
    )
    unused, silu_pull = jax.vjp(jax.nn.silu, condition_own)
    grad_condition = silu_pull(grad_act)[0]
    grad_class = lax.dot_general(
        grad_condition,
        class_rows.astype(f32),
        (((1,), (0,)), ((), ())),
        precision=lax.Precision.HIGHEST,
        preferred_element_type=f32,
    )[:, :CLASSES]
    grad_time_low = grad_condition.astype(low)
    grad_second_bias = jnp.sum(grad_time_low.astype(f32), axis=1)
    grad_second = product(grad_time_low, first_low)
    grad_time_sent, shard_mod = lax.optimization_barrier((grad_time_low, shard_mod))
    grad_time_all = lax.all_to_all(
        jnp.broadcast_to(grad_time_sent[None], (count, rows, samples)).reshape(D, samples),
        "fsdp",
        split_axis=0,
        concat_axis=0,
        tiled=True,
    )
    grad_first_act = lax.dynamic_slice(
        left_product(tables_full[:, :D], grad_time_all), (me * rows, 0), (rows, samples)
    )
    own_bias = lax.dynamic_slice(first_bias, (me * rows,), (rows,))
    first_pre_own = right_product(tables_low[:, first_at:class_at], features_low) + own_bias[:, None]
    unused, first_pull = jax.vjp(jax.nn.silu, first_pre_own)
    grad_first_low = first_pull(grad_first_act)[0].astype(low)
    grad_first_bias = jnp.sum(grad_first_low.astype(f32), axis=1)
    grad_first = product(grad_first_low, features_low)
    grad_middle = jnp.concatenate([grad_first, grad_second, grad_class], axis=1).T

    def spread(piece, length):
        return lax.dynamic_update_slice(jnp.zeros((length,), f32), piece, (me * piece.shape[0],))

    summed = sum_all(jnp.concatenate(pieces), count)
    bias_length = biases.shape[0] - 2 * D
    ends = summed[bias_length:].reshape(2 * PD, D)
    own_ends = lax.dynamic_slice(ends, (0, me * rows), (2 * PD, rows))
    shard_tables = jnp.concatenate([own_ends[:PD], grad_middle, own_ends[PD:]], axis=0)
    for layer_index in range(LAYERS):
        shard = mlp_shards[layer_index]
        parts = [attn_sums[layer_index].finish()[part * rows : (part + 1) * rows] for part in range(4)]
        parts += [shard[part * rows : (part + 1) * rows] for part in range(4)]
        shards[layer_index] = (
            jnp.concatenate(parts[:3], axis=1),
            parts[3],
            jnp.concatenate(parts[4:], axis=1),
            shard[4 * rows :],
        )
    shard_squares = jnp.sum(shard_mod * shard_mod) + jnp.sum(shard_tables * shard_tables)
    for layer_index in range(LAYERS):
        for item in shards[layer_index]:
            shard_squares = shard_squares + jnp.sum(item * item)
    last_sums = sum_all(
        jnp.concatenate(
            [
                spread(grad_first_bias, D),
                spread(grad_second_bias, D),
                shard_squares[None],
                loss_local[None],
            ]
        ),
        count,
    )
    square_total, loss_value = last_sums[2 * D], last_sums[2 * D + 1]
    bias_grad = jnp.concatenate(
        [summed[: bias_length - PD], last_sums[: 2 * D], summed[bias_length - PD : bias_length]]
    )
    grad_norm = jnp.sqrt(square_total + jnp.sum(bias_grad * bias_grad))
    factor = jnp.minimum(1.0, clip_limit / (grad_norm + 1e-06))
    shard_qkv, shard_proj, shard_up, shard_down = [
        jnp.stack([shards[layer_index][part] for layer_index in range(LAYERS)]) for part in range(4)
    ]
    qkv_update, qkv_first_new, qkv_second_new = adam_step(
        qkv_weight, shard_qkv, qkv_first, qkv_second, factor
    )
    proj_update, proj_first_new, proj_second_new = adam_step(
        proj_weight, shard_proj, proj_first, proj_second, factor
    )
    up_update, up_first_new, up_second_new = adam_step(
        up_weight, shard_up, up_first, up_second, factor
    )
    down_update, down_first_new, down_second_new = adam_step(
        down_weight, shard_down, down_first, down_second, factor
    )
    mod_update, mod_first_new, mod_second_new = adam_step(
        mod_weight, shard_mod, mod_first, mod_second, factor
    )
    tables_update, tables_first_new, tables_second_new = adam_step(
        tables, shard_tables, tables_first, tables_second, factor
    )
    biases_update, biases_first_new, biases_second_new = adam_step(
        biases, bias_grad, biases_first, biases_second, factor
    )
    return (
        loss_value,
        grad_norm,
        qkv_update,
        qkv_first_new,
        qkv_second_new,
        proj_update,
        proj_first_new,
        proj_second_new,
        up_update,
        up_first_new,
        up_second_new,
        down_update,
        down_first_new,
        down_second_new,
        mod_update,
        mod_first_new,
        mod_second_new,
        tables_update,
        tables_first_new,
        tables_second_new,
        biases_update,
        biases_first_new,
        biases_second_new,
    )


def solution(mesh):
    in_specs = (
        P("fsdp", None, None),
        P("fsdp", None, None),
        P("fsdp"),
        P("fsdp"),
        P(None, "fsdp", None),
        P(None, "fsdp", None),
        P(None, "fsdp", None),
        P(None, "fsdp", None),
        P("fsdp", None),
        P(None, "fsdp"),
        P(),
        P(None, "fsdp", None),
        P(None, "fsdp", None),
        P(None, "fsdp", None),
        P(None, "fsdp", None),
        P("fsdp", None),
        P(None, "fsdp"),
        P(),
        P(None, "fsdp", None),
        P(None, "fsdp", None),
        P(None, "fsdp", None),
        P(None, "fsdp", None),
        P("fsdp", None),
        P(None, "fsdp"),
        P(),
    )
    out_specs = (
        P(),
        P(),
        P(None, "fsdp", None),
        P(None, "fsdp", None),
        P(None, "fsdp", None),
        P(None, "fsdp", None),
        P(None, "fsdp", None),
        P(None, "fsdp", None),
        P(None, "fsdp", None),
        P(None, "fsdp", None),
        P(None, "fsdp", None),
        P(None, "fsdp", None),
        P(None, "fsdp", None),
        P(None, "fsdp", None),
        P("fsdp", None),
        P("fsdp", None),
        P("fsdp", None),
        P(None, "fsdp"),
        P(None, "fsdp"),
        P(None, "fsdp"),
        P(),
        P(),
        P(),
    )
    return jax.shard_map(body, mesh=mesh, in_specs=in_specs, out_specs=out_specs, check_vma=False)
```

```python
import math

import jax
import jax.numpy as jnp
from jax import lax
from jax.experimental import pallas as pl
from jax.sharding import PartitionSpec as P

D = 768
HEADS = 12
HD = 64
FF = 3072
FREQ = 256
CLASSES = 1000
DIFF_STEPS = 1000
LAYERS = 2
TOK = 256
PD = 16
MODW = 10752


norm_eps = 1e-06
clip_limit = 2.5
learn_rate = 0.01
beta_first = 0.9
beta_second = 0.95
adam_eps = 1e-08
weight_decay = 0.01
first_fix = 1.0 - 0.9**10
second_fix = 1.0 - 0.95**10


def modulate(residual, shift_term, scale_term):
    centred = residual - jnp.mean(residual, axis=-1, keepdims=True)
    spread = jnp.mean(centred * centred, axis=-1, keepdims=True)
    normed = centred * lax.rsqrt(spread + norm_eps)
    return normed * (1.0 + scale_term[:, None, :]) + shift_term[:, None, :]


gelu_rate = math.sqrt(2.0 / math.pi)
gelu_cubic = 0.044715 * gelu_rate


def gelu_tanh(values):
    raised = jnp.tanh(values * (gelu_rate + gelu_cubic * (values * values)))
    return (0.5 * values) * (1.0 + raised)


def gelu_pull(values, grad):
    square = values * values
    raised = jnp.tanh(values * (gelu_rate + gelu_cubic * square))
    slope = (1.0 - raised) * (values * (gelu_rate + 3.0 * gelu_cubic * square))
    return (0.5 * grad) * ((1.0 + raised) * (1.0 + slope))


def product(left_side, right_side):
    return jnp.dot(left_side, right_side, preferred_element_type=jnp.float32)


def left_product(left_side, right_side):
    return lax.dot_general(
        left_side, right_side, (((0,), (0,)), ((), ())), preferred_element_type=jnp.float32
    )


def right_product(left_side, right_side):
    return lax.dot_general(
        left_side, right_side, (((1,), (1,)), ((), ())), preferred_element_type=jnp.float32
    )


def time_features(steps_in):
    half_count = FREQ // 2
    frequencies = jnp.exp(
        -math.log(10000.0) * jnp.arange(half_count, dtype=jnp.float32) / half_count
    )
    angles = steps_in.astype(jnp.float32)[:, None] * frequencies[None, :]
    return jnp.concatenate([jnp.cos(angles), jnp.sin(angles)], axis=1)


def noise_share(steps_in):
    beta_values = jnp.linspace(0.0001, 0.02, DIFF_STEPS, dtype=jnp.float32)
    log_keep = jnp.log(1.0 - beta_values)
    taken = jnp.arange(DIFF_STEPS, dtype=jnp.int32)[None, :] <= steps_in[:, None]
    return jnp.exp(jnp.sum(jnp.where(taken, log_keep[None, :], 0.0), axis=1))


def bias_parts(biases):
    per_layer = 10 * D + FF
    layer_parts = []
    for layer_index in range(LAYERS):
        anchor = layer_index * per_layer
        layer_parts.append(
            (
                biases[anchor : anchor + D],
                biases[anchor + D : anchor + 2 * D],
                biases[anchor + 2 * D : anchor + 3 * D],
                biases[anchor + 3 * D : anchor + 3 * D + FF],
                biases[anchor + 3 * D + FF : anchor + 4 * D + FF],
                biases[anchor + 4 * D + FF : anchor + per_layer],
            )
        )
    anchor = LAYERS * per_layer
    global_parts = (
        biases[anchor : anchor + 2 * D],
        biases[anchor + 2 * D : anchor + 3 * D],
        biases[anchor + 3 * D : anchor + 4 * D],
        biases[anchor + 4 * D : anchor + 5 * D],
        biases[anchor + 5 * D : anchor + 5 * D + PD],
    )
    return (layer_parts, global_parts)


def hop_plan(count):
    if count == 32:
        return [(8, 4), (2, 2), (4, 2), (1, 2)]
    plan = []
    stride = 1
    while stride < count:
        plan.append((stride, 2))
        stride *= 2
    return plan


def shifted(index, stride, size, amount):
    coord = (index // stride) % size
    return index + ((coord + amount) % size - coord) * stride


def send(value, count, stride, size, amount=1):
    pairs = [(index, shifted(index, stride, size, amount)) for index in range(count)]
    return lax.ppermute(value, "fsdp", pairs)


def gather_near(value, count):
    gathered = value[None]
    for stride, size in hop_plan(count):
        pieces = [gathered]
        for unused in range(size - 1):
            pieces.append(send(pieces[-1], count, stride, size))
        gathered = jnp.concatenate(pieces, axis=0)
    return gathered


def near_places(count):
    me = lax.axis_index("fsdp")
    others = jnp.arange(count, dtype=jnp.int32)
    places = jnp.zeros((count,), jnp.int32)
    weight = 1
    for stride, size in hop_plan(count):
        steps = ((me // stride) % size - (others // stride) % size) % size
        places = places + steps * weight
        weight *= size
    return places


def mesh_dims(count):
    if count == 32:
        return (4, 2, 2, 2)
    return (2,) * (count.bit_length() - 1)


def fold(parts, axis, stride, count):
    size = parts[0].shape[axis]
    mine = (lax.axis_index("fsdp") // stride) % size

    def entry(index):
        picked = [lax.dynamic_index_in_dim(part, index, axis, keepdims=False) for part in parts]
        return picked[0] if len(picked) == 1 else jnp.concatenate(picked, axis=-2)

    arrived = [
        send(entry((mine + step) % size), count, stride, size, step) for step in range(1, size)
    ]
    total = entry(mine).astype(jnp.float32)
    for piece in arrived:
        total = total + piece.astype(jnp.float32)
    return total


class ScatterSum:
    def __init__(self, parts, count, swap):
        dims = mesh_dims(count)
        self.count = count
        self.strides = [1]
        for size in reversed(dims[1:]):
            self.strides.insert(0, self.strides[0] * size)
        self.value = [part.reshape(dims + part.shape[1:]) for part in parts]
        self.axes = list(range(len(dims)))
        self.order = list(reversed(self.axes))
        if swap:
            self.order[1], self.order[2] = self.order[2], self.order[1]

    def step(self):
        if not self.order:
            return
        axis = self.order.pop(0)
        place = self.axes.index(axis)
        total = fold(self.value, place, self.strides[axis], self.count)
        self.axes.remove(axis)
        self.value = [total.astype(jnp.bfloat16) if self.order else total]

    def before(self, values):
        self.value[0], values = lax.optimization_barrier((self.value[0], values))
        return values

    def finish(self):
        while self.order:
            self.step()
        return self.value[0]


def sum_all(value, count, kind=jnp.float32):
    stride = 1
    while stride < count:
        sent = value.astype(kind)
        value = sent.astype(jnp.float32) + send(sent, count, stride, 2).astype(jnp.float32)
        stride *= 2
    return value


def pair_scores(queries, keys_all, first_half):
    only = jnp.where(first_half, queries, jnp.zeros_like(queries))
    return only, right_product(only, keys_all) * HD ** (-0.5)


def attention_forward_kernel(queries_ref, keys_ref, values_ref, mixed_ref, total_ref):
    lanes = lax.broadcasted_iota(jnp.int32, (TOK, 2 * HD), 1)
    totals = jnp.zeros((TOK, 2 * HD), jnp.float32)
    for pair in range(HEADS // 2):
        span = slice(pair * 2 * HD, (pair + 1) * 2 * HD)
        queries, keys_all, values_all = queries_ref[:, span], keys_ref[:, span], values_ref[:, span]
        halves = []
        for half in range(2):
            mine = (lanes < HD) if half == 0 else (lanes >= HD)
            unused, scores = pair_scores(queries, keys_all, mine)
            row_max = jnp.max(scores, axis=1, keepdims=True)
            raised = jnp.exp(scores - row_max)
            row_sum = jnp.sum(raised, axis=1, keepdims=True)
            soft_low = (raised / row_sum).astype(jnp.bfloat16)
            halves.append(product(soft_low, values_all))
            totals = jnp.where(lanes == 2 * pair + half, row_max + jnp.log(row_sum), totals)
        mixed_ref[:, span] = jnp.where(lanes < HD, halves[0], halves[1]).astype(jnp.bfloat16)
    total_ref[...] = totals


def attention_backward_kernel(
    queries_ref, keys_ref, values_ref, total_ref, grad_ref, dqueries_ref, dkeys_ref, dvalues_ref
):
    lanes = lax.broadcasted_iota(jnp.int32, (TOK, 2 * HD), 1)
    for pair in range(HEADS // 2):
        span = slice(pair * 2 * HD, (pair + 1) * 2 * HD)
        queries, keys_all, values_all = queries_ref[:, span], keys_ref[:, span], values_ref[:, span]
        grads = grad_ref[:, span]
        made = []
        for half in range(2):
            mine = (lanes < HD) if half == 0 else (lanes >= HD)
            unused, scores = pair_scores(queries, keys_all, mine)
            head = 2 * pair + half
            soft_weights = jnp.exp(scores - total_ref[:, head : head + 1])
            grad_values = left_product(soft_weights.astype(jnp.bfloat16), grads)
            grad_soft = right_product(jnp.where(mine, grads, jnp.zeros_like(grads)), values_all)
            spread = jnp.sum(soft_weights * grad_soft, axis=1, keepdims=True)
            score_low = (soft_weights * (grad_soft - spread)).astype(jnp.bfloat16)
            made.append(
                (
                    product(score_low, keys_all) * HD ** (-0.5),
                    left_product(score_low, queries) * HD ** (-0.5),
                    grad_values,
                )
            )
        for part, target in enumerate((dqueries_ref, dkeys_ref, dvalues_ref)):
            target[:, span] = jnp.where(lanes < HD, made[0][part], made[1][part]).astype(
                jnp.bfloat16
            )


def token_block(width):
    return pl.BlockSpec((TOK, width), lambda sample: (sample, 0))


def attention_forward(packed_low, sample_count):
    row_count = sample_count * TOK
    return pl.pallas_call(
        attention_forward_kernel,
        grid=(sample_count,),
        in_specs=[token_block(D)] * 3,
        out_specs=[token_block(D), token_block(2 * HD)],
        out_shape=[
            jax.ShapeDtypeStruct((row_count, D), jnp.bfloat16),
            jax.ShapeDtypeStruct((row_count, 2 * HD), jnp.float32),
        ],
        cost_estimate=pl.CostEstimate(
            flops=8 * 10**9, bytes_accessed=8 * row_count * D, transcendentals=row_count * TOK * HEADS
        ),
        name="attention_forward",
    )(*packed_low)


def attention_backward(packed_low, log_total, grad_mixed_low, sample_count):
    row_count = sample_count * TOK
    return pl.pallas_call(
        attention_backward_kernel,
        grid=(sample_count,),
        in_specs=[token_block(D)] * 3 + [token_block(2 * HD), token_block(D)],
        out_specs=[token_block(D)] * 3,
        out_shape=[jax.ShapeDtypeStruct((row_count, D), jnp.bfloat16)] * 3,
        cost_estimate=pl.CostEstimate(
            flops=20 * 10**9, bytes_accessed=14 * row_count * D, transcendentals=row_count * TOK * HEADS
        ),
        name="attention_backward",
    )(*packed_low, log_total, grad_mixed_low)


def adam_step(weight_now, grad_now, first_old, second_old, factor):
    clipped = grad_now * factor
    first_new = beta_first * first_old + (1.0 - beta_first) * clipped
    second_new = beta_second * second_old + (1.0 - beta_second) * clipped * clipped
    step_size = -learn_rate * (
        first_new / first_fix / (jnp.sqrt(second_new / second_fix) + adam_eps)
        + weight_decay * weight_now
    )
    return (step_size, first_new, second_new)


def body(
    latents,
    noise,
    timesteps,
    labels,
    qkv_weight,
    proj_weight,
    up_weight,
    down_weight,
    mod_weight,
    tables,
    biases,
    qkv_first,
    proj_first,
    up_first,
    down_first,
    mod_first,
    tables_first,
    biases_first,
    qkv_second,
    proj_second,
    up_second,
    down_second,
    mod_second,
    tables_second,
    biases_second,
):
    count = lax.axis_size("fsdp")
    me = lax.axis_index("fsdp")
    local = latents.shape[0]
    samples = local * count
    rows = D // count
    row_count = local * TOK
    total_count = samples * TOK * PD
    low = jnp.bfloat16
    f32 = jnp.float32
    layer_parts, global_parts = bias_parts(biases)
    final_bias, patch_bias, first_bias, second_bias, head_bias = global_parts
    mod_bias = jnp.concatenate([part_item[5] for part_item in layer_parts] + [final_bias])

    attn_pieces, mlp_pieces = [], []
    for layer_index in range(LAYERS):
        pieces = [qkv_weight[layer_index][:, part * D : (part + 1) * D] for part in range(3)]
        attn_pieces.append(pieces + [proj_weight[layer_index]])
        pieces = [up_weight[layer_index][:, part * D : (part + 1) * D] for part in range(4)]
        mlp_pieces.append(pieces + [down_weight[layer_index]])

    def gather(pieces):
        packed = jnp.concatenate(pieces, axis=0).astype(low).reshape(-1, rows, D)
        return lax.all_gather(packed, "fsdp", axis=1, tiled=True)

    early = gather(attn_pieces[0] + mlp_pieces[0] + attn_pieces[1])
    late = gather(mlp_pieces[1])

    mod_low = mod_weight.astype(low)
    mod_columns = lax.all_to_all(mod_low, "fsdp", split_axis=1, concat_axis=0, tiled=True)
    digits = jnp.concatenate([timesteps // 32, timesteps % 32, labels // 32, labels % 32]).astype(low)
    table_low = tables.astype(low).T
    room = -(-CLASSES // 128) * 128
    first_at, class_at, patch_at = D, D + FREQ, D + FREQ + room
    head_at, digit_at = patch_at + PD, patch_at + 2 * PD
    tables_low = jnp.concatenate(
        [
            table_low[:, PD + FREQ : PD + FREQ + D],
            table_low[:, PD : PD + FREQ],
            table_low[:, PD + FREQ + D : PD + FREQ + D + CLASSES],
            jnp.zeros((rows, room - CLASSES), low),
            table_low[:, :PD],
            table_low[:, PD + FREQ + D + CLASSES :],
            jnp.broadcast_to(digits[None, :], (rows, 4 * local)),
        ],
        axis=1,
    )
    tables_near = gather_near(tables_low, count)
    places = near_places(count)
    tables_far = jnp.take(tables_near, places, axis=0, mode="clip")
    tables_full = tables_far.reshape(D, digit_at + 4 * local)

    numbers = tables_far[:, 0, digit_at:].astype(jnp.int32).reshape(count, 4, local)
    steps_all = (numbers[:, 0] * 32 + numbers[:, 1]).reshape(samples)
    labels_all = (numbers[:, 2] * 32 + numbers[:, 3]).reshape(samples)
    features_low = time_features(steps_all).astype(low)
    first_pre = right_product(features_low, tables_full[:, first_at:class_at]) + first_bias
    first_low = jax.nn.silu(first_pre).astype(low)
    class_rows = (labels_all[:, None] == jnp.arange(room, dtype=jnp.int32)[None, :]).astype(low)
    condition = (
        right_product(first_low, tables_full[:, :D])
        + second_bias
        + right_product(class_rows, tables_full[:, class_at:patch_at])
    )
    cond_low = jax.nn.silu(condition).astype(low)
    mods_columns = product(cond_low, mod_columns)
    modulations = (
        lax.all_to_all(mods_columns, "fsdp", split_axis=0, concat_axis=1, tiled=True) + mod_bias
    )

    keep_share = noise_share(timesteps)
    noised = (
        jnp.sqrt(keep_share)[:, None, None] * latents
        + jnp.sqrt(1.0 - keep_share)[:, None, None] * noise
    )
    noised_low = noised.reshape(row_count, PD).astype(low)
    patch_columns = tables_full[:, patch_at:head_at]
    head_columns = tables_full[:, head_at:digit_at]
    residual = (right_product(noised_low, patch_columns) + patch_bias).reshape(local, TOK, D)

    def weights_of_attn(layer_index):
        whole = attn_whole[layer_index]
        return [whole[part] for part in range(3)], whole[3]

    def weights_of_mlp(layer_index):
        whole = mlp_whole[layer_index]
        up_full = whole[:4].transpose(1, 0, 2).reshape(D, FF)
        down_full = whole[4:].reshape(4, count, rows, D).transpose(1, 0, 2, 3).reshape(FF, D)
        return lax.optimization_barrier((up_full, down_full))

    mlp_weights = []
    stored = []
    for layer_index in range(LAYERS):
        if layer_index == 0:
            early, residual = lax.optimization_barrier((early, residual))
            attn_whole = [early[:4], early[12:]]
            mlp_whole = [early[4:12], late]
        qkv_full, proj_full = weights_of_attn(layer_index)
        query_bias, value_bias, proj_bias, up_bias, down_bias, unused = layer_parts[layer_index]
        segment = modulations[:, layer_index * 6 * D : (layer_index + 1) * 6 * D]
        mod_terms = [segment[:, part_index * D : (part_index + 1) * D] for part_index in range(6)]
        shift_attn, scale_attn, gate_attn, shift_mlp, scale_mlp, gate_mlp = mod_terms
        residual_in = residual
        hidden_low = modulate(residual_in, shift_attn, scale_attn).reshape(row_count, D).astype(low)
        packed_low = [
            (product(hidden_low, qkv_full[0]) + query_bias).astype(low),
            product(hidden_low, qkv_full[1]).astype(low),
            (product(hidden_low, qkv_full[2]) + value_bias).astype(low),
        ]
        mixed, log_total = attention_forward(packed_low, local)
        mixed_low = mixed.astype(low)
        attn_out = (product(mixed_low, proj_full) + proj_bias).reshape(local, TOK, D)
        residual_mid = residual_in + gate_attn[:, None, :] * attn_out
        if layer_index == 1:
            mlp_whole[1], residual_mid = lax.optimization_barrier((mlp_whole[1], residual_mid))
        up_full, down_full = weights_of_mlp(layer_index)
        mlp_weights.append((up_full, down_full))
        hidden_two_low = modulate(residual_mid, shift_mlp, scale_mlp).reshape(row_count, D).astype(low)
        pre_act = product(hidden_two_low, up_full) + up_bias
        act_low = lax.optimization_barrier(gelu_tanh(pre_act).astype(low))
        mlp_out = (product(act_low, down_full) + down_bias).reshape(local, TOK, D)
        residual = residual_mid + gate_mlp[:, None, :] * mlp_out
        stored.append(
            (
                residual_in,
                hidden_low,
                packed_low,
                log_total,
                mixed_low,
                attn_out,
                residual_mid,
                hidden_two_low,
                pre_act,
                act_low,
                mlp_out,
            )
        )
    final_mods = modulations[:, LAYERS * 6 * D :]
    final_hidden = modulate(residual, final_mods[:, :D], final_mods[:, D:])
    final_low = final_hidden.reshape(row_count, D).astype(low)
    predicted = product(final_low, head_columns) + head_bias
    errors = predicted - noise.reshape(row_count, PD)
    loss_local = jnp.sum(errors * errors) / total_count
    grad_pred_low = (2.0 * errors / total_count).astype(low)
    grad_head_bias = jnp.sum(grad_pred_low.astype(f32), axis=0)
    grad_head = left_product(grad_pred_low, final_low)
    grad_final = right_product(grad_pred_low, head_columns).reshape(local, TOK, D)
    unused, final_pull = jax.vjp(modulate, residual, final_mods[:, :D], final_mods[:, D:])
    grad_residual, grad_shift_final, grad_scale_final = final_pull(grad_final)
    mod_grads = [None] * LAYERS
    attn_sums = [None] * LAYERS
    mlp_shards = [None] * LAYERS
    shards = [None] * LAYERS
    bias_pieces = [None] * LAYERS
    for layer_index in reversed(range(LAYERS)):
        qkv_full, proj_full = weights_of_attn(layer_index)
        up_full, down_full = mlp_weights[layer_index]
        (
            residual_in,
            hidden_low,
            packed_low,
            log_total,
            mixed_low,
            attn_out,
            residual_mid,
            hidden_two_low,
            pre_act,
            act_low,
            mlp_out,
        ) = stored[layer_index]
        segment = modulations[:, layer_index * 6 * D : (layer_index + 1) * 6 * D]
        mod_terms = [segment[:, part_index * D : (part_index + 1) * D] for part_index in range(6)]
        shift_attn, scale_attn, gate_attn, shift_mlp, scale_mlp, gate_mlp = mod_terms
        grad_gate_mlp = jnp.sum(grad_residual * mlp_out, axis=1)
        grad_mlp_low = (grad_residual * gate_mlp[:, None, :]).reshape(row_count, D).astype(low)
        grad_down_bias = jnp.sum(grad_mlp_low.astype(f32), axis=0)
        grad_down = left_product(act_low, grad_mlp_low)
        grad_act = right_product(grad_mlp_low, down_full)
        grad_pre_low = gelu_pull(pre_act, grad_act).astype(low)
        grad_up_bias = jnp.sum(grad_pre_low.astype(f32), axis=0)
        grad_up = left_product(hidden_two_low, grad_pre_low)
        sent_mlp = [
            grad_up[:, part * D : (part + 1) * D].astype(low).reshape(count, rows, D)
            for part in range(4)
        ]
        sent_mlp.append(grad_down.astype(low).reshape(count, 4 * rows, D))
        sent_mlp = jnp.concatenate(sent_mlp, axis=1).reshape(count * 8 * rows, D)
        sent_mlp, grad_pre_low = lax.optimization_barrier((sent_mlp, grad_pre_low))
        mlp_shards[layer_index] = lax.psum_scatter(
            sent_mlp, "fsdp", scatter_dimension=0, tiled=True
        ).astype(f32)
        grad_hidden_two = right_product(grad_pre_low, up_full).reshape(local, TOK, D)
        unused, mlp_pull = jax.vjp(modulate, residual_mid, shift_mlp, scale_mlp)
        part_residual, grad_shift_mlp, grad_scale_mlp = mlp_pull(grad_hidden_two)
        grad_residual = grad_residual + part_residual
        grad_gate_attn = jnp.sum(grad_residual * attn_out, axis=1)
        grad_attn_low = (grad_residual * gate_attn[:, None, :]).reshape(row_count, D).astype(low)
        grad_proj_bias = jnp.sum(grad_attn_low.astype(f32), axis=0)
        grad_proj = left_product(mixed_low, grad_attn_low)
        grad_mixed_low = right_product(grad_attn_low, proj_full).astype(low)
        grad_packed_low = attention_backward(packed_low, log_total, grad_mixed_low, local)
        if layer_index + 1 < LAYERS:
            grad_packed_low = attn_sums[layer_index + 1].before(grad_packed_low)
            attn_sums[layer_index + 1].step()
        grad_query_bias = jnp.sum(grad_packed_low[0].astype(f32), axis=0)
        grad_value_bias = jnp.sum(grad_packed_low[2].astype(f32), axis=0)
        grad_qkv = [left_product(hidden_low, item) for item in grad_packed_low]
        grad_hidden = (
            right_product(grad_packed_low[0], qkv_full[0])
            + right_product(grad_packed_low[1], qkv_full[1])
            + right_product(grad_packed_low[2], qkv_full[2])
        ).reshape(local, TOK, D)
        unused, attn_pull = jax.vjp(modulate, residual_in, shift_attn, scale_attn)
        part_residual, grad_shift_attn, grad_scale_attn = attn_pull(grad_hidden)
        grad_residual = grad_residual + part_residual
        mod_grads[layer_index] = jnp.concatenate(
            [
                grad_shift_attn,
                grad_scale_attn,
                grad_gate_attn,
                grad_shift_mlp,
                grad_scale_mlp,
                grad_gate_mlp,
            ],
            axis=1,
        )
        sent = [item.astype(low).reshape(count, rows, D) for item in grad_qkv + [grad_proj]]
        attn_sums[layer_index] = ScatterSum(sent, count, layer_index % 2 == 0)
        attn_sums[layer_index].step()
        if layer_index + 1 < LAYERS:
            grad_residual, mod_grads[layer_index] = attn_sums[layer_index + 1].before(
                (grad_residual, mod_grads[layer_index])
            )
            attn_sums[layer_index + 1].step()
        (grad_residual, mod_grads[layer_index]) = attn_sums[layer_index].before(
            (grad_residual, mod_grads[layer_index])
        )
        attn_sums[layer_index].step()
        bias_pieces[layer_index] = [
            grad_query_bias,
            grad_value_bias,
            grad_proj_bias,
            grad_up_bias,
            grad_down_bias,
        ]
    grad_zero_low = grad_residual.reshape(row_count, D).astype(low)
    grad_patch_bias = jnp.sum(grad_zero_low.astype(f32), axis=0)
    grad_patch = left_product(noised_low, grad_zero_low)

    grad_mods_low = jnp.concatenate(
        mod_grads + [grad_shift_final, grad_scale_final], axis=1
    ).astype(low)
    grad_mods_columns = lax.all_to_all(
        grad_mods_low, "fsdp", split_axis=1, concat_axis=0, tiled=True
    )
    grad_mods_columns = attn_sums[0].before(grad_mods_columns)
    attn_sums[0].step()
    grad_act_sent = right_product(mod_columns, grad_mods_columns).astype(low)
    own_mod_bias = jnp.sum(grad_mods_low.astype(f32), axis=0)
    pieces = []
    for layer_index in range(LAYERS):
        pieces += bias_pieces[layer_index]
        pieces.append(own_mod_bias[layer_index * 6 * D : (layer_index + 1) * 6 * D])
    pieces += [
        own_mod_bias[LAYERS * 6 * D :],
        grad_patch_bias,
        grad_head_bias,
    ]
    pieces += [grad_patch.reshape(-1), grad_head.reshape(-1)]
    pieces, grad_act_sent = lax.optimization_barrier((pieces, grad_act_sent))
    grad_act = lax.all_to_all(
        grad_act_sent,
        "fsdp",
        split_axis=0,
        concat_axis=0,
        tiled=True,
    )
    grad_act = jnp.sum(grad_act.reshape(count, rows, samples).astype(f32), axis=0)
    grad_act = attn_sums[0].before(grad_act)
    attn_sums[0].step()
    grad_act, mlp_shards[1] = lax.optimization_barrier((grad_act, mlp_shards[1]))
    grad_act_sent, grad_mods_later = lax.optimization_barrier((grad_act_sent, grad_mods_columns))
    shard_mod = lax.all_to_all(
        left_product(cond_low, grad_mods_later).astype(low),
        "fsdp",
        split_axis=0,
        concat_axis=1,
        tiled=True,
    ).astype(f32)
    own_bias = lax.dynamic_slice(second_bias, (me * rows,), (rows,))
    condition_own = (
        right_product(tables_low[:, :D], first_low)
        + own_bias[:, None]
        + right_product(tables_low[:, class_at:patch_at], class_rows)
    )
    unused, silu_pull = jax.vjp(jax.nn.silu, condition_own)
    grad_condition = silu_pull(grad_act)[0]
    grad_class = lax.dot_general(
        grad_condition,
        class_rows.astype(f32),
        (((1,), (0,)), ((), ())),
        precision=lax.Precision.HIGHEST,
        preferred_element_type=f32,
    )[:, :CLASSES]
    grad_time_low = grad_condition.astype(low)
    grad_second_bias = jnp.sum(grad_time_low.astype(f32), axis=1)
    grad_second = product(grad_time_low, first_low)
    grad_time_sent, shard_mod, mlp_shards[0] = lax.optimization_barrier(
        (grad_time_low, shard_mod, mlp_shards[0])
    )
    grad_time_all = lax.all_to_all(
        jnp.broadcast_to(grad_time_sent[None], (count, rows, samples)).reshape(D, samples),
        "fsdp",
        split_axis=0,
        concat_axis=0,
        tiled=True,
    )
    grad_first_act = lax.dynamic_slice(
        left_product(tables_full[:, :D], grad_time_all), (me * rows, 0), (rows, samples)
    )
    own_bias = lax.dynamic_slice(first_bias, (me * rows,), (rows,))
    first_pre_own = right_product(tables_low[:, first_at:class_at], features_low) + own_bias[:, None]
    unused, first_pull = jax.vjp(jax.nn.silu, first_pre_own)
    grad_first_low = first_pull(grad_first_act)[0].astype(low)
    grad_first_bias = jnp.sum(grad_first_low.astype(f32), axis=1)
    grad_first = product(grad_first_low, features_low)
    grad_middle = jnp.concatenate([grad_first, grad_second, grad_class], axis=1).T

    def spread(piece, length):
        return lax.dynamic_update_slice(jnp.zeros((length,), f32), piece, (me * piece.shape[0],))

    summed = sum_all(jnp.concatenate(pieces), count, low)
    bias_length = biases.shape[0] - 2 * D
    ends = summed[bias_length:].reshape(2 * PD, D)
    own_ends = lax.dynamic_slice(ends, (0, me * rows), (2 * PD, rows))
    shard_tables = jnp.concatenate([own_ends[:PD], grad_middle, own_ends[PD:]], axis=0)
    for layer_index in range(LAYERS):
        shard = mlp_shards[layer_index]
        parts = [attn_sums[layer_index].finish()[part * rows : (part + 1) * rows] for part in range(4)]
        parts += [shard[part * rows : (part + 1) * rows] for part in range(4)]
        shards[layer_index] = (
            jnp.concatenate(parts[:3], axis=1),
            parts[3],
            jnp.concatenate(parts[4:], axis=1),
            shard[4 * rows :],
        )
    shard_squares = jnp.sum(shard_mod * shard_mod) + jnp.sum(shard_tables * shard_tables)
    for layer_index in range(LAYERS):
        for item in shards[layer_index]:
            shard_squares = shard_squares + jnp.sum(item * item)
    last_sums = sum_all(
        jnp.concatenate(
            [
                spread(grad_first_bias, D),
                spread(grad_second_bias, D),
                shard_squares[None],
                loss_local[None],
            ]
        ),
        count,
    )
    square_total, loss_value = last_sums[2 * D], last_sums[2 * D + 1]
    bias_grad = jnp.concatenate(
        [summed[: bias_length - PD], last_sums[: 2 * D], summed[bias_length - PD : bias_length]]
    )
    grad_norm = jnp.sqrt(square_total + jnp.sum(bias_grad * bias_grad))
    factor = jnp.minimum(1.0, clip_limit / (grad_norm + 1e-06))
    shard_qkv, shard_proj, shard_up, shard_down = [
        jnp.stack([shards[layer_index][part] for layer_index in range(LAYERS)]) for part in range(4)
    ]
    qkv_update, qkv_first_new, qkv_second_new = adam_step(
        qkv_weight, shard_qkv, qkv_first, qkv_second, factor
    )
    proj_update, proj_first_new, proj_second_new = adam_step(
        proj_weight, shard_proj, proj_first, proj_second, factor
    )
    up_update, up_first_new, up_second_new = adam_step(
        up_weight, shard_up, up_first, up_second, factor
    )
    down_update, down_first_new, down_second_new = adam_step(
        down_weight, shard_down, down_first, down_second, factor
    )
    mod_update, mod_first_new, mod_second_new = adam_step(
        mod_weight, shard_mod, mod_first, mod_second, factor
    )
    tables_update, tables_first_new, tables_second_new = adam_step(
        tables, shard_tables, tables_first, tables_second, factor
    )
    biases_update, biases_first_new, biases_second_new = adam_step(
        biases, bias_grad, biases_first, biases_second, factor
    )
    return (
        loss_value,
        grad_norm,
        qkv_update,
        qkv_first_new,
        qkv_second_new,
        proj_update,
        proj_first_new,
        proj_second_new,
        up_update,
        up_first_new,
        up_second_new,
        down_update,
        down_first_new,
        down_second_new,
        mod_update,
        mod_first_new,
        mod_second_new,
        tables_update,
        tables_first_new,
        tables_second_new,
        biases_update,
        biases_first_new,
        biases_second_new,
    )


def solution(mesh):
    in_specs = (
        P("fsdp", None, None),
        P("fsdp", None, None),
        P("fsdp"),
        P("fsdp"),
        P(None, "fsdp", None),
        P(None, "fsdp", None),
        P(None, "fsdp", None),
        P(None, "fsdp", None),
        P("fsdp", None),
        P(None, "fsdp"),
        P(),
        P(None, "fsdp", None),
        P(None, "fsdp", None),
        P(None, "fsdp", None),
        P(None, "fsdp", None),
        P("fsdp", None),
        P(None, "fsdp"),
        P(),
        P(None, "fsdp", None),
        P(None, "fsdp", None),
        P(None, "fsdp", None),
        P(None, "fsdp", None),
        P("fsdp", None),
        P(None, "fsdp"),
        P(),
    )
    out_specs = (
        P(),
        P(),
        P(None, "fsdp", None),
        P(None, "fsdp", None),
        P(None, "fsdp", None),
        P(None, "fsdp", None),
        P(None, "fsdp", None),
        P(None, "fsdp", None),
        P(None, "fsdp", None),
        P(None, "fsdp", None),
        P(None, "fsdp", None),
        P(None, "fsdp", None),
        P(None, "fsdp", None),
        P(None, "fsdp", None),
        P("fsdp", None),
        P("fsdp", None),
        P("fsdp", None),
        P(None, "fsdp"),
        P(None, "fsdp"),
        P(None, "fsdp"),
        P(),
        P(),
        P(),
    )
    return jax.shard_map(body, mesh=mesh, in_specs=in_specs, out_specs=out_specs, check_vma=False)
```
